128 devices in a mesh: row: 8 (over z, x_lo), col: 16 (over x_hi, y, core).
Axes of the slice: x: 4 (x_hi: 2, x_lo: 2; x = x_hi * 2 + x_lo), y: 4, z: 4, core: 2. Of those that a mesh axis runs over, the one named last changes fastest.
Arguments:
- observed: bfloat16 [512, 2048], P('row', 'col'), may hold values from -12 to 12
- probe_signs: int32 [512, 2048], P('row', 'col'), may hold values from 0 to 1
- weights: float32 [2, 512, 2048], P(None, 'row', 'col'), may hold values from 0.2 to 1
- kernels: bfloat16 [2, 129, 129], replicated, may hold values from -0.046875 to 0.046875
Outputs:
- solution: float32 [2, 512, 2048], P(None, 'row', 'col')
- residual: float32 [2, 512, 2048], P(None, 'row', 'col')
The draws below stay inside these ranges and needn't reach their ends.
All inputs are finite; a program needn't handle non-finite values.
Results may differ from the reference program's by a relative error of at most 0.02.
Values may be sent and summed in bfloat16 or wider, within the bound.
A program may use at most 320 MiB of HBM per device.

```python
import jax
import jax.numpy as jnp

RADIUS = 64
MODES = 2
ITERS = 2
NY = 512
NX = 2048


def draw_observed(key, part):
    row_pos = jnp.arange(NY, dtype=jnp.float32) / max(NY - 1, 1)
    col_pos = jnp.arange(NX, dtype=jnp.float32) / max(NX - 1, 1)
    trend = jnp.exp(jnp.log(3.0) * 0.5 * (row_pos[:, None] + col_pos[None, :]))
    base = jnp.clip(jax.random.normal(key, (NY, NX), jnp.float32), -4.0, 4.0)
    return (base * trend).astype(jnp.bfloat16)


def plant(entries, rng, low, high):
    spot = [jax.random.randint(jax.random.fold_in(rng, axis), (), 0, length) for axis, length in enumerate(entries.shape)]
    widest = entries.shape.index(max(entries.shape))
    next_to = spot[:widest] + [(spot[widest] + 1) % entries.shape[widest]] + spot[widest + 1:]
    return entries.at[tuple(spot)].set(low).at[tuple(next_to)].set(high)


def block_scale(stream_key, dims, split, low, largest):
    def one(axis_at, parts):
        heights = jax.random.uniform(jax.random.fold_in(jax.random.fold_in(stream_key, 6), axis_at), (parts,), jnp.float32, low / len(split), largest / len(split))
        return jnp.repeat(jnp.exp(heights), dims[axis_at] // parts).reshape((-1,) + (1,) * (len(dims) - axis_at - 1))

    level = one(*split[0])
    for cut in split[1:]:
        level = level * one(*cut)
    return level


def gaussian(stream_key, dims, scale, limit, kind=jnp.bfloat16):
    drawn = jax.random.normal(stream_key, dims, jnp.float32) * scale
    return jnp.minimum(jnp.maximum(drawn, -limit), limit).astype(kind)


def setup_inputs(seed: int = 0) -> dict:
    seeds = jax.random.split(jax.random.key(seed), 5)
    observed = draw_observed(jax.random.fold_in(seeds[4], 71), 0)
    probe_signs = plant(jax.random.randint(seeds[1], (NY, NX), 0, 2), jax.random.fold_in(seeds[1], 1), 0, 1).astype(jnp.int32)
    weights = jnp.clip(0.2 + 0.8 * jax.random.uniform(seeds[2], (MODES, NY, NX), jnp.float32) ** block_scale(seeds[2], (MODES, NY, NX), ((1, 8), (2, 16)), -0.2, 0.2), 0.2, 1.0)
    kernels = gaussian(seeds[3], (MODES, 2 * RADIUS + 1, 2 * RADIUS + 1), ((2 * RADIUS + 1) * (2 * RADIUS + 1)) ** -0.5, 0.046875)
    return {"observed": observed, "probe_signs": probe_signs, "weights": weights, "kernels": kernels}


DAMPING = 1.0


def correlate(current, kernel):
    height = current.shape[1]
    breadth = current.shape[2]
    kernel_width = kernel.shape[0]
    padded = jnp.pad(current, ((0, 0), (RADIUS, RADIUS), (RADIUS, RADIUS)))
    extent = (height + 2 * RADIUS, breadth + 2 * RADIUS)
    kernel_pad = jnp.zeros(extent, current.dtype).at[:kernel_width, :kernel_width].set(kernel)
    spectrum = jnp.fft.rfft2(padded, s=extent) * jnp.conj(jnp.fft.rfft2(kernel_pad, s=extent))
    whole_map = jnp.fft.irfft2(spectrum, s=extent)
    return whole_map[:, :height, :breadth].astype(current.dtype)


def forward_blur(current, weights, kernels):
    summed = jnp.zeros(current.shape, jnp.float32)
    for mode_index in range(MODES):
        weighted = (weights[mode_index][None] * current).astype(jnp.bfloat16)
        summed = summed + correlate(weighted.astype(jnp.float32), kernels[mode_index].astype(jnp.float32))
    return summed


def adjoint_blur(blurred, weights, kernels):
    source = blurred.astype(jnp.float32)
    summed = jnp.zeros(source.shape, jnp.float32)
    for mode_index in range(MODES):
        flipped = kernels[mode_index].astype(jnp.float32)[::-1, ::-1]
        summed = summed + weights[mode_index][None] * correlate(source, flipped)
    return summed


def reference(observed, probe_signs, weights, kernels):
    sign_image = (2 * probe_signs - 1).astype(jnp.bfloat16)
    start = jnp.stack([observed, sign_image])
    right_side = adjoint_blur(start, weights, kernels)
    solution = jnp.zeros_like(right_side)
    residual = right_side
    direction = right_side
    norm_now = jnp.sum(residual * residual, axis=(1, 2))
    for iteration in range(ITERS):
        blurred = forward_blur(direction, weights, kernels).astype(jnp.bfloat16)
        product_image = adjoint_blur(blurred, weights, kernels) + DAMPING * direction
        step_size = norm_now / jnp.sum(direction * product_image, axis=(1, 2))
        solution = solution + step_size[:, None, None] * direction
        residual = residual - step_size[:, None, None] * product_image
        norm_next = jnp.sum(residual * residual, axis=(1, 2))
        direction = residual + (norm_next / norm_now)[:, None, None] * direction
        norm_now = norm_next
    return solution, residual
```

```python
import functools

import jax
import jax.numpy as jnp
import ml_dtypes
import numpy as np
from jax import lax
from jax.experimental import pallas as pl
from jax.experimental.pallas import tpu as pltpu
from jax.sharding import PartitionSpec as P

RADIUS = 64
MODES = 2
DAMPING = 1.0
TILE_ROWS = 64
TILE_COLS = 128
FREQS = 128
TAPS = 2 * RADIUS + 1
BF16 = jnp.bfloat16
F32 = jnp.float32
MESH = pl.DeviceIdType.MESH

WEIGHT_STAGE = 5
SLOTS = 12


def split(table):
    high = table.astype(ml_dtypes.bfloat16)
    low = (table - high.astype(np.float64)).astype(ml_dtypes.bfloat16)
    return np.stack([high, low])


def tables():
    theta = 2 * np.pi * (np.arange(FREQS) + 0.5) / 256
    phi = 2 * np.pi * np.arange(FREQS) / 128
    column = np.concatenate([64 + np.arange(128), 192 + np.arange(64), np.arange(64)])
    arg = np.outer(column, theta)
    into_cols = np.concatenate([np.cos(arg), -np.sin(arg)], 1)
    pieces = []
    for block in range(2):
        arg = np.outer(phi, 64 * block + np.arange(64))
        pieces.append(np.block([[np.cos(arg), np.sin(arg)], [-np.sin(arg), np.cos(arg)]]))
    into_rows = np.concatenate(pieces, 1)
    arg = np.outer(np.arange(64), phi)
    from_rows = np.block([[np.cos(arg), -np.sin(arg)], [np.sin(arg), np.cos(arg)]]) / 128
    arg = np.outer(theta, np.arange(128))
    from_cols = np.concatenate([np.cos(arg), -np.sin(arg)], 0) / 128
    arg = np.outer(np.arange(128), theta)
    tap_cols = np.concatenate([np.cos(arg), np.sin(arg)], 1)
    arg = np.outer(phi, np.arange(64))
    tap_rows = np.block([[np.cos(arg), -np.sin(arg)], [np.sin(arg), np.cos(arg)]])
    return [split(t) for t in (into_cols, into_rows, from_rows, from_cols, tap_cols, tap_rows)]


def dot(a, b):
    return jnp.dot(a, b, preferred_element_type=F32)


def halves(x):
    high = x.astype(BF16)
    return high, (x - high.astype(F32)).astype(BF16)


def dot_table_left(table, x):
    high, low = halves(x)
    return dot(table[0], high) + (dot(table[0], low) + dot(table[1], high))


def dot_table_right(x, table):
    high, low = halves(x)
    return dot(high, table[0]) + (dot(low, table[0]) + dot(high, table[1]))


def kernel(
    row_count,
    col_count,
    observed,
    probe,
    weights,
    taps,
    into_cols,
    into_rows,
    from_rows,
    from_cols,
    tap_cols,
    tap_rows,
    solution_out,
    residual_out,
    got,
    own,
    packed,
    patch_weights,
    responses,
    first,
    image,
    second,
    sums,
    row_sums,
    col_sums,
    got_sem,
    sent_sem,
    row_got,
    row_sent,
    col_got,
    col_sent,
):
    my_row = lax.axis_index("row")
    my_col = lax.axis_index("col")

    def at_row(d):
        return lax.rem(my_row + d + row_count, row_count)

    def at_col(d):
        return lax.rem(my_col + d + col_count, col_count)

    barrier = pltpu.get_barrier_semaphore()

    def greet(row, col):
        pl.semaphore_signal(barrier, inc=1, device_id=(row, col), device_id_type=MESH)

    for dr in (-1, 1):
        for dc in (-1, 1):
            greet(at_row(dr), at_col(dc))

    def greet_row(d, c):
        greet(at_row(d), my_col)
        return c

    def greet_col(d, c):
        greet(my_row, at_col(d))
        return c

    lax.fori_loop(1, row_count, greet_row, 0)
    lax.fori_loop(1, col_count, greet_col, 0)

    lane = lax.broadcasted_iota(jnp.int32, (32, TILE_COLS), 1)
    low_lanes = lane < 64

    def place(slot, tile):
        own[slot] = tile.astype(BF16)
        turned = pltpu.roll(tile, 64, 1)
        packed[slot, 0:32] = jnp.where(low_lanes, tile[0:32], turned[32:64]).astype(BF16)
        packed[slot, 32:64] = jnp.where(low_lanes, turned[0:32], tile[32:64]).astype(BF16)

    def copies(slot):
        def copy(src, start, size, dr, dc):
            return pltpu.make_async_remote_copy(
                src_ref=src,
                dst_ref=got.at[slot, pl.ds(start, size)],
                send_sem=sent_sem.at[slot],
                recv_sem=got_sem.at[slot],
                device_id=(at_row(dr), at_col(dc)),
                device_id_type=MESH,
            )

        out = [copy(own.at[slot], 0, 64, 1, 0), copy(own.at[slot], 64, 64, -1, 0)]
        for dr in (1, -1, 0):
            block = 128 + 64 * (1 - dr)
            out.append(copy(packed.at[slot, pl.ds(0, 32)], block, 32, dr, -1))
            out.append(copy(packed.at[slot, pl.ds(32, 32)], block + 32, 32, dr, 1))
        return out

    def send(slot):
        for c in copies(slot):
            c.start()

    def arrived(slot):
        pltpu.make_async_copy(got.at[slot], got.at[slot], got_sem.at[slot]).wait()

    def sent(slot):
        pltpu.make_async_copy(got.at[slot], got.at[slot], sent_sem.at[slot]).wait()

    right_ok = (my_col < col_count - 1).astype(F32)
    left_ok = (my_col > 0).astype(F32)
    wide = lax.broadcasted_iota(jnp.int32, (1, 2 * TILE_COLS), 1)
    col_ok = jnp.where(wide < 128, 1.0, jnp.where(wide < 192, right_ok, left_ok))
    block_ok = [
        col_ok * (my_row > 0).astype(F32),
        col_ok,
        col_ok * (my_row < row_count - 1).astype(F32),
    ]

    def block(slot, k):
        if k == 1:
            middle = own[slot].astype(F32)
        else:
            middle = got[slot, 32 * k : 32 * k + 64].astype(F32)
        right = got[slot, 128 + 64 * k : 160 + 64 * k].astype(F32)
        left = got[slot, 160 + 64 * k : 192 + 64 * k].astype(F32)
        top = jnp.where(low_lanes, right, pltpu.roll(left, 64, 1))
        bottom = jnp.where(low_lanes, pltpu.roll(right, 64, 1), left)
        return jnp.concatenate([middle, jnp.concatenate([top, bottom], 0)], 1)

    def columns_of(x):
        return dot(x, into_cols[0]) + dot(x, into_cols[1])

    def stacked(y, k):
        parts = []
        for b in (k, k + 1):
            rows = y[64 * b : 64 * b + 64]
            parts += [rows[:, :128], rows[:, 128:]]
        return jnp.concatenate(parts, 0)

    def adjoint(slot):
        x = jnp.concatenate([(block(slot, k) * block_ok[k]).astype(BF16) for k in range(3)], 0)
        y = columns_of(x)
        z = dot_table_left(into_rows, jnp.concatenate([stacked(y, 0), stacked(y, 1)], 1))
        are, aim = z[:128, :128], z[128:, :128]
        bre, bim = z[:128, 128:], z[128:, 128:]
        reals, imags = [], []
        for m in range(MODES):
            h = [responses[1, m, i] for i in range(4)]
            reals.append(h[0] * are - h[1] * aim + (h[2] * bre - h[3] * bim))
            imags.append(h[0] * aim + h[1] * are + (h[2] * bim + h[3] * bre))
        spectrum = jnp.concatenate([jnp.concatenate(reals, 1), jnp.concatenate(imags, 1)], 0)
        v = dot_table_left(from_rows, spectrum)
        rows = [
            jnp.concatenate([v[:64, 128 * m : 128 * m + 128], v[64:, 128 * m : 128 * m + 128]], 1)
            for m in range(MODES)
        ]
        out = dot_table_right(jnp.concatenate(rows, 0), from_cols)
        return weights[0] * out[:64] + weights[1] * out[64:]

    def forward(slot):
        values = [block(slot, k) for k in range(3)]
        x = jnp.concatenate(
            [
                (patch_weights[m, 64 * k : 64 * k + 64] * values[k]).astype(BF16)
                for m in range(MODES)
                for k in range(3)
            ],
            0,
        )
        y = columns_of(x)
        z = [
            dot_table_left(
                into_rows, jnp.concatenate([stacked(y[:192], k), stacked(y[192:], k)], 1)
            )
            for k in range(2)
        ]
        real = jnp.zeros((FREQS, FREQS), F32)
        imag = real
        for m in range(MODES):
            h = [responses[0, m, i] for i in range(4)]
            lanes = slice(128 * m, 128 * m + 128)
            are, aim = z[0][:128, lanes], z[0][128:, lanes]
            bre, bim = z[1][:128, lanes], z[1][128:, lanes]
            real = real + (h[0] * are - h[1] * aim + (h[2] * bre - h[3] * bim))
            imag = imag + (h[0] * aim + h[1] * are + (h[2] * bim + h[3] * bre))
        v = dot_table_left(from_rows, jnp.concatenate([real, imag], 0))
        return dot_table_right(jnp.concatenate([v[:64], v[64:]], 1), from_cols)

    def build_responses(m, c):
        narrow = taps[m, :, 0:128]
        even_lane = lax.broadcasted_iota(jnp.int32, (1, FREQS), 1) % 2 == 0
        sign_f = jnp.where(even_lane, 1.0, -1.0)
        even_row = lax.broadcasted_iota(jnp.int32, (FREQS, 1), 0) % 2 == 0
        sign_q = jnp.where(even_row, 1.0, -1.0)
        cols = dot(narrow, tap_cols[0]) + dot(narrow, tap_cols[1])
        re = cols[:, :128]
        im = cols[:, 128:] + taps[m, :, 128:129].astype(F32) * sign_f
        pairs = jnp.concatenate(
            [
                jnp.concatenate([re[0:64], re[64:128]], 1),
                jnp.concatenate([im[0:64], im[64:128]], 1),
            ],
            0,
        )
        g = dot_table_left(tap_rows, pairs)
        g0re, g0im, g1re, g1im = g[:128, :128], g[128:, :128], g[:128, 128:], g[128:, 128:]
        mid_re, mid_im, last_re, last_im = re[64:65], im[64:65], re[128:129], im[128:129]
        responses[0, m, 0] = g0re
        responses[0, m, 1] = g0im
        responses[0, m, 2] = g1re + sign_q * last_re
        responses[0, m, 3] = g1im + sign_q * last_im
        responses[1, m, 0] = sign_f * (sign_q * (g1im - mid_im) + last_im)
        responses[1, m, 1] = sign_f * (sign_q * (g1re - mid_re) + last_re)
        responses[1, m, 2] = sign_f * (sign_q * g0im + mid_im)
        responses[1, m, 3] = sign_f * (sign_q * g0re + mid_re)
        return c

    def fold(x):
        return jnp.sum(x, axis=0, keepdims=True)

    def share_rows(which):
        row_sums[which, my_row] = sums[which]

        def go(d, c):
            pltpu.make_async_remote_copy(
                src_ref=sums.at[which],
                dst_ref=row_sums.at[which, my_row],
                send_sem=row_sent.at[which],
                recv_sem=row_got.at[which],
                device_id=(at_row(d), my_col),
                device_id_type=MESH,
            ).start()
            return c

        lax.fori_loop(1, row_count, go, 0)

    def rows_arrived(which):
        all_but_one = row_sums.at[which, pl.ds(0, row_count - 1)]
        pltpu.make_async_copy(all_but_one, all_but_one, row_got.at[which]).wait()

    def share_cols(which):
        rows_arrived(which)
        total = row_sums[which, 0]
        for i in range(1, row_count):
            total = total + row_sums[which, i]
        sums[2 + which] = total
        col_sums[which, my_col] = total

        def go(d, c):
            pltpu.make_async_remote_copy(
                src_ref=sums.at[2 + which],
                dst_ref=col_sums.at[which, my_col],
                send_sem=col_sent.at[which],
                recv_sem=col_got.at[which],
                device_id=(my_row, at_col(d)),
                device_id_type=MESH,
            ).start()
            return c

        lax.fori_loop(1, col_count, go, 0)

    def whole(which):
        all_but_one = col_sums.at[which, pl.ds(0, col_count - 1)]
        pltpu.make_async_copy(all_but_one, all_but_one, col_got.at[which]).wait()
        total = col_sums[which, 0]
        for i in range(1, col_count):
            total = total + col_sums[which, i]
        return jnp.sum(total, axis=1, keepdims=True)

    def sums_sent(which):
        rows = row_sums.at[which, pl.ds(0, row_count - 1)]
        pltpu.make_async_copy(rows, rows, row_sent.at[which]).wait()
        cols = col_sums.at[which, pl.ds(0, col_count - 1)]
        pltpu.make_async_copy(cols, cols, col_sent.at[which]).wait()

    place(0, observed[...].astype(F32))
    place(1, (2 * probe[...] - 1).astype(F32))
    for m in range(MODES):
        place(2 * WEIGHT_STAGE + m, weights[m])
    pl.semaphore_wait(barrier, row_count + col_count + 2)
    for slot in (0, 1, 2 * WEIGHT_STAGE, 2 * WEIGHT_STAGE + 1):
        send(slot)
    lax.fori_loop(0, MODES, build_responses, 0)
    sums[...] = jnp.zeros_like(sums)

    def right_side(n, c):
        arrived(n)
        r = adjoint(n)
        first[n] = r
        place(2 + n, r)
        send(2 + n)
        return c

    lax.fori_loop(0, 2, right_side, 0)

    def spread_weights(m, c):
        slot = 2 * WEIGHT_STAGE + m
        arrived(slot)
        for k in range(3):
            patch_weights[m, 64 * k : 64 * k + 64] = block(slot, k) * block_ok[k]
        return c

    lax.fori_loop(0, MODES, spread_weights, 0)

    def blur_first(n, c):
        arrived(2 + n)
        u = forward(2 + n)
        place(4 + n, u)
        send(4 + n)
        r = first[n]
        sums[0, pl.ds(n, 1)] = fold(r * r)
        sums[0, pl.ds(2 + n, 1)] = fold(u * own[4 + n].astype(F32))
        return c

    lax.fori_loop(0, 2, blur_first, 0)
    share_rows(0)

    def back_first(n, c):
        arrived(4 + n)
        image[n] = adjoint(4 + n) + DAMPING * first[n]

        @pl.when(n == 0)
        def _():
            share_cols(0)

        return c

    lax.fori_loop(0, 2, back_first, 0)
    total = whole(0)
    norm0 = [total[n : n + 1] for n in range(2)]
    curve0 = [total[2 + n : 3 + n] + DAMPING * norm0[n] for n in range(2)]
    step0 = [norm0[n] / curve0[n] for n in range(2)]
    for n in range(2):
        r = first[n] - step0[n] * image[n]
        second[n] = r
        place(6 + n, r)
        send(6 + n)

    def blur_second(n, c):
        arrived(6 + n)
        u = forward(6 + n)
        place(8 + n, u)
        send(8 + n)
        r = second[n]
        sums[1, pl.ds(n, 1)] = fold(r * r)
        sums[1, pl.ds(2 + n, 1)] = fold(u * own[8 + n].astype(F32))
        sums[1, pl.ds(4 + n, 1)] = fold(r * image[n])
        return c

    lax.fori_loop(0, 2, blur_second, 0)
    share_rows(1)

    def back_second(n, c):
        arrived(8 + n)
        residual_out[n] = adjoint(8 + n) + DAMPING * second[n]

        @pl.when(n == 0)
        def _():
            share_cols(1)

        return c

    lax.fori_loop(0, 2, back_second, 0)
    total = whole(1)
    for n in range(2):
        norm1 = total[n : n + 1]
        ratio = norm1 / norm0[n]
        curve1 = (
            total[2 + n : 3 + n]
            + DAMPING * norm1
            + 2.0 * ratio * total[4 + n : 5 + n]
            + ratio * ratio * curve0[n]
        )
        step1 = norm1 / curve1
        r0, r1 = first[n], second[n]
        solution_out[n] = step0[n] * r0 + step1 * (r1 + ratio * r0)
        residual_out[n] = r1 - step1 * (residual_out[n] + ratio * image[n])

    def drain(slot, c):
        sent(slot)
        return c

    lax.fori_loop(0, SLOTS, drain, 0)
    for which in range(2):
        sums_sent(which)


def solution(mesh):
    row_count, col_count = mesh.shape["row"], mesh.shape["col"]
    constants = tables()

    def shards(observed, probe_signs, weights, kernels):
        pair = (2, TILE_ROWS, TILE_COLS)
        vmem = pl.BlockSpec(memory_space=pltpu.VMEM)
        return pl.pallas_call(
            functools.partial(kernel, row_count, col_count),
            out_shape=(jax.ShapeDtypeStruct(pair, F32), jax.ShapeDtypeStruct(pair, F32)),
            in_specs=[vmem] * 10,
            out_specs=(vmem, vmem),
            scratch_shapes=[
                pltpu.VMEM((SLOTS, 320, TILE_COLS), BF16),
                pltpu.VMEM((SLOTS, TILE_ROWS, TILE_COLS), BF16),
                pltpu.VMEM((SLOTS, TILE_ROWS, TILE_COLS), BF16),
                pltpu.VMEM((MODES, 3 * TILE_ROWS, 2 * TILE_COLS), F32),
                pltpu.VMEM((2, MODES, 4, FREQS, FREQS), F32),
                pltpu.VMEM(pair, F32),
                pltpu.VMEM(pair, F32),
                pltpu.VMEM(pair, F32),
                pltpu.VMEM((4, 8, TILE_COLS), F32),
                pltpu.VMEM((2, row_count, 8, TILE_COLS), F32),
                pltpu.VMEM((2, col_count, 8, TILE_COLS), F32),
                pltpu.SemaphoreType.DMA((SLOTS,)),
                pltpu.SemaphoreType.DMA((SLOTS,)),
                pltpu.SemaphoreType.DMA((2,)),
                pltpu.SemaphoreType.DMA((2,)),
                pltpu.SemaphoreType.DMA((2,)),
                pltpu.SemaphoreType.DMA((2,)),
            ],
            compiler_params=pltpu.CompilerParams(
                collective_id=0, has_side_effects=True, vmem_limit_bytes=40 * 2**20
            ),
            name="deconvolve",
        )(observed, probe_signs, weights, kernels, *[jnp.asarray(c) for c in constants])

    return jax.shard_map(
        shards,
        mesh=mesh,
        in_specs=(P("row", "col"), P("row", "col"), P(None, "row", "col"), P()),
        out_specs=(P(None, "row", "col"), P(None, "row", "col")),
        check_vma=False,
    )
```

```python
import functools

import jax
import jax.numpy as jnp
import ml_dtypes
import numpy as np
from jax import lax
from jax.experimental import pallas as pl
from jax.experimental.pallas import tpu as pltpu
from jax.sharding import PartitionSpec as P

RADIUS = 64
MODES = 2
DAMPING = 1.0
TILE_ROWS = 64
TILE_COLS = 128
FREQS = 128
TAPS = 2 * RADIUS + 1
BF16 = jnp.bfloat16
F32 = jnp.float32
MESH = pl.DeviceIdType.MESH

WEIGHT_STAGE = 5
SLOTS = 12


def split(table):
    high = table.astype(ml_dtypes.bfloat16)
    low = (table - high.astype(np.float64)).astype(ml_dtypes.bfloat16)
    return np.stack([high, low])


def tables():
    theta = 2 * np.pi * (np.arange(FREQS) + 0.5) / 256
    phi = 2 * np.pi * np.arange(FREQS) / 128
    column = np.concatenate([64 + np.arange(128), 192 + np.arange(64), np.arange(64)])
    arg = np.outer(column, theta)
    into_cols = np.concatenate([np.cos(arg), -np.sin(arg)], 1)
    pieces = []
    for block in range(2):
        arg = np.outer(phi, 64 * block + np.arange(64))
        pieces.append(np.block([[np.cos(arg), np.sin(arg)], [-np.sin(arg), np.cos(arg)]]))
    into_rows = np.concatenate(pieces, 1)
    arg = np.outer(np.arange(64), phi)
    from_rows = np.block([[np.cos(arg), -np.sin(arg)], [np.sin(arg), np.cos(arg)]]) / 128
    arg = np.outer(theta, np.arange(128))
    from_cols = np.concatenate([np.cos(arg), -np.sin(arg)], 0) / 128
    arg = np.outer(np.arange(128), theta)
    tap_cols = np.concatenate([np.cos(arg), np.sin(arg)], 1)
    arg = np.outer(phi, np.arange(64))
    tap_rows = np.block([[np.cos(arg), -np.sin(arg)], [np.sin(arg), np.cos(arg)]])
    return [split(t) for t in (into_cols, into_rows, from_rows, from_cols, tap_cols, tap_rows)]


def dot(a, b):
    return jnp.dot(a, b, preferred_element_type=F32)


def halves(x):
    high = x.astype(BF16)
    return high, (x - high.astype(F32)).astype(BF16)


def dot_table_left(table, x):
    high, low = halves(x)
    return dot(table[0], high) + (dot(table[0], low) + dot(table[1], high))


def dot_table_right(x, table):
    high, low = halves(x)
    return dot(high, table[0]) + (dot(low, table[0]) + dot(high, table[1]))


def kernel(
    row_count,
    col_count,
    observed_hbm,
    probe_hbm,
    weights_hbm,
    taps_hbm,
    into_cols_hbm,
    into_rows_hbm,
    from_rows_hbm,
    from_cols_hbm,
    tap_cols_hbm,
    tap_rows_hbm,
    solution_out,
    residual_out,
    observed,
    probe,
    weights,
    taps,
    into_cols,
    into_rows,
    from_rows,
    from_cols,
    tap_cols,
    tap_rows,
    got,
    own,
    packed,
    zeros,
    patch_weights,
    responses,
    first,
    image,
    second,
    steps,
    sums,
    near_sums,
    far_sums,
    load_sem,
    got_sem,
    sent_sem,
    near_got,
    near_sent,
    far_got,
    far_sent,
):
    my_row = lax.axis_index("row")
    my_col = lax.axis_index("col")
    up_ok, down_ok = my_row > 0, my_row < row_count - 1
    left_ok, right_ok = my_col > 0, my_col < col_count - 1

    loads = [
        pltpu.make_async_copy(src, dst, load_sem.at[i])
        for i, (src, dst) in enumerate(
            (
                (observed_hbm, observed),
                (probe_hbm, probe),
                (weights_hbm, weights),
                (taps_hbm, taps),
                (tap_cols_hbm, tap_cols),
                (tap_rows_hbm, tap_rows),
                (into_cols_hbm, into_cols),
                (into_rows_hbm, into_rows),
                (from_rows_hbm, from_rows),
                (from_cols_hbm, from_cols),
            )
        )
    ]
    for load in loads:
        load.start()

    barrier = pltpu.get_barrier_semaphore()

    def greet(row, col):
        pl.semaphore_signal(barrier, inc=1, device_id=(row, col), device_id_type=MESH)

    z_count, y_count = row_count // 2, col_count // 4
    near_count, far_count = 8, z_count * y_count
    my_x_low, my_z = lax.rem(my_row, 2), my_row // 2
    my_core, my_y, my_x_high = lax.rem(my_col, 2), lax.rem(my_col // 2, y_count), my_col // (2 * y_count)
    my_near = my_x_high * 4 + my_x_low * 2 + my_core
    my_far = my_z * y_count + my_y

    def near(d):
        x_high = lax.rem(my_x_high + d // 4, 2)
        x_low = lax.rem(my_x_low + lax.rem(d // 2, 2), 2)
        core = lax.rem(my_core + lax.rem(d, 2), 2)
        return my_z * 2 + x_low, x_high * 2 * y_count + my_y * 2 + core

    def far(d):
        z = lax.rem(my_z + d // y_count, z_count)
        y = lax.rem(my_y + lax.rem(d, y_count), y_count)
        return z * 2 + my_x_low, my_x_high * 2 * y_count + y * 2 + my_core

    def greet_near(d, c):
        greet(*near(d))
        return c

    def greet_far(d, c):
        greet(*far(d))
        return c

    lax.fori_loop(1, far_count, greet_far, 0)
    lax.fori_loop(1, near_count, greet_near, 0)
    neighbours = []
    for dr, row_ok in ((-1, up_ok), (1, down_ok), (0, None)):
        for dc, col_ok in ((0, None), (-1, left_ok), (1, right_ok)):
            if dr or dc:
                there = row_ok if col_ok is None else col_ok if row_ok is None else row_ok & col_ok
                neighbours.append((dr, dc, there))
    for dr, dc, there in neighbours:
        pl.when(there)(functools.partial(greet, my_row + dr, my_col + dc))
    rows_here = 1 + up_ok.astype(jnp.int32) + down_ok.astype(jnp.int32)
    cols_here = 1 + left_ok.astype(jnp.int32) + right_ok.astype(jnp.int32)
    partners = rows_here * cols_here - 1 + (near_count - 1) + (far_count - 1)

    lane = lax.broadcasted_iota(jnp.int32, (32, TILE_COLS), 1)
    low_lanes = lane < 64

    def place(slot, tile):
        own[slot] = tile.astype(BF16)
        turned = pltpu.roll(tile, 64, 1)
        packed[slot, 0:32] = jnp.where(low_lanes, tile[0:32], turned[32:64]).astype(BF16)
        packed[slot, 32:64] = jnp.where(low_lanes, turned[0:32], tile[32:64]).astype(BF16)

    def landing(slot, dr, dc):
        if dc == 0:
            return got.at[slot, pl.ds(0 if dr < 0 else 64, 64)]
        return got.at[slot, pl.ds(128 + 64 * (1 + dr) + (32 if dc < 0 else 0), 32)]

    def send(slot):
        for i, (dr, dc, there) in enumerate(neighbours):
            if dc == 0:
                piece = own.at[slot]
            else:
                piece = packed.at[slot, pl.ds(0 if dc < 0 else 32, 32)]
            out = pltpu.make_async_remote_copy(
                src_ref=piece,
                dst_ref=landing(slot, -dr, -dc),
                send_sem=sent_sem.at[i],
                recv_sem=got_sem.at[slot],
                device_id=(my_row + dr, my_col + dc),
                device_id_type=MESH,
            )
            edge = landing(slot, dr, dc)
            fill = pltpu.make_async_copy(zeros.at[pl.ds(0, edge.shape[0])], edge, got_sem.at[slot])
            lax.cond(there, lambda out=out: out.start(), lambda fill=fill: fill.start())

    def arrived(slot):
        pltpu.make_async_copy(got.at[slot], got.at[slot], got_sem.at[slot]).wait()

    def all_sent():
        for i, (dr, dc, there) in enumerate(neighbours):
            every = got.at[:, pl.ds(0, 64 if dc == 0 else 32)]
            pl.when(there)(pltpu.make_async_copy(every, every, sent_sem.at[i]).wait)

    def halo(slot, k):
        right = got[slot, 128 + 64 * k : 160 + 64 * k].astype(F32)
        left = got[slot, 160 + 64 * k : 192 + 64 * k].astype(F32)
        top = jnp.where(low_lanes, right, pltpu.roll(left, 64, 1))
        bottom = jnp.where(low_lanes, pltpu.roll(right, 64, 1), left)
        return jnp.concatenate([top, bottom], 0)

    def patch(slot, middle):
        above, below = got[slot, 0:64].astype(F32), got[slot, 64:128].astype(F32)
        return [
            jnp.concatenate([tile, halo(slot, k)], 1) for k, tile in enumerate((above, middle, below))
        ]

    def columns_of(x):
        return dot(x, into_cols[0]) + dot(x, into_cols[1])

    def stacked(y, k):
        parts = []
        for b in (k, k + 1):
            rows = y[64 * b : 64 * b + 64]
            parts += [rows[:, :128], rows[:, 128:]]
        return jnp.concatenate(parts, 0)

    def adjoint(slot):
        x = jnp.concatenate([b.astype(BF16) for b in patch(slot, own[slot].astype(F32))], 0)
        y = columns_of(x)
        z = dot_table_left(into_rows, jnp.concatenate([stacked(y, 0), stacked(y, 1)], 1))
        are, aim = z[:128, :128], z[128:, :128]
        bre, bim = z[:128, 128:], z[128:, 128:]
        reals, imags = [], []
        for m in range(MODES):
            h = [responses[1, m, i] for i in range(4)]
            reals.append(h[0] * are - h[1] * aim + (h[2] * bre - h[3] * bim))
            imags.append(h[0] * aim + h[1] * are + (h[2] * bim + h[3] * bre))
        spectrum = jnp.concatenate([jnp.concatenate(reals, 1), jnp.concatenate(imags, 1)], 0)
        v = dot_table_left(from_rows, spectrum)
        rows = [
            jnp.concatenate([v[:64, 128 * m : 128 * m + 128], v[64:, 128 * m : 128 * m + 128]], 1)
            for m in range(MODES)
        ]
        out = dot_table_right(jnp.concatenate(rows, 0), from_cols)
        return weights[0] * out[:64] + weights[1] * out[64:]

    def forward(values):
        x = jnp.concatenate(
            [
                (patch_weights[m, 64 * k : 64 * k + 64] * values[k]).astype(BF16)
                for m in range(MODES)
                for k in range(3)
            ],
            0,
        )
        y = columns_of(x)
        z = [
            dot_table_left(
                into_rows, jnp.concatenate([stacked(y[:192], k), stacked(y[192:], k)], 1)
            )
            for k in range(2)
        ]
        real = jnp.zeros((FREQS, FREQS), F32)
        imag = real
        for m in range(MODES):
            h = [responses[0, m, i] for i in range(4)]
            lanes = slice(128 * m, 128 * m + 128)
            are, aim = z[0][:128, lanes], z[0][128:, lanes]
            bre, bim = z[1][:128, lanes], z[1][128:, lanes]
            real = real + (h[0] * are - h[1] * aim + (h[2] * bre - h[3] * bim))
            imag = imag + (h[0] * aim + h[1] * are + (h[2] * bim + h[3] * bre))
        v = dot_table_left(from_rows, jnp.concatenate([real, imag], 0))
        return dot_table_right(jnp.concatenate([v[:64], v[64:]], 1), from_cols)

    def build_responses(m, c):
        narrow = taps[m, :, 0:128]
        even_lane = lax.broadcasted_iota(jnp.int32, (1, FREQS), 1) % 2 == 0
        sign_f = jnp.where(even_lane, 1.0, -1.0)
        even_row = lax.broadcasted_iota(jnp.int32, (FREQS, 1), 0) % 2 == 0
        sign_q = jnp.where(even_row, 1.0, -1.0)
        cols = dot(narrow, tap_cols[0]) + dot(narrow, tap_cols[1])
        re = cols[:, :128]
        im = cols[:, 128:] + taps[m, :, 128:129].astype(F32) * sign_f
        pairs = jnp.concatenate(
            [
                jnp.concatenate([re[0:64], re[64:128]], 1),
                jnp.concatenate([im[0:64], im[64:128]], 1),
            ],
            0,
        )
        g = dot_table_left(tap_rows, pairs)
        g0re, g0im, g1re, g1im = g[:128, :128], g[128:, :128], g[:128, 128:], g[128:, 128:]
        mid_re, mid_im, last_re, last_im = re[64:65], im[64:65], re[128:129], im[128:129]
        responses[0, m, 0] = g0re
        responses[0, m, 1] = g0im
        responses[0, m, 2] = g1re + sign_q * last_re
        responses[0, m, 3] = g1im + sign_q * last_im
        responses[1, m, 0] = sign_f * (sign_q * (g1im - mid_im) + last_im)
        responses[1, m, 1] = sign_f * (sign_q * (g1re - mid_re) + last_re)
        responses[1, m, 2] = sign_f * (sign_q * g0im + mid_im)
        responses[1, m, 3] = sign_f * (sign_q * g0re + mid_re)
        return c

    def fold(x):
        return jnp.sum(x, axis=0, keepdims=True)

    def share(which, source, member, count, place_of, slots, got_sems, sent_sems):
        slots[which, member] = sums[source]

        def go(d, c):
            pltpu.make_async_remote_copy(
                src_ref=sums.at[source],
                dst_ref=slots.at[which, member],
                send_sem=sent_sems.at[which],
                recv_sem=got_sems.at[which],
                device_id=place_of(d),
                device_id_type=MESH,
            ).start()
            return c

        lax.fori_loop(1, count, go, 0)

    def gathered(which, count, slots, got_sems):
        others = slots.at[which, pl.ds(0, count - 1)]
        pltpu.make_async_copy(others, others, got_sems.at[which]).wait()
        total = slots[which, 0]
        for i in range(1, count):
            total = total + slots[which, i]
        return total

    def start_sums(which):
        share(which, which, my_near, near_count, near, near_sums, near_got, near_sent)
        sums[2 + which] = gathered(which, near_count, near_sums, near_got)
        share(which, 2 + which, my_far, far_count, far, far_sums, far_got, far_sent)

    def whole(which):
        return jnp.sum(gathered(which, far_count, far_sums, far_got), axis=1, keepdims=True)

    def sums_sent(which):
        for count, slots, sent in ((near_count, near_sums, near_sent), (far_count, far_sums, far_sent)):
            others = slots.at[which, pl.ds(0, count - 1)]
            pltpu.make_async_copy(others, others, sent.at[which]).wait()

    zeros[...] = jnp.zeros_like(zeros)
    sums[...] = jnp.zeros_like(sums)
    for load in loads[:3]:
        load.wait()
    place(0, observed[...].astype(F32))
    place(1, (2 * probe[...] - 1).astype(F32))
    for m in range(MODES):
        place(2 * WEIGHT_STAGE + m, weights[m])
    pl.semaphore_wait(barrier, partners)
    for slot in (0, 1, 2 * WEIGHT_STAGE, 2 * WEIGHT_STAGE + 1):
        send(slot)
    for load in loads[3:]:
        load.wait()
    lax.fori_loop(0, MODES, build_responses, 0)

    def right_side(n, c):
        arrived(n)
        r = adjoint(n)
        first[n] = r
        place(2 + n, r)
        send(2 + n)
        return c

    lax.fori_loop(0, 2, right_side, 0)

    def spread_weights(m, c):
        slot = 2 * WEIGHT_STAGE + m
        arrived(slot)
        for k, b in enumerate(patch(slot, weights[m])):
            patch_weights[m, 64 * k : 64 * k + 64] = b
        return c

    lax.fori_loop(0, MODES, spread_weights, 0)

    def blur_first(n, c):
        arrived(2 + n)
        r = first[n]
        u = forward(patch(2 + n, r))
        place(4 + n, u)
        send(4 + n)
        sums[0, pl.ds(n, 1)] = fold(r * r)
        sums[0, pl.ds(2 + n, 1)] = fold(u * own[4 + n].astype(F32))
        return c

    lax.fori_loop(0, 2, blur_first, 0)
    start_sums(0)

    def back_first(n, c):
        arrived(4 + n)
        w = adjoint(4 + n) + DAMPING * first[n]
        image[n] = w
        place(6 + n, w)
        send(6 + n)
        return c

    lax.fori_loop(0, 2, back_first, 0)
    total = whole(0)
    norm0 = [total[n : n + 1] for n in range(2)]
    curve0 = [total[2 + n : 3 + n] + DAMPING * norm0[n] for n in range(2)]
    step0 = [norm0[n] / curve0[n] for n in range(2)]
    for n in range(2):
        steps[n] = jnp.broadcast_to(step0[n], (1, TILE_COLS))

    def blur_second(n, c):
        step = steps[n]
        r = first[n] - step * image[n]
        second[n] = r
        wide = jnp.concatenate([step, step], 1)
        before = patch(2 + n, first[n])
        arrived(6 + n)
        moved = patch(6 + n, image[n])
        u = forward([b - wide * w for b, w in zip(before, moved)])
        place(8 + n, u)
        send(8 + n)
        sums[1, pl.ds(n, 1)] = fold(r * r)
        sums[1, pl.ds(2 + n, 1)] = fold(u * own[8 + n].astype(F32))
        sums[1, pl.ds(4 + n, 1)] = fold(r * image[n])
        return c

    lax.fori_loop(0, 2, blur_second, 0)
    start_sums(1)

    def back_second(n, c):
        arrived(8 + n)
        residual_out[n] = adjoint(8 + n) + DAMPING * second[n]
        return c

    lax.fori_loop(0, 2, back_second, 0)
    total = whole(1)
    for n in range(2):
        norm1 = total[n : n + 1]
        ratio = norm1 / norm0[n]
        curve1 = (
            total[2 + n : 3 + n]
            + DAMPING * norm1
            + 2.0 * ratio * total[4 + n : 5 + n]
            + ratio * ratio * curve0[n]
        )
        step1 = norm1 / curve1
        r0, r1 = first[n], second[n]
        solution_out[n] = step0[n] * r0 + step1 * (r1 + ratio * r0)
        residual_out[n] = r1 - step1 * (residual_out[n] + ratio * image[n])

    all_sent()
    for which in range(2):
        sums_sent(which)


def solution(mesh):
    row_count, col_count = mesh.shape["row"], mesh.shape["col"]
    constants = tables()

    def shards(observed, probe_signs, weights, kernels):
        pair = (2, TILE_ROWS, TILE_COLS)
        vmem = pl.BlockSpec(memory_space=pltpu.VMEM)
        operands = [observed, probe_signs, weights, kernels, *[jnp.asarray(c) for c in constants]]
        return pl.pallas_call(
            functools.partial(kernel, row_count, col_count),
            out_shape=(jax.ShapeDtypeStruct(pair, F32), jax.ShapeDtypeStruct(pair, F32)),
            in_specs=[pl.BlockSpec(memory_space=pltpu.HBM)] * len(operands),
            out_specs=(vmem, vmem),
            scratch_shapes=[
                *[pltpu.VMEM(x.shape, x.dtype) for x in operands],
                pltpu.VMEM((SLOTS, 320, TILE_COLS), BF16),
                pltpu.VMEM((SLOTS, TILE_ROWS, TILE_COLS), BF16),
                pltpu.VMEM((SLOTS, TILE_ROWS, TILE_COLS), BF16),
                pltpu.VMEM((TILE_ROWS, TILE_COLS), BF16),
                pltpu.VMEM((MODES, 3 * TILE_ROWS, 2 * TILE_COLS), F32),
                pltpu.VMEM((2, MODES, 4, FREQS, FREQS), F32),
                pltpu.VMEM(pair, F32),
                pltpu.VMEM(pair, F32),
                pltpu.VMEM(pair, F32),
                pltpu.VMEM((2, 1, TILE_COLS), F32),
                pltpu.VMEM((4, 8, TILE_COLS), F32),
                pltpu.VMEM((2, 8, 8, TILE_COLS), F32),
                pltpu.VMEM((2, row_count * col_count // 8, 8, TILE_COLS), F32),
                pltpu.SemaphoreType.DMA((len(operands),)),
                pltpu.SemaphoreType.DMA((SLOTS,)),
                pltpu.SemaphoreType.DMA((8,)),
                pltpu.SemaphoreType.DMA((2,)),
                pltpu.SemaphoreType.DMA((2,)),
                pltpu.SemaphoreType.DMA((2,)),
                pltpu.SemaphoreType.DMA((2,)),
            ],
            compiler_params=pltpu.CompilerParams(
                collective_id=0, has_side_effects=True, vmem_limit_bytes=60 * 2**20
            ),
            name="deconvolve",
        )(*operands)

    return jax.shard_map(
        shards,
        mesh=mesh,
        in_specs=(P("row", "col"), P("row", "col"), P(None, "row", "col"), P()),
        out_specs=(P(None, "row", "col"), P(None, "row", "col")),
        check_vma=False,
    )
```

```python
import functools

import jax
import jax.numpy as jnp
import ml_dtypes
import numpy as np
from jax import lax
from jax.experimental import pallas as pl
from jax.experimental.pallas import tpu as pltpu
from jax.sharding import PartitionSpec as P

RADIUS = 64
MODES = 2
DAMPING = 1.0
TILE_ROWS = 64
TILE_COLS = 128
FREQS = 128
TAPS = 2 * RADIUS + 1
BF16 = jnp.bfloat16
F32 = jnp.float32
MESH = pl.DeviceIdType.MESH

WEIGHT_STAGE = 5
SLOTS = 12


def split(table):
    high = table.astype(ml_dtypes.bfloat16)
    low = (table - high.astype(np.float64)).astype(ml_dtypes.bfloat16)
    return np.stack([high, low])


def tables():
    theta = 2 * np.pi * (np.arange(FREQS) + 0.5) / 256
    phi = 2 * np.pi * np.arange(FREQS) / 128
    column = np.concatenate([64 + np.arange(128), 192 + np.arange(64), np.arange(64)])
    arg = np.outer(column, theta)
    into_cols = np.concatenate([np.cos(arg), -np.sin(arg)], 1)
    pieces = []
    for block in range(2):
        arg = np.outer(phi, 64 * block + np.arange(64))
        pieces.append(np.block([[np.cos(arg), np.sin(arg)], [-np.sin(arg), np.cos(arg)]]))
    into_rows = np.concatenate(pieces, 1)
    arg = np.outer(np.arange(64), phi)
    from_rows = np.block([[np.cos(arg), -np.sin(arg)], [np.sin(arg), np.cos(arg)]]) / 128
    arg = np.outer(theta, np.arange(128))
    from_cols = np.concatenate([np.cos(arg), -np.sin(arg)], 0) / 128
    arg = np.outer(np.arange(128), theta)
    tap_cols = np.concatenate([np.cos(arg), np.sin(arg)], 1)
    arg = np.outer(phi, np.arange(64))
    tap_rows = np.block([[np.cos(arg), -np.sin(arg)], [np.sin(arg), np.cos(arg)]])
    return [split(t) for t in (into_cols, into_rows, from_rows, from_cols, tap_cols, tap_rows)]


def dot(a, b):
    return jnp.dot(a, b, preferred_element_type=F32)


def halves(x):
    high = x.astype(BF16)
    return high, (x - high.astype(F32)).astype(BF16)


def dot_table_left(table, x):
    high, low = halves(x)
    return dot(table[0], high) + (dot(table[0], low) + dot(table[1], high))


def dot_table_right(x, table):
    high, low = halves(x)
    return dot(high, table[0]) + (dot(low, table[0]) + dot(high, table[1]))


def kernel(
    row_count,
    col_count,
    observed_hbm,
    probe_hbm,
    weights_hbm,
    taps_hbm,
    into_cols_hbm,
    into_rows_hbm,
    from_rows_hbm,
    from_cols_hbm,
    tap_cols_hbm,
    tap_rows_hbm,
    solution_out,
    residual_out,
    observed,
    probe,
    weights,
    taps,
    into_cols,
    into_rows,
    from_rows,
    from_cols,
    tap_cols,
    tap_rows,
    got,
    own,
    packed,
    zeros,
    planes,
    patch_weights,
    responses,
    first,
    image,
    second,
    steps,
    sums,
    near_sums,
    far_sums,
    load_sem,
    got_sem,
    sent_sem,
    near_got,
    near_sent,
    far_got,
    far_sent,
):
    my_row = lax.axis_index("row")
    my_col = lax.axis_index("col")
    up_ok, down_ok = my_row > 0, my_row < row_count - 1
    left_ok, right_ok = my_col > 0, my_col < col_count - 1

    loads = [
        pltpu.make_async_copy(src, dst, load_sem.at[i])
        for i, (src, dst) in enumerate(
            (
                (observed_hbm, observed),
                (probe_hbm, probe),
                (weights_hbm, weights),
                (taps_hbm, taps),
                (tap_cols_hbm, tap_cols),
                (tap_rows_hbm, tap_rows),
                (into_cols_hbm, into_cols),
                (into_rows_hbm, into_rows),
                (from_rows_hbm, from_rows),
                (from_cols_hbm, from_cols),
            )
        )
    ]
    for load in loads:
        load.start()

    barrier = pltpu.get_barrier_semaphore()

    def greet(row, col):
        pl.semaphore_signal(barrier, inc=1, device_id=(row, col), device_id_type=MESH)

    z_count, y_count = row_count // 2, col_count // 4
    near_count, far_count = 8, z_count * y_count
    my_x_low, my_z = lax.rem(my_row, 2), my_row // 2
    my_core, my_y, my_x_high = lax.rem(my_col, 2), lax.rem(my_col // 2, y_count), my_col // (2 * y_count)
    my_near = my_x_high * 4 + my_x_low * 2 + my_core
    my_far = my_z * y_count + my_y

    def near(d):
        x_high = lax.rem(my_x_high + d // 4, 2)
        x_low = lax.rem(my_x_low + lax.rem(d // 2, 2), 2)
        core = lax.rem(my_core + lax.rem(d, 2), 2)
        return my_z * 2 + x_low, x_high * 2 * y_count + my_y * 2 + core

    def far(d):
        z = lax.rem(my_z + d // y_count, z_count)
        y = lax.rem(my_y + lax.rem(d, y_count), y_count)
        return z * 2 + my_x_low, my_x_high * 2 * y_count + y * 2 + my_core

    def greet_near(d, c):
        greet(*near(d))
        return c

    def greet_far(d, c):
        greet(*far(d))
        return c

    lax.fori_loop(1, far_count, greet_far, 0)
    lax.fori_loop(1, near_count, greet_near, 0)
    neighbours = []
    for dr, row_ok in ((-1, up_ok), (1, down_ok), (0, None)):
        for dc, col_ok in ((0, None), (-1, left_ok), (1, right_ok)):
            if dr or dc:
                there = row_ok if col_ok is None else col_ok if row_ok is None else row_ok & col_ok
                neighbours.append((dr, dc, there))
    for dr, dc, there in neighbours:
        pl.when(there)(functools.partial(greet, my_row + dr, my_col + dc))
    rows_here = 1 + up_ok.astype(jnp.int32) + down_ok.astype(jnp.int32)
    cols_here = 1 + left_ok.astype(jnp.int32) + right_ok.astype(jnp.int32)
    partners = rows_here * cols_here - 1 + (near_count - 1) + (far_count - 1)

    lane = lax.broadcasted_iota(jnp.int32, (32, TILE_COLS), 1)
    low_lanes = lane < 64

    def place(slot, tile):
        own[slot] = tile.astype(BF16)
        turned = pltpu.roll(tile, 64, 1)
        packed[slot, 0:32] = jnp.where(low_lanes, tile[0:32], turned[32:64]).astype(BF16)
        packed[slot, 32:64] = jnp.where(low_lanes, turned[0:32], tile[32:64]).astype(BF16)

    def landing(slot, dr, dc):
        if dc == 0:
            return got.at[slot, pl.ds(0 if dr < 0 else 64, 64)]
        return got.at[slot, pl.ds(128 + 64 * (1 + dr) + (32 if dc < 0 else 0), 32)]

    def send(slot):
        for i, (dr, dc, there) in enumerate(neighbours):
            if dc == 0:
                piece = own.at[slot]
            else:
                piece = packed.at[slot, pl.ds(0 if dc < 0 else 32, 32)]
            out = pltpu.make_async_remote_copy(
                src_ref=piece,
                dst_ref=landing(slot, -dr, -dc),
                send_sem=sent_sem.at[i],
                recv_sem=got_sem.at[slot],
                device_id=(my_row + dr, my_col + dc),
                device_id_type=MESH,
            )
            edge = landing(slot, dr, dc)
            fill = pltpu.make_async_copy(zeros.at[pl.ds(0, edge.shape[0])], edge, got_sem.at[slot])
            lax.cond(there, lambda out=out: out.start(), lambda fill=fill: fill.start())

    def arrived(slot):
        pltpu.make_async_copy(got.at[slot], got.at[slot], got_sem.at[slot]).wait()

    def all_sent():
        for i, (dr, dc, there) in enumerate(neighbours):
            every = got.at[:, pl.ds(0, 64 if dc == 0 else 32)]
            pl.when(there)(pltpu.make_async_copy(every, every, sent_sem.at[i]).wait)

    def halo(slot, k):
        right = got[slot, 128 + 64 * k : 160 + 64 * k].astype(F32)
        left = got[slot, 160 + 64 * k : 192 + 64 * k].astype(F32)
        top = jnp.where(low_lanes, right, pltpu.roll(left, 64, 1))
        bottom = jnp.where(low_lanes, pltpu.roll(right, 64, 1), left)
        return jnp.concatenate([top, bottom], 0)

    def patch(slot, middle):
        above, below = got[slot, 0:64].astype(F32), got[slot, 64:128].astype(F32)
        return [
            jnp.concatenate([tile, halo(slot, k)], 1) for k, tile in enumerate((above, middle, below))
        ]

    def columns_of(x):
        return dot(x, into_cols[0]) + dot(x, into_cols[1])

    def stacked(y, k):
        parts = []
        for b in (k, k + 1):
            rows = y[64 * b : 64 * b + 64]
            parts += [rows[:, :128], rows[:, 128:]]
        return jnp.concatenate(parts, 0)

    def adjoint(slot):
        x = jnp.concatenate([b.astype(BF16) for b in patch(slot, own[slot].astype(F32))], 0)
        y = columns_of(x)
        z = dot_table_left(into_rows, jnp.concatenate([stacked(y, 0), stacked(y, 1)], 1))
        are, aim = z[:128, :128], z[128:, :128]
        bre, bim = z[:128, 128:], z[128:, 128:]
        reals, imags = [], []
        for m in range(MODES):
            h = [responses[1, m, i] for i in range(4)]
            reals.append(h[0] * are - h[1] * aim + (h[2] * bre - h[3] * bim))
            imags.append(h[0] * aim + h[1] * are + (h[2] * bim + h[3] * bre))
        spectrum = jnp.concatenate([jnp.concatenate(reals, 1), jnp.concatenate(imags, 1)], 0)
        v = dot_table_left(from_rows, spectrum)
        rows = [
            jnp.concatenate([v[:64, 128 * m : 128 * m + 128], v[64:, 128 * m : 128 * m + 128]], 1)
            for m in range(MODES)
        ]
        out = dot_table_right(jnp.concatenate(rows, 0), from_cols)
        return weights[0] * out[:64] + weights[1] * out[64:]

    def forward(values):
        x = jnp.concatenate(
            [
                (patch_weights[m, 64 * k : 64 * k + 64] * values[k]).astype(BF16)
                for m in range(MODES)
                for k in range(3)
            ],
            0,
        )
        y = columns_of(x)
        z = [
            dot_table_left(
                into_rows, jnp.concatenate([stacked(y[:192], k), stacked(y[192:], k)], 1)
            )
            for k in range(2)
        ]
        real = jnp.zeros((FREQS, FREQS), F32)
        imag = real
        for m in range(MODES):
            h = [responses[0, m, i] for i in range(4)]
            lanes = slice(128 * m, 128 * m + 128)
            are, aim = z[0][:128, lanes], z[0][128:, lanes]
            bre, bim = z[1][:128, lanes], z[1][128:, lanes]
            real = real + (h[0] * are - h[1] * aim + (h[2] * bre - h[3] * bim))
            imag = imag + (h[0] * aim + h[1] * are + (h[2] * bim + h[3] * bre))
        v = dot_table_left(from_rows, jnp.concatenate([real, imag], 0))
        return dot_table_right(jnp.concatenate([v[:64], v[64:]], 1), from_cols)

    def build_responses(m, c):
        narrow = planes[m, :, 0:128].astype(BF16)
        even_lane = lax.broadcasted_iota(jnp.int32, (1, FREQS), 1) % 2 == 0
        sign_f = jnp.where(even_lane, 1.0, -1.0)
        even_row = lax.broadcasted_iota(jnp.int32, (FREQS, 1), 0) % 2 == 0
        sign_q = jnp.where(even_row, 1.0, -1.0)
        cols = dot(narrow, tap_cols[0]) + dot(narrow, tap_cols[1])
        re = cols[:, :128]
        im = cols[:, 128:] + planes[m, :, 128:129] * sign_f
        pairs = jnp.concatenate(
            [
                jnp.concatenate([re[0:64], re[64:128]], 1),
                jnp.concatenate([im[0:64], im[64:128]], 1),
            ],
            0,
        )
        g = dot_table_left(tap_rows, pairs)
        g0re, g0im, g1re, g1im = g[:128, :128], g[128:, :128], g[:128, 128:], g[128:, 128:]
        mid_re, mid_im, last_re, last_im = re[64:65], im[64:65], re[128:129], im[128:129]
        responses[0, m, 0] = g0re
        responses[0, m, 1] = g0im
        responses[0, m, 2] = g1re + sign_q * last_re
        responses[0, m, 3] = g1im + sign_q * last_im
        responses[1, m, 0] = sign_f * (sign_q * (g1im - mid_im) + last_im)
        responses[1, m, 1] = sign_f * (sign_q * (g1re - mid_re) + last_re)
        responses[1, m, 2] = sign_f * (sign_q * g0im + mid_im)
        responses[1, m, 3] = sign_f * (sign_q * g0re + mid_re)
        return c

    def fold(x):
        return jnp.sum(x, axis=0, keepdims=True)

    def share(which, source, member, count, place_of, slots, got_sems, sent_sems):
        slots[which, member] = sums[source]

        def go(d, c):
            pltpu.make_async_remote_copy(
                src_ref=sums.at[source],
                dst_ref=slots.at[which, member],
                send_sem=sent_sems.at[which],
                recv_sem=got_sems.at[which],
                device_id=place_of(d),
                device_id_type=MESH,
            ).start()
            return c

        lax.fori_loop(1, count, go, 0)

    def gathered(which, count, slots, got_sems):
        others = slots.at[which, pl.ds(0, count - 1)]
        pltpu.make_async_copy(others, others, got_sems.at[which]).wait()
        total = slots[which, 0]
        for i in range(1, count):
            total = total + slots[which, i]
        return total

    def start_sums(which):
        share(which, which, my_near, near_count, near, near_sums, near_got, near_sent)
        sums[2 + which] = gathered(which, near_count, near_sums, near_got)
        share(which, 2 + which, my_far, far_count, far, far_sums, far_got, far_sent)

    def whole(which):
        return jnp.sum(gathered(which, far_count, far_sums, far_got), axis=1, keepdims=True)

    def sums_sent(which):
        for count, slots, sent in ((near_count, near_sums, near_sent), (far_count, far_sums, far_sent)):
            others = slots.at[which, pl.ds(0, count - 1)]
            pltpu.make_async_copy(others, others, sent.at[which]).wait()

    zeros[...] = jnp.zeros_like(zeros)
    sums[...] = jnp.zeros_like(sums)
    for load in loads[:3]:
        load.wait()
    place(0, observed[...].astype(F32))
    place(1, (2 * probe[...] - 1).astype(F32))
    for m in range(MODES):
        place(2 * WEIGHT_STAGE + m, weights[m])
    pl.semaphore_wait(barrier, partners)
    for slot in (0, 1, 2 * WEIGHT_STAGE, 2 * WEIGHT_STAGE + 1):
        send(slot)
    for load in loads[3:]:
        load.wait()
    for m in range(MODES):
        planes[m] = taps[:, m, :].astype(F32)
    lax.fori_loop(0, MODES, build_responses, 0)

    def right_side(n, c):
        arrived(n)
        r = adjoint(n)
        first[n] = r
        place(2 + n, r)
        send(2 + n)
        return c

    lax.fori_loop(0, 2, right_side, 0)

    def spread_weights(m, c):
        slot = 2 * WEIGHT_STAGE + m
        arrived(slot)
        for k, b in enumerate(patch(slot, weights[m])):
            patch_weights[m, 64 * k : 64 * k + 64] = b
        return c

    lax.fori_loop(0, MODES, spread_weights, 0)

    def blur_first(n, c):
        arrived(2 + n)
        r = first[n]
        u = forward(patch(2 + n, r))
        place(4 + n, u)
        send(4 + n)
        sums[0, pl.ds(n, 1)] = fold(r * r)
        sums[0, pl.ds(2 + n, 1)] = fold(u * own[4 + n].astype(F32))
        return c

    lax.fori_loop(0, 2, blur_first, 0)
    start_sums(0)

    def back_first(n, c):
        arrived(4 + n)
        w = adjoint(4 + n) + DAMPING * first[n]
        image[n] = w
        place(6 + n, w)
        send(6 + n)
        return c

    lax.fori_loop(0, 2, back_first, 0)
    total = whole(0)
    norm0 = [total[n : n + 1] for n in range(2)]
    curve0 = [total[2 + n : 3 + n] + DAMPING * norm0[n] for n in range(2)]
    step0 = [norm0[n] / curve0[n] for n in range(2)]
    for n in range(2):
        steps[n] = jnp.broadcast_to(step0[n], (1, TILE_COLS))

    def blur_second(n, c):
        step = steps[n]
        r = first[n] - step * image[n]
        second[n] = r
        wide = jnp.concatenate([step, step], 1)
        before = patch(2 + n, first[n])
        arrived(6 + n)
        moved = patch(6 + n, image[n])
        u = forward([b - wide * w for b, w in zip(before, moved)])
        place(8 + n, u)
        send(8 + n)
        sums[1, pl.ds(n, 1)] = fold(r * r)
        sums[1, pl.ds(2 + n, 1)] = fold(u * own[8 + n].astype(F32))
        sums[1, pl.ds(4 + n, 1)] = fold(r * image[n])
        return c

    lax.fori_loop(0, 2, blur_second, 0)
    start_sums(1)

    def back_second(n, c):
        arrived(8 + n)
        residual_out[n] = adjoint(8 + n) + DAMPING * second[n]
        return c

    lax.fori_loop(0, 2, back_second, 0)
    total = whole(1)
    for n in range(2):
        norm1 = total[n : n + 1]
        ratio = norm1 / norm0[n]
        curve1 = (
            total[2 + n : 3 + n]
            + DAMPING * norm1
            + 2.0 * ratio * total[4 + n : 5 + n]
            + ratio * ratio * curve0[n]
        )
        step1 = norm1 / curve1
        r0, r1 = first[n], second[n]
        solution_out[n] = step0[n] * r0 + step1 * (r1 + ratio * r0)
        residual_out[n] = r1 - step1 * (residual_out[n] + ratio * image[n])

    all_sent()
    for which in range(2):
        sums_sent(which)


def solution(mesh):
    row_count, col_count = mesh.shape["row"], mesh.shape["col"]
    constants = tables()

    def shards(observed, probe_signs, weights, kernels):
        pair = (2, TILE_ROWS, TILE_COLS)
        vmem = pl.BlockSpec(memory_space=pltpu.VMEM)
        operands = [observed, probe_signs, weights, jnp.transpose(kernels, (1, 0, 2)), *[jnp.asarray(c) for c in constants]]
        return pl.pallas_call(
            functools.partial(kernel, row_count, col_count),
            out_shape=(jax.ShapeDtypeStruct(pair, F32), jax.ShapeDtypeStruct(pair, F32)),
            in_specs=[pl.BlockSpec(memory_space=pltpu.HBM)] * len(operands),
            out_specs=(vmem, vmem),
            scratch_shapes=[
                *[pltpu.VMEM(x.shape, x.dtype) for x in operands],
                pltpu.VMEM((SLOTS, 320, TILE_COLS), BF16),
                pltpu.VMEM((SLOTS, TILE_ROWS, TILE_COLS), BF16),
                pltpu.VMEM((SLOTS, TILE_ROWS, TILE_COLS), BF16),
                pltpu.VMEM((TILE_ROWS, TILE_COLS), BF16),
                pltpu.VMEM((MODES, TAPS, TAPS), F32),
                pltpu.VMEM((MODES, 3 * TILE_ROWS, 2 * TILE_COLS), F32),
                pltpu.VMEM((2, MODES, 4, FREQS, FREQS), F32),
                pltpu.VMEM(pair, F32),
                pltpu.VMEM(pair, F32),
                pltpu.VMEM(pair, F32),
                pltpu.VMEM((2, 1, TILE_COLS), F32),
                pltpu.VMEM((4, 8, TILE_COLS), F32),
                pltpu.VMEM((2, 8, 8, TILE_COLS), F32),
                pltpu.VMEM((2, row_count * col_count // 8, 8, TILE_COLS), F32),
                pltpu.SemaphoreType.DMA((len(operands),)),
                pltpu.SemaphoreType.DMA((SLOTS,)),
                pltpu.SemaphoreType.DMA((8,)),
                pltpu.SemaphoreType.DMA((2,)),
                pltpu.SemaphoreType.DMA((2,)),
                pltpu.SemaphoreType.DMA((2,)),
                pltpu.SemaphoreType.DMA((2,)),
            ],
            compiler_params=pltpu.CompilerParams(
                collective_id=0, has_side_effects=True, vmem_limit_bytes=32 * 2**20
            ),
            name="deconvolve",
        )(*[pltpu.with_memory_space_constraint(x, pltpu.HBM) for x in operands])

    return jax.shard_map(
        shards,
        mesh=mesh,
        in_specs=(P("row", "col"), P("row", "col"), P(None, "row", "col"), P()),
        out_specs=(P(None, "row", "col"), P(None, "row", "col")),
        check_vma=False,
    )
```

```python
import functools

import jax
import jax.numpy as jnp
import ml_dtypes
import numpy as np
from jax import lax
from jax.experimental import pallas as pl
from jax.experimental.pallas import tpu as pltpu
from jax.sharding import PartitionSpec as P

RADIUS = 64
MODES = 2
DAMPING = 1.0
TILE_ROWS = 64
TILE_COLS = 128
FREQS = 128
TAPS = 2 * RADIUS + 1
BF16 = jnp.bfloat16
F32 = jnp.float32
MESH = pl.DeviceIdType.MESH

WEIGHT_STAGE = 5
SLOTS = 12


def split(table):
    high = table.astype(ml_dtypes.bfloat16)
    low = (table - high.astype(np.float64)).astype(ml_dtypes.bfloat16)
    return np.stack([high, low])


def tables():
    theta = 2 * np.pi * (np.arange(FREQS) + 0.5) / 256
    phi = 2 * np.pi * np.arange(FREQS) / 128
    column = np.concatenate([64 + np.arange(128), 192 + np.arange(64), np.arange(64)])
    arg = np.outer(column, theta)
    into_cols = np.concatenate([np.cos(arg), -np.sin(arg)], 1)
    pieces = []
    for block in range(2):
        arg = np.outer(phi, 64 * block + np.arange(64))
        pieces.append(np.block([[np.cos(arg), np.sin(arg)], [-np.sin(arg), np.cos(arg)]]))
    into_rows = np.concatenate(pieces, 1)
    arg = np.outer(np.arange(64), phi)
    from_rows = np.block([[np.cos(arg), -np.sin(arg)], [np.sin(arg), np.cos(arg)]]) / 128
    arg = np.outer(theta, np.arange(128))
    from_cols = np.concatenate([np.cos(arg), -np.sin(arg)], 0) / 128
    arg = np.outer(np.arange(128), theta)
    tap_cols = np.concatenate([np.cos(arg), np.sin(arg)], 1)
    arg = np.outer(phi, np.arange(64))
    tap_rows = np.block([[np.cos(arg), -np.sin(arg)], [np.sin(arg), np.cos(arg)]])
    return [split(t) for t in (into_cols, into_rows, from_rows, from_cols, tap_cols, tap_rows)]


def dot(a, b):
    return jnp.dot(a, b, preferred_element_type=F32)


def halves(x):
    high = x.astype(BF16)
    return high, (x - high.astype(F32)).astype(BF16)


def dot_table_left(table, x):
    high, low = halves(x)
    rows = table.shape[1]
    both = dot(table[...].reshape(2 * rows, table.shape[2]), high)
    return both[:rows] + (both[rows:] + dot(table[0], low))


def dot_table_right(x, table):
    high, low = halves(x)
    rows = x.shape[0]
    both = dot(jnp.concatenate([high, low], 0), table[0])
    return both[:rows] + (both[rows:] + dot(high, table[1]))


def kernel(
    row_count,
    col_count,
    observed_hbm,
    probe_hbm,
    weights_hbm,
    taps_hbm,
    into_cols_hbm,
    into_rows_hbm,
    from_rows_hbm,
    from_cols_hbm,
    tap_cols_hbm,
    tap_rows_hbm,
    solution_out,
    residual_out,
    observed,
    probe,
    weights,
    taps,
    into_cols,
    into_rows,
    from_rows,
    from_cols,
    tap_cols,
    tap_rows,
    got,
    own,
    packed,
    zeros,
    planes,
    patch_weights,
    responses,
    first,
    image,
    second,
    parts,
    near_mine,
    far_mine,
    near_sums,
    far_sums,
    load_sem,
    got_sem,
    sent_sem,
    near_got,
    near_sent,
    far_got,
    far_sent,
):
    my_row = lax.axis_index("row")
    my_col = lax.axis_index("col")
    up_ok, down_ok = my_row > 0, my_row < row_count - 1
    left_ok, right_ok = my_col > 0, my_col < col_count - 1

    loads = [
        pltpu.make_async_copy(src, dst, load_sem.at[i])
        for i, (src, dst) in enumerate(
            (
                (observed_hbm, observed),
                (probe_hbm, probe),
                (weights_hbm, weights),
                (taps_hbm, taps),
                (tap_cols_hbm, tap_cols),
                (tap_rows_hbm, tap_rows),
                (into_cols_hbm, into_cols),
                (into_rows_hbm, into_rows),
                (from_rows_hbm, from_rows),
                (from_cols_hbm, from_cols),
            )
        )
    ]
    for load in loads:
        load.start()

    barrier = pltpu.get_barrier_semaphore()

    def greet(row, col):
        pl.semaphore_signal(barrier, inc=1, device_id=(row, col), device_id_type=MESH)

    z_count, y_count = row_count // 2, col_count // 4
    near_count, far_count = 8, z_count * y_count
    my_x_low, my_z = lax.rem(my_row, 2), my_row // 2
    my_core, my_y, my_x_high = lax.rem(my_col, 2), lax.rem(my_col // 2, y_count), my_col // (2 * y_count)
    my_near = my_x_high * 4 + my_x_low * 2 + my_core
    my_far = my_z * y_count + my_y

    def near(d):
        x_high = lax.rem(my_x_high + d // 4, 2)
        x_low = lax.rem(my_x_low + lax.rem(d // 2, 2), 2)
        core = lax.rem(my_core + lax.rem(d, 2), 2)
        return my_z * 2 + x_low, x_high * 2 * y_count + my_y * 2 + core

    def far(d):
        z = lax.rem(my_z + d // y_count, z_count)
        y = lax.rem(my_y + lax.rem(d, y_count), y_count)
        return z * 2 + my_x_low, my_x_high * 2 * y_count + y * 2 + my_core

    def greet_near(d, c):
        greet(*near(d))
        return c

    def greet_far(d, c):
        greet(*far(d))
        return c

    lax.fori_loop(1, far_count, greet_far, 0)
    lax.fori_loop(1, near_count, greet_near, 0)
    row_there, col_there = {-1: up_ok, 1: down_ok}, {-1: left_ok, 1: right_ok}
    neighbours = [(dr, dc, row_there[dr] & col_there[dc]) for dr in (-1, 1) for dc in (-1, 1)]
    neighbours += [(dr, 0, row_there[dr]) for dr in (-1, 1)]
    neighbours += [(0, dc, col_there[dc]) for dc in (-1, 1)]
    for dr, dc, there in neighbours:
        pl.when(there)(functools.partial(greet, my_row + dr, my_col + dc))
    rows_here = 1 + up_ok.astype(jnp.int32) + down_ok.astype(jnp.int32)
    cols_here = 1 + left_ok.astype(jnp.int32) + right_ok.astype(jnp.int32)
    partners = rows_here * cols_here - 1 + (near_count - 1) + (far_count - 1)

    lane = lax.broadcasted_iota(jnp.int32, (32, TILE_COLS), 1)
    low_lanes = lane < 64

    def place(slot, tile):
        own[slot] = tile.astype(BF16)
        turned = pltpu.roll(tile, 64, 1)
        packed[slot, 0:32] = jnp.where(low_lanes, tile[0:32], turned[32:64]).astype(BF16)
        packed[slot, 32:64] = jnp.where(low_lanes, turned[0:32], tile[32:64]).astype(BF16)

    def landing(slot, dr, dc):
        if dc == 0:
            return got.at[slot, pl.ds(0 if dr < 0 else 64, 64)]
        return got.at[slot, pl.ds(128 + 64 * (1 + dr) + (32 if dc < 0 else 0), 32)]

    def send(slot):
        for i, (dr, dc, there) in enumerate(neighbours):
            if dc == 0:
                piece = own.at[slot]
            else:
                piece = packed.at[slot, pl.ds(0 if dc < 0 else 32, 32)]
            out = pltpu.make_async_remote_copy(
                src_ref=piece,
                dst_ref=landing(slot, -dr, -dc),
                send_sem=sent_sem.at[i],
                recv_sem=got_sem.at[slot],
                device_id=(my_row + dr, my_col + dc),
                device_id_type=MESH,
            )
            pl.when(there)(out.start)

    def fill_edges(slot, c):
        for dr, dc, there in neighbours:
            edge = landing(slot, dr, dc)
            fill = pltpu.make_async_copy(zeros.at[pl.ds(0, edge.shape[0])], edge, got_sem.at[slot])
            pl.when(jnp.logical_not(there))(fill.start)
        return c

    def arrived(slot):
        pltpu.make_async_copy(got.at[slot], got.at[slot], got_sem.at[slot]).wait()

    def all_sent():
        for i, (dr, dc, there) in enumerate(neighbours):
            every = got.at[:, pl.ds(0, 64 if dc == 0 else 32)]
            pl.when(there)(pltpu.make_async_copy(every, every, sent_sem.at[i]).wait)

    def halo(slot, k):
        right = got[slot, 128 + 64 * k : 160 + 64 * k].astype(F32)
        left = got[slot, 160 + 64 * k : 192 + 64 * k].astype(F32)
        top = jnp.where(low_lanes, right, pltpu.roll(left, 64, 1))
        bottom = jnp.where(low_lanes, pltpu.roll(right, 64, 1), left)
        return jnp.concatenate([top, bottom], 0)

    def patch(slot, middle):
        above, below = got[slot, 0:64].astype(F32), got[slot, 64:128].astype(F32)
        return [
            jnp.concatenate([tile, halo(slot, k)], 1) for k, tile in enumerate((above, middle, below))
        ]

    def columns_of(x):
        return dot(x, into_cols[0]) + dot(x, into_cols[1])

    def stacked(y, k):
        parts = []
        for b in (k, k + 1):
            rows = y[64 * b : 64 * b + 64]
            parts += [rows[:, :128], rows[:, 128:]]
        return jnp.concatenate(parts, 0)

    def adjoint(slot):
        x = jnp.concatenate([b.astype(BF16) for b in patch(slot, own[slot].astype(F32))], 0)
        y = columns_of(x)
        z = dot_table_left(into_rows, jnp.concatenate([stacked(y, 0), stacked(y, 1)], 1))
        are, aim = z[:128, :128], z[128:, :128]
        bre, bim = z[:128, 128:], z[128:, 128:]
        reals, imags = [], []
        for m in range(MODES):
            h = [responses[1, m, i] for i in range(4)]
            reals.append(h[0] * are - h[1] * aim + (h[2] * bre - h[3] * bim))
            imags.append(h[0] * aim + h[1] * are + (h[2] * bim + h[3] * bre))
        spectrum = jnp.concatenate([jnp.concatenate(reals, 1), jnp.concatenate(imags, 1)], 0)
        v = dot_table_left(from_rows, spectrum)
        rows = [
            jnp.concatenate([v[:64, 128 * m : 128 * m + 128], v[64:, 128 * m : 128 * m + 128]], 1)
            for m in range(MODES)
        ]
        out = dot_table_right(jnp.concatenate(rows, 0), from_cols)
        return weights[0] * out[:64] + weights[1] * out[64:]

    def forward(values):
        x = jnp.concatenate(
            [
                (patch_weights[m, 64 * k : 64 * k + 64] * values[k]).astype(BF16)
                for m in range(MODES)
                for k in range(3)
            ],
            0,
        )
        y = columns_of(x)
        z = [
            dot_table_left(
                into_rows, jnp.concatenate([stacked(y[:192], k), stacked(y[192:], k)], 1)
            )
            for k in range(2)
        ]
        real = jnp.zeros((FREQS, FREQS), F32)
        imag = real
        for m in range(MODES):
            h = [responses[0, m, i] for i in range(4)]
            lanes = slice(128 * m, 128 * m + 128)
            are, aim = z[0][:128, lanes], z[0][128:, lanes]
            bre, bim = z[1][:128, lanes], z[1][128:, lanes]
            real = real + (h[0] * are - h[1] * aim + (h[2] * bre - h[3] * bim))
            imag = imag + (h[0] * aim + h[1] * are + (h[2] * bim + h[3] * bre))
        v = dot_table_left(from_rows, jnp.concatenate([real, imag], 0))
        return dot_table_right(jnp.concatenate([v[:64], v[64:]], 1), from_cols)

    def build_responses(m, c):
        narrow = planes[m, :, 0:128].astype(BF16)
        even_lane = lax.broadcasted_iota(jnp.int32, (1, FREQS), 1) % 2 == 0
        sign_f = jnp.where(even_lane, 1.0, -1.0)
        even_row = lax.broadcasted_iota(jnp.int32, (FREQS, 1), 0) % 2 == 0
        sign_q = jnp.where(even_row, 1.0, -1.0)
        cols = dot(narrow, tap_cols[0]) + dot(narrow, tap_cols[1])
        re = cols[:, :128]
        im = cols[:, 128:] + planes[m, :, 128:129] * sign_f
        pairs = jnp.concatenate(
            [
                jnp.concatenate([re[0:64], re[64:128]], 1),
                jnp.concatenate([im[0:64], im[64:128]], 1),
            ],
            0,
        )
        g = dot_table_left(tap_rows, pairs)
        g0re, g0im, g1re, g1im = g[:128, :128], g[128:, :128], g[:128, 128:], g[128:, 128:]
        mid_re, mid_im, last_re, last_im = re[64:65], im[64:65], re[128:129], im[128:129]
        responses[0, m, 0] = g0re
        responses[0, m, 1] = g0im
        responses[0, m, 2] = g1re + sign_q * last_re
        responses[0, m, 3] = g1im + sign_q * last_im
        responses[1, m, 0] = sign_f * (sign_q * (g1im - mid_im) + last_im)
        responses[1, m, 1] = sign_f * (sign_q * (g1re - mid_re) + last_re)
        responses[1, m, 2] = sign_f * (sign_q * g0im + mid_im)
        responses[1, m, 3] = sign_f * (sign_q * g0re + mid_re)
        return c

    def note(n, i, part):
        parts[pl.ds(6 * n + i, 1)] = jnp.sum(part, axis=0, keepdims=True)

    def share(source, member, count, place_of, slots, got_sems, sent_sems):
        slots[member] = source[...]

        def go(d, c):
            pltpu.make_async_remote_copy(
                src_ref=source,
                dst_ref=slots.at[member],
                send_sem=sent_sems,
                recv_sem=got_sems,
                device_id=place_of(d),
                device_id_type=MESH,
            ).start()
            return c

        lax.fori_loop(1, count, go, 0)

    def gathered(count, slots, got_sems):
        others = slots.at[pl.ds(0, count - 1)]
        pltpu.make_async_copy(others, others, got_sems).wait()
        total = slots[0]
        for i in range(1, count):
            total = total + slots[i]
        return total

    def start_sums():
        totals = jnp.sum(parts[...], axis=1, keepdims=True)
        here = lax.broadcasted_iota(jnp.int32, (16, TILE_COLS), 0) == lax.broadcasted_iota(
            jnp.int32, (16, TILE_COLS), 1
        )
        near_mine[...] = jnp.sum(jnp.where(here, totals, 0.0), axis=0, keepdims=True)
        share(near_mine, my_near, near_count, near, near_sums, near_got, near_sent)

    def pass_sums_on():
        far_mine[...] = gathered(near_count, near_sums, near_got)
        share(far_mine, my_far, far_count, far, far_sums, far_got, far_sent)

    def sums_sent():
        for count, slots, sent in ((near_count, near_sums, near_sent), (far_count, far_sums, far_sent)):
            others = slots.at[pl.ds(0, count - 1)]
            pltpu.make_async_copy(others, others, sent).wait()

    zeros[...] = jnp.zeros_like(zeros)
    parts[...] = jnp.zeros_like(parts)
    lax.fori_loop(0, SLOTS, fill_edges, 0)
    for load in loads[:3]:
        load.wait()
    place(0, observed[...].astype(F32))
    place(1, (2 * probe[...] - 1).astype(F32))
    for m in range(MODES):
        place(2 * WEIGHT_STAGE + m, weights[m])
    pl.semaphore_wait(barrier, partners)
    for slot in (0, 1, 2 * WEIGHT_STAGE, 2 * WEIGHT_STAGE + 1):
        send(slot)
    for load in loads[3:]:
        load.wait()
    for m in range(MODES):
        planes[m] = taps[:, m, :].astype(F32)
    energy = jnp.sum(jnp.sum(planes[0] * planes[0] + planes[1] * planes[1], axis=0, keepdims=True), axis=1, keepdims=True)
    trial = 1.0 / (DAMPING + 0.85 * energy)
    lax.fori_loop(0, MODES, build_responses, 0)

    def right_side(n, c):
        arrived(n)
        r = adjoint(n)
        first[n] = r
        place(2 + n, r)
        send(2 + n)
        return c

    lax.fori_loop(0, 2, right_side, 0)

    def spread_weights(m, c):
        slot = 2 * WEIGHT_STAGE + m
        arrived(slot)
        for k, b in enumerate(patch(slot, weights[m])):
            patch_weights[m, 64 * k : 64 * k + 64] = b
        return c

    lax.fori_loop(0, MODES, spread_weights, 0)

    def blur_first(n, c):
        arrived(2 + n)
        r = first[n]
        place(4 + n, forward(patch(2 + n, r)))
        send(4 + n)
        u = own[4 + n].astype(F32)
        note(n, 0, r * r)
        note(n, 3, u * u)
        return c

    lax.fori_loop(0, 2, blur_first, 0)

    def back_first(n, c):
        arrived(4 + n)
        r = first[n]
        w = adjoint(4 + n) + DAMPING * r
        v = r - trial * w
        place(6 + n, v)
        send(6 + n)
        image[n] = w
        second[n] = v
        note(n, 1, r * v)
        note(n, 2, v * v)
        return c

    lax.fori_loop(0, 2, back_first, 0)

    def blur_second(n, c):
        arrived(6 + n)
        place(8 + n, forward(patch(6 + n, second[n])))
        u, before = own[8 + n].astype(F32), own[4 + n].astype(F32)
        note(n, 4, u * before)
        note(n, 5, u * u)
        pl.when(n == 1)(start_sums)
        send(8 + n)
        return c

    lax.fori_loop(0, 2, blur_second, 0)
    pass_sums_on()

    def back_second(n, c):
        arrived(8 + n)
        residual_out[n] = adjoint(8 + n) + DAMPING * second[n]
        return c

    lax.fori_loop(0, 2, back_second, 0)
    total = gathered(far_count, far_sums, far_got)
    for n in range(2):
        rr, rv, vv, uu, ut, tt = (total[:, i : i + 1] for i in range(6 * n, 6 * n + 6))
        curve0 = uu + DAMPING * rr
        step0 = rr / curve0
        turn = step0 / trial
        keep = 1.0 - turn
        norm1 = keep * keep * rr + 2.0 * keep * turn * rv + turn * turn * vv
        along = keep + norm1 / rr
        curve1 = along * along * curve0 + (
            2.0 * along * turn * (ut + DAMPING * rv) + turn * turn * (tt + DAMPING * vv)
        )
        step1 = norm1 / curve1
        r, v = first[n], second[n]
        solution_out[n] = (step0 + step1 * along) * r + (step1 * turn) * v
        residual_out[n] = (keep * r + turn * v) - step1 * (along * image[n] + turn * residual_out[n])

    all_sent()
    sums_sent()


def solution(mesh):
    row_count, col_count = mesh.shape["row"], mesh.shape["col"]
    constants = tables()

    def shards(observed, probe_signs, weights, kernels):
        pair = (2, TILE_ROWS, TILE_COLS)
        vmem = pl.BlockSpec(memory_space=pltpu.VMEM)
        operands = [observed, probe_signs, weights, jnp.transpose(kernels, (1, 0, 2)), *[jnp.asarray(c) for c in constants]]
        return pl.pallas_call(
            functools.partial(kernel, row_count, col_count),
            out_shape=(jax.ShapeDtypeStruct(pair, F32), jax.ShapeDtypeStruct(pair, F32)),
            in_specs=[pl.BlockSpec(memory_space=pltpu.HBM)] * len(operands),
            out_specs=(vmem, vmem),
            scratch_shapes=[
                *[pltpu.VMEM(x.shape, x.dtype) for x in operands],
                pltpu.VMEM((SLOTS, 320, TILE_COLS), BF16),
                pltpu.VMEM((SLOTS, TILE_ROWS, TILE_COLS), BF16),
                pltpu.VMEM((SLOTS, TILE_ROWS, TILE_COLS), BF16),
                pltpu.VMEM((TILE_ROWS, TILE_COLS), BF16),
                pltpu.VMEM((MODES, TAPS, TAPS), F32),
                pltpu.VMEM((MODES, 3 * TILE_ROWS, 2 * TILE_COLS), F32),
                pltpu.VMEM((2, MODES, 4, FREQS, FREQS), F32),
                pltpu.VMEM(pair, F32),
                pltpu.VMEM(pair, F32),
                pltpu.VMEM(pair, F32),
                pltpu.VMEM((16, TILE_COLS), F32),
                pltpu.VMEM((1, TILE_COLS), F32),
                pltpu.VMEM((1, TILE_COLS), F32),
                pltpu.VMEM((8, 1, TILE_COLS), F32),
                pltpu.VMEM((row_count * col_count // 8, 1, TILE_COLS), F32),
                pltpu.SemaphoreType.DMA((len(operands),)),
                pltpu.SemaphoreType.DMA((SLOTS,)),
                pltpu.SemaphoreType.DMA((8,)),
                *[pltpu.SemaphoreType.DMA] * 4,
            ],
            compiler_params=pltpu.CompilerParams(
                collective_id=0, has_side_effects=True, vmem_limit_bytes=32 * 2**20
            ),
            name="deconvolve",
        )(*[pltpu.with_memory_space_constraint(x, pltpu.HBM) for x in operands])

    return jax.shard_map(
        shards,
        mesh=mesh,
        in_specs=(P("row", "col"), P("row", "col"), P(None, "row", "col"), P()),
        out_specs=(P(None, "row", "col"), P(None, "row", "col")),
        check_vma=False,
    )
```

```python
import functools

import jax
import jax.numpy as jnp
import ml_dtypes
import numpy as np
from jax import lax
from jax.experimental import pallas as pl
from jax.experimental.pallas import tpu as pltpu
from jax.sharding import PartitionSpec as P

RADIUS = 64
MODES = 2
DAMPING = 1.0
TILE_ROWS = 64
TILE_COLS = 128
FREQS = 128
TAPS = 2 * RADIUS + 1
BF16 = jnp.bfloat16
F32 = jnp.float32
MESH = pl.DeviceIdType.MESH

WEIGHT_STAGE = 5
SLOTS = 12


def split(table):
    high = table.astype(ml_dtypes.bfloat16)
    low = (table - high.astype(np.float64)).astype(ml_dtypes.bfloat16)
    return np.stack([high, low])


def tables():
    theta = 2 * np.pi * (np.arange(FREQS) + 0.5) / 256
    phi = 2 * np.pi * np.arange(FREQS) / 128
    column = np.concatenate([64 + np.arange(128), 192 + np.arange(64), np.arange(64)])
    arg = np.outer(column, theta)
    into_cols = np.concatenate([np.cos(arg), -np.sin(arg)], 1)
    pieces = []
    for block in range(2):
        arg = np.outer(phi, 64 * block + np.arange(64))
        pieces.append(np.block([[np.cos(arg), np.sin(arg)], [-np.sin(arg), np.cos(arg)]]))
    into_rows = np.concatenate(pieces, 1)
    arg = np.outer(np.arange(64), phi)
    from_rows = np.block([[np.cos(arg), -np.sin(arg)], [np.sin(arg), np.cos(arg)]]) / 128
    arg = np.outer(theta, np.arange(128))
    from_cols = np.concatenate([np.cos(arg), -np.sin(arg)], 0) / 128
    arg = np.outer(np.arange(128), theta)
    tap_cols = np.concatenate([np.cos(arg), np.sin(arg)], 1)
    arg = np.outer(phi, np.arange(64))
    tap_rows = np.block([[np.cos(arg), -np.sin(arg)], [np.sin(arg), np.cos(arg)]])
    one_part = [t.astype(ml_dtypes.bfloat16) for t in (into_cols, into_rows, from_rows, from_cols)]
    return one_part + [split(t) for t in (tap_cols, tap_rows)]


def dot(a, b):
    return jnp.dot(a, b, preferred_element_type=F32)


def halves(x):
    high = x.astype(BF16)
    return high, (x - high.astype(F32)).astype(BF16)


def dot_parts_right(table, x):
    high, low = halves(x)
    return dot(table, high) + dot(table, low)


def dot_parts_left(x, table):
    high, low = halves(x)
    both = dot(jnp.concatenate([high, low], 0), table)
    return both[: x.shape[0]] + both[x.shape[0] :]


def kernel(
    row_count,
    col_count,
    observed_hbm,
    probe_hbm,
    weights_hbm,
    taps_hbm,
    into_cols_hbm,
    into_rows_hbm,
    from_rows_hbm,
    from_cols_hbm,
    tap_cols_hbm,
    tap_rows_hbm,
    solution_out,
    residual_out,
    observed,
    probe,
    weights,
    taps,
    into_cols,
    into_rows,
    from_rows,
    from_cols,
    tap_cols,
    tap_rows,
    got,
    own,
    packed,
    zeros,
    planes,
    patch_weights,
    responses,
    first,
    image,
    second,
    parts,
    mine,
    all_sums,
    load_sem,
    got_sem,
    sent_sem,
    sums_in,
    sums_out,
    told_4,
    told_8,
):
    my_row = lax.axis_index("row")
    my_col = lax.axis_index("col")
    up_ok, down_ok = my_row > 0, my_row < row_count - 1
    left_ok, right_ok = my_col > 0, my_col < col_count - 1

    loads = [
        pltpu.make_async_copy(src, dst, load_sem.at[i])
        for i, (src, dst) in enumerate(
            (
                (observed_hbm, observed),
                (probe_hbm, probe),
                (weights_hbm, weights),
                (taps_hbm, taps),
                (tap_cols_hbm, tap_cols),
                (tap_rows_hbm, tap_rows),
                (into_cols_hbm, into_cols),
                (into_rows_hbm, into_rows),
                (from_rows_hbm, from_rows),
                (from_cols_hbm, from_cols),
            )
        )
    ]
    barrier = pltpu.get_barrier_semaphore()

    def greet(row, col):
        pl.semaphore_signal(barrier, inc=1, device_id=(row, col), device_id_type=MESH)

    row_there, col_there = {-1: up_ok, 1: down_ok}, {-1: left_ok, 1: right_ok}
    neighbours = [(dr, dc, row_there[dr] & col_there[dc]) for dr in (-1, 1) for dc in (-1, 1)]
    neighbours += [(dr, 0, row_there[dr]) for dr in (-1, 1)]
    neighbours += [(0, dc, col_there[dc]) for dc in (-1, 1)]
    for dr, dc, there in neighbours:
        pl.when(there)(functools.partial(greet, my_row + dr, my_col + dc))
    for load in loads[:2]:
        load.start()
    for load in loads[2:]:
        load.start()
    rows_here = 1 + up_ok.astype(jnp.int32) + down_ok.astype(jnp.int32)
    cols_here = 1 + left_ok.astype(jnp.int32) + right_ok.astype(jnp.int32)
    partners = rows_here * cols_here - 1

    lane = lax.broadcasted_iota(jnp.int32, (32, TILE_COLS), 1)
    low_lanes = lane < 64

    def place(slot, tile):
        own[slot] = tile.astype(BF16)
        turned = pltpu.roll(tile, 64, 1)
        packed[slot, 0:32] = jnp.where(low_lanes, tile[0:32], turned[32:64]).astype(BF16)
        packed[slot, 32:64] = jnp.where(low_lanes, turned[0:32], tile[32:64]).astype(BF16)

    def landing(slot, dr, dc):
        if dc == 0:
            return got.at[slot, pl.ds(0 if dr < 0 else 64, 64)]
        return got.at[slot, pl.ds(128 + 64 * (1 + dr) + (32 if dc < 0 else 0), 32)]

    def send(slot):
        for i, (dr, dc, there) in enumerate(neighbours):
            if dc == 0:
                piece = own.at[slot]
            else:
                piece = packed.at[slot, pl.ds(0 if dc < 0 else 32, 32)]
            out = pltpu.make_async_remote_copy(
                src_ref=piece,
                dst_ref=landing(slot, -dr, -dc),
                send_sem=sent_sem.at[i],
                recv_sem=got_sem.at[slot],
                device_id=(my_row + dr, my_col + dc),
                device_id_type=MESH,
            )
            pl.when(there)(out.start)

    def fill_edges(slot, c):
        for dr, dc, there in neighbours:
            edge = landing(slot, dr, dc)
            fill = pltpu.make_async_copy(zeros.at[pl.ds(0, edge.shape[0])], edge, got_sem.at[slot])
            pl.when(jnp.logical_not(there))(fill.start)
        return c

    def arrived(slot):
        pltpu.make_async_copy(got.at[slot], got.at[slot], got_sem.at[slot]).wait()

    def all_sent():
        for i, (dr, dc, there) in enumerate(neighbours):
            every = got.at[:, pl.ds(0, 64 if dc == 0 else 32)]
            pl.when(there)(pltpu.make_async_copy(every, every, sent_sem.at[i]).wait)

    def halo(slot, k):
        right = got[slot, 128 + 64 * k : 160 + 64 * k].astype(F32)
        left = got[slot, 160 + 64 * k : 192 + 64 * k].astype(F32)
        top = jnp.where(low_lanes, right, pltpu.roll(left, 64, 1))
        bottom = jnp.where(low_lanes, pltpu.roll(right, 64, 1), left)
        return jnp.concatenate([top, bottom], 0)

    def patch(slot, middle):
        above, below = got[slot, 0:64].astype(F32), got[slot, 64:128].astype(F32)
        return [
            jnp.concatenate([tile, halo(slot, k)], 1) for k, tile in enumerate((above, middle, below))
        ]

    def columns_of(x):
        return dot(x, into_cols[...])

    def stacked(y, k):
        parts = []
        for b in (k, k + 1):
            rows = y[64 * b : 64 * b + 64]
            parts += [rows[:, :128], rows[:, 128:]]
        return jnp.concatenate(parts, 0)

    def adjoint(slot):
        x = jnp.concatenate([b.astype(BF16) for b in patch(slot, own[slot].astype(F32))], 0)
        y = columns_of(x)
        z = dot_parts_right(into_rows[...], jnp.concatenate([stacked(y, 0), stacked(y, 1)], 1))
        are, aim = z[:128, :128], z[128:, :128]
        bre, bim = z[:128, 128:], z[128:, 128:]
        reals, imags = [], []
        for m in range(MODES):
            h = [responses[1, m, i] for i in range(4)]
            reals.append(h[0] * are - h[1] * aim + (h[2] * bre - h[3] * bim))
            imags.append(h[0] * aim + h[1] * are + (h[2] * bim + h[3] * bre))
        spectrum = jnp.concatenate([jnp.concatenate(reals, 1), jnp.concatenate(imags, 1)], 0)
        v = dot_parts_right(from_rows[...], spectrum)
        rows = [
            jnp.concatenate([v[:64, 128 * m : 128 * m + 128], v[64:, 128 * m : 128 * m + 128]], 1)
            for m in range(MODES)
        ]
        out = dot_parts_left(jnp.concatenate(rows, 0), from_cols[...])
        return weights[0] * out[:64] + weights[1] * out[64:]

    def forward(values):
        x = jnp.concatenate(
            [
                (patch_weights[m, 64 * k : 64 * k + 64] * values[k]).astype(BF16)
                for m in range(MODES)
                for k in range(3)
            ],
            0,
        )
        y = columns_of(x)
        z = [
            dot_parts_right(
                into_rows[...], jnp.concatenate([stacked(y[:192], k), stacked(y[192:], k)], 1)
            )
            for k in range(2)
        ]
        real = jnp.zeros((FREQS, FREQS), F32)
        imag = real
        for m in range(MODES):
            h = [responses[0, m, i] for i in range(4)]
            lanes = slice(128 * m, 128 * m + 128)
            are, aim = z[0][:128, lanes], z[0][128:, lanes]
            bre, bim = z[1][:128, lanes], z[1][128:, lanes]
            real = real + (h[0] * are - h[1] * aim + (h[2] * bre - h[3] * bim))
            imag = imag + (h[0] * aim + h[1] * are + (h[2] * bim + h[3] * bre))
        v = dot_parts_right(from_rows[...], jnp.concatenate([real, imag], 0))
        return dot_parts_left(jnp.concatenate([v[:64], v[64:]], 1), from_cols[...])

    def build_responses(m, c):
        narrow = planes[m, :, 0:128].astype(BF16)
        even_lane = lax.broadcasted_iota(jnp.int32, (1, FREQS), 1) % 2 == 0
        sign_f = jnp.where(even_lane, 1.0, -1.0)
        even_row = lax.broadcasted_iota(jnp.int32, (FREQS, 1), 0) % 2 == 0
        sign_q = jnp.where(even_row, 1.0, -1.0)
        cols = dot(narrow, tap_cols[0]) + dot(narrow, tap_cols[1])
        re = cols[:, :128]
        im = cols[:, 128:] + planes[m, :, 128:129] * sign_f
        pairs = jnp.concatenate(
            [
                jnp.concatenate([re[0:64], re[64:128]], 1),
                jnp.concatenate([im[0:64], im[64:128]], 1),
            ],
            0,
        )
        high, low = halves(pairs)
        g = dot(tap_rows[0], high) + (dot(tap_rows[0], low) + dot(tap_rows[1], high))
        g0re, g0im, g1re, g1im = g[:128, :128], g[128:, :128], g[:128, 128:], g[128:, 128:]
        mid_re, mid_im, last_re, last_im = re[64:65], im[64:65], re[128:129], im[128:129]
        responses[0, m, 0] = g0re
        responses[0, m, 1] = g0im
        responses[0, m, 2] = g1re + sign_q * last_re
        responses[0, m, 3] = g1im + sign_q * last_im
        responses[1, m, 0] = sign_f * (sign_q * (g1im - mid_im) + last_im)
        responses[1, m, 1] = sign_f * (sign_q * (g1re - mid_re) + last_re)
        responses[1, m, 2] = sign_f * (sign_q * g0im + mid_im)
        responses[1, m, 3] = sign_f * (sign_q * g0re + mid_re)
        return c

    def note(n, i, part):
        parts[pl.ds(6 * n + i, 1)] = jnp.sum(part, axis=0, keepdims=True)

    def tell(semaphore, steps):
        for dr, dc in steps:
            row, col = my_row + dr, my_col + dc
            there = (row >= 0) & (row < row_count) & (col >= 0) & (col < col_count)

            @pl.when(there)
            def _(row=row, col=col):
                pl.semaphore_signal(semaphore, inc=1, device_id=(row, col), device_id_type=MESH)

    def both_ways(down, across):
        rows = 1 + (my_row >= down).astype(jnp.int32) + (my_row + down < row_count).astype(jnp.int32)
        cols = 1 + (my_col >= across).astype(jnp.int32) + (my_col + across < col_count).astype(jnp.int32)
        return rows * cols - 1

    def tell_4():
        tell(told_4, [(4 * i, 4 * j) for i in (-1, 0, 1) for j in (-1, 0, 1) if i or j])

    def tell_8():
        tell(told_8, [(0, -8), (0, 8)])

    z_count, y_count = row_count // 2, col_count // 4
    my_z, my_y = my_row // 2, lax.rem(my_col // 2, y_count)
    my_x, my_core = 2 * (my_col // (2 * y_count)) + lax.rem(my_row, 2), lax.rem(my_col, 2)
    me = my_row * col_count + my_col

    def start_sums():
        totals = jnp.sum(parts[...], axis=1, keepdims=True)
        here = lax.broadcasted_iota(jnp.int32, (16, TILE_COLS), 0) == lax.broadcasted_iota(
            jnp.int32, (16, TILE_COLS), 1
        )
        mine[...] = jnp.sum(jnp.where(here, totals, 0.0), axis=0, keepdims=True)
        all_sums[me] = mine[...]
        places = []
        for dx in (2, 1, 3, 0):
            x = lax.rem(my_x + dx, 4)
            for dcore in (1, 0):
                core = lax.rem(my_core + dcore, 2)
                places.append((lax.rem(x, 2), (x // 2) * 2 * y_count + core, dx == 0 and dcore == 0))

        def go(i, c):
            dz = lax.rem(z_count // 2 + (i // y_count) * (z_count - 1), z_count)
            dy = lax.rem(y_count // 2 + lax.rem(i, y_count) * (y_count - 1), y_count)
            row = 2 * lax.rem(my_z + dz, z_count)
            col = 2 * lax.rem(my_y + dy, y_count)
            for x_row, x_col, same in places:
                out = pltpu.make_async_remote_copy(
                    src_ref=mine,
                    dst_ref=all_sums.at[me],
                    send_sem=sums_out,
                    recv_sem=sums_in,
                    device_id=(row + x_row, col + x_col),
                    device_id_type=MESH,
                )
                if same:
                    pl.when(dz + dy > 0)(out.start)
                else:
                    out.start()
            return c

        lax.fori_loop(0, z_count * y_count, go, 0)

    def summed():
        others = all_sums.at[pl.ds(0, row_count * col_count - 1)]
        pltpu.make_async_copy(others, others, sums_in).wait()
        return jnp.sum(all_sums[...], axis=0)

    def sums_sent():
        others = all_sums.at[pl.ds(0, row_count * col_count - 1)]
        pltpu.make_async_copy(others, others, sums_out).wait()

    zeros[...] = jnp.zeros_like(zeros)
    parts[...] = jnp.zeros_like(parts)
    lax.fori_loop(0, SLOTS, fill_edges, 0)
    for load in loads[:2]:
        load.wait()
    place(0, observed[...].astype(F32))
    place(1, (2 * probe[...] - 1).astype(F32))
    pl.semaphore_wait(barrier, partners)
    for slot in (0, 1):
        send(slot)
    loads[2].wait()
    for m in range(MODES):
        place(2 * WEIGHT_STAGE + m, weights[m])
        send(2 * WEIGHT_STAGE + m)
    for load in loads[3:]:
        load.wait()
    for m in range(MODES):
        planes[m] = taps[:, m, :].astype(F32)
    energy = jnp.sum(jnp.sum(planes[0] * planes[0] + planes[1] * planes[1], axis=0, keepdims=True), axis=1, keepdims=True)
    trial = 1.0 / (DAMPING + 0.85 * energy)
    lax.fori_loop(0, MODES, build_responses, 0)

    def right_side(n, c):
        arrived(n)
        r = adjoint(n)
        first[n] = r
        place(2 + n, r)
        send(2 + n)
        return c

    lax.fori_loop(0, 2, right_side, 0)

    def spread_weights(m, c):
        slot = 2 * WEIGHT_STAGE + m
        arrived(slot)
        for k, b in enumerate(patch(slot, weights[m])):
            patch_weights[m, 64 * k : 64 * k + 64] = b
        return c

    lax.fori_loop(0, MODES, spread_weights, 0)

    def blur_first(n, c):
        arrived(2 + n)
        r = first[n]
        place(4 + n, forward(patch(2 + n, r)))
        send(4 + n)
        u = own[4 + n].astype(F32)
        note(n, 0, r * r)
        note(n, 3, u * u)
        return c

    lax.fori_loop(0, 2, blur_first, 0)

    def back_first(n, c):
        arrived(4 + n)

        @pl.when(n == 0)
        def _():
            tell_4()

        r = first[n]
        w = adjoint(4 + n) + DAMPING * r
        v = r - trial * w
        place(6 + n, v)
        send(6 + n)
        image[n] = w
        second[n] = v
        note(n, 1, r * v)
        note(n, 2, v * v)
        return c

    lax.fori_loop(0, 2, back_first, 0)
    pl.semaphore_wait(told_4, both_ways(4, 4))
    tell_8()

    def blur_second(n, c):
        arrived(6 + n)
        place(8 + n, forward(patch(6 + n, second[n])))
        u, before = own[8 + n].astype(F32), own[4 + n].astype(F32)
        note(n, 4, u * before)
        note(n, 5, u * u)
        send(8 + n)
        return c

    lax.fori_loop(0, 2, blur_second, 0)
    pl.semaphore_wait(told_8, both_ways(row_count, 8))
    start_sums()

    def back_second(n, c):
        arrived(8 + n)
        residual_out[n] = adjoint(8 + n) + DAMPING * second[n]
        return c

    lax.fori_loop(0, 2, back_second, 0)
    total = summed()
    for n in range(2):
        rr, rv, vv, uu, ut, tt = (total[:, i : i + 1] for i in range(6 * n, 6 * n + 6))
        curve0 = uu + DAMPING * rr
        step0 = rr / curve0
        turn = step0 / trial
        keep = 1.0 - turn
        norm1 = keep * keep * rr + 2.0 * keep * turn * rv + turn * turn * vv
        along = keep + norm1 / rr
        curve1 = along * along * curve0 + (
            2.0 * along * turn * (ut + DAMPING * rv) + turn * turn * (tt + DAMPING * vv)
        )
        step1 = norm1 / curve1
        r, v = first[n], second[n]
        solution_out[n] = (step0 + step1 * along) * r + (step1 * turn) * v
        residual_out[n] = (keep * r + turn * v) - step1 * (along * image[n] + turn * residual_out[n])

    all_sent()
    sums_sent()


def solution(mesh):
    row_count, col_count = mesh.shape["row"], mesh.shape["col"]
    constants = tables()

    def shards(observed, probe_signs, weights, kernels):
        pair = (2, TILE_ROWS, TILE_COLS)
        vmem = pl.BlockSpec(memory_space=pltpu.VMEM)
        operands = [observed, probe_signs, weights, jnp.transpose(kernels, (1, 0, 2)), *[jnp.asarray(c) for c in constants]]
        return pl.pallas_call(
            functools.partial(kernel, row_count, col_count),
            out_shape=(jax.ShapeDtypeStruct(pair, F32), jax.ShapeDtypeStruct(pair, F32)),
            in_specs=[pl.BlockSpec(memory_space=pltpu.HBM)] * len(operands),
            out_specs=(vmem, vmem),
            scratch_shapes=[
                *[pltpu.VMEM(x.shape, x.dtype) for x in operands],
                pltpu.VMEM((SLOTS, 320, TILE_COLS), BF16),
                pltpu.VMEM((SLOTS, TILE_ROWS, TILE_COLS), BF16),
                pltpu.VMEM((SLOTS, TILE_ROWS, TILE_COLS), BF16),
                pltpu.VMEM((TILE_ROWS, TILE_COLS), BF16),
                pltpu.VMEM((MODES, TAPS, TAPS), F32),
                pltpu.VMEM((MODES, 3 * TILE_ROWS, 2 * TILE_COLS), F32),
                pltpu.VMEM((2, MODES, 4, FREQS, FREQS), F32),
                pltpu.VMEM(pair, F32),
                pltpu.VMEM(pair, F32),
                pltpu.VMEM(pair, F32),
                pltpu.VMEM((16, TILE_COLS), F32),
                pltpu.VMEM((1, TILE_COLS), F32),
                pltpu.VMEM((row_count * col_count, 1, TILE_COLS), F32),
                pltpu.SemaphoreType.DMA((len(operands),)),
                pltpu.SemaphoreType.DMA((SLOTS,)),
                pltpu.SemaphoreType.DMA((8,)),
                *[pltpu.SemaphoreType.DMA] * 2,
                *[pltpu.SemaphoreType.REGULAR] * 2,
            ],
            compiler_params=pltpu.CompilerParams(
                collective_id=0, has_side_effects=True, vmem_limit_bytes=32 * 2**20
            ),
            name="deconvolve",
        )(*[pltpu.with_memory_space_constraint(x, pltpu.HBM) for x in operands])

    return jax.shard_map(
        shards,
        mesh=mesh,
        in_specs=(P("row", "col"), P("row", "col"), P(None, "row", "col"), P()),
        out_specs=(P(None, "row", "col"), P(None, "row", "col")),
        check_vma=False,
    )
```

```python
import functools

import jax
import jax.numpy as jnp
import ml_dtypes
import numpy as np
from jax import lax
from jax.experimental import pallas as pl
from jax.experimental.pallas import tpu as pltpu
from jax.sharding import PartitionSpec as P

RADIUS = 64
MODES = 2
DAMPING = 1.0
TILE_ROWS = 64
TILE_COLS = 128
FREQS = 128
TAPS = 2 * RADIUS + 1
BF16 = jnp.bfloat16
F32 = jnp.float32
MESH = pl.DeviceIdType.MESH

WEIGHT_STAGE = 5
SLOTS = 12


def split(table):
    high = table.astype(ml_dtypes.bfloat16)
    low = (table - high.astype(np.float64)).astype(ml_dtypes.bfloat16)
    return np.stack([high, low])


def tables():
    theta = 2 * np.pi * (np.arange(FREQS) + 0.5) / 256
    phi = 2 * np.pi * np.arange(FREQS) / 128
    column = np.concatenate([64 + np.arange(128), 192 + np.arange(64), np.arange(64)])
    arg = np.outer(column, theta)
    into_cols = np.concatenate([np.cos(arg), -np.sin(arg)], 1)
    pieces = []
    for block in range(2):
        arg = np.outer(phi, 64 * block + np.arange(64))
        pieces.append(np.block([[np.cos(arg), np.sin(arg)], [-np.sin(arg), np.cos(arg)]]))
    into_rows = np.concatenate(pieces, 1)
    arg = np.outer(np.arange(64), phi)
    from_rows = np.block([[np.cos(arg), -np.sin(arg)], [np.sin(arg), np.cos(arg)]]) / 128
    arg = np.outer(theta, np.arange(128))
    from_cols = np.concatenate([np.cos(arg), -np.sin(arg)], 0) / 128
    arg = np.outer(np.arange(128), theta)
    tap_cols = np.concatenate([np.cos(arg), np.sin(arg)], 1)
    arg = np.outer(phi, np.arange(64))
    tap_rows = np.block([[np.cos(arg), -np.sin(arg)], [np.sin(arg), np.cos(arg)]])
    one_part = [t.astype(ml_dtypes.bfloat16) for t in (into_cols, into_rows)]
    return one_part + [split(t) for t in (from_rows, from_cols, tap_cols, tap_rows)]


def dot(a, b):
    return jnp.dot(a, b, preferred_element_type=F32)


def halves(x):
    high = x.astype(BF16)
    return high, (x - high.astype(F32)).astype(BF16)


def dot_parts_right(table, x):
    high, low = halves(x)
    return dot(table, high) + dot(table, low)


def dot_both_right(table, x):
    high, low = halves(x)
    rows = table.shape[1]
    both = dot(table[...].reshape(2 * rows, table.shape[2]), high)
    return both[:rows] + (both[rows:] + dot(table[0], low))


def dot_both_left(x, table):
    high, low = halves(x)
    rows = x.shape[0]
    both = dot(jnp.concatenate([high, low], 0), table[0])
    return both[:rows] + (both[rows:] + dot(high, table[1]))


def kernel(
    row_count,
    col_count,
    observed_hbm,
    probe_hbm,
    weights_hbm,
    taps_hbm,
    into_cols_hbm,
    into_rows_hbm,
    from_rows_hbm,
    from_cols_hbm,
    tap_cols_hbm,
    tap_rows_hbm,
    out,
    observed,
    probe,
    weights,
    taps,
    into_cols,
    into_rows,
    from_rows,
    from_cols,
    tap_cols,
    tap_rows,
    got,
    own,
    packed,
    zeros,
    planes,
    patch_weights,
    responses,
    first,
    image,
    second,
    parts,
    mine,
    all_sums,
    load_sem,
    got_sem,
    sent_sem,
    core_in,
    core_out,
    sums_in,
    sums_out,
    told_4,
    told_8,
):
    my_row = lax.axis_index("row")
    my_col = lax.axis_index("col")
    up_ok, down_ok = my_row > 0, my_row < row_count - 1
    left_ok, right_ok = my_col > 0, my_col < col_count - 1

    loads = [
        pltpu.make_async_copy(src, dst, load_sem.at[i])
        for i, (src, dst) in enumerate(
            (
                (observed_hbm, observed),
                (probe_hbm, probe),
                (weights_hbm, weights),
                (taps_hbm, taps),
                (tap_cols_hbm, tap_cols),
                (tap_rows_hbm, tap_rows),
                (into_cols_hbm, into_cols),
                (into_rows_hbm, into_rows),
                (from_rows_hbm, from_rows),
                (from_cols_hbm, from_cols),
            )
        )
    ]
    barrier = pltpu.get_barrier_semaphore()

    def greet(row, col):
        pl.semaphore_signal(barrier, inc=1, device_id=(row, col), device_id_type=MESH)

    row_there, col_there = {-1: up_ok, 1: down_ok}, {-1: left_ok, 1: right_ok}
    neighbours = [(dr, dc, row_there[dr] & col_there[dc]) for dr in (-1, 1) for dc in (-1, 1)]
    neighbours += [(dr, 0, row_there[dr]) for dr in (-1, 1)]
    neighbours += [(0, dc, col_there[dc]) for dc in (-1, 1)]
    for dr, dc, there in neighbours:
        pl.when(there)(functools.partial(greet, my_row + dr, my_col + dc))
    for load in loads[:2]:
        load.start()
    for load in loads[2:]:
        load.start()
    rows_here = 1 + up_ok.astype(jnp.int32) + down_ok.astype(jnp.int32)
    cols_here = 1 + left_ok.astype(jnp.int32) + right_ok.astype(jnp.int32)
    partners = rows_here * cols_here - 1

    lane = lax.broadcasted_iota(jnp.int32, (32, TILE_COLS), 1)
    low_lanes = lane < 64

    def place(slot, tile):
        own[slot] = tile.astype(BF16)
        turned = pltpu.roll(tile, 64, 1)
        packed[slot, 0:32] = jnp.where(low_lanes, tile[0:32], turned[32:64]).astype(BF16)
        packed[slot, 32:64] = jnp.where(low_lanes, turned[0:32], tile[32:64]).astype(BF16)

    def landing(slot, dr, dc):
        if dc == 0:
            return got.at[slot, pl.ds(0 if dr < 0 else 64, 64)]
        return got.at[slot, pl.ds(128 + 64 * (1 + dr) + (32 if dc < 0 else 0), 32)]

    def send(slot):
        for i, (dr, dc, there) in enumerate(neighbours):
            if dc == 0:
                piece = own.at[slot]
            else:
                piece = packed.at[slot, pl.ds(0 if dc < 0 else 32, 32)]
            out = pltpu.make_async_remote_copy(
                src_ref=piece,
                dst_ref=landing(slot, -dr, -dc),
                send_sem=sent_sem.at[i],
                recv_sem=got_sem.at[slot],
                device_id=(my_row + dr, my_col + dc),
                device_id_type=MESH,
            )
            pl.when(there)(out.start)

    def fill_edges(slot, c):
        for dr, dc, there in neighbours:
            edge = landing(slot, dr, dc)
            fill = pltpu.make_async_copy(zeros.at[pl.ds(0, edge.shape[0])], edge, got_sem.at[slot])
            pl.when(jnp.logical_not(there))(fill.start)
        return c

    def arrived(slot):
        pltpu.make_async_copy(got.at[slot], got.at[slot], got_sem.at[slot]).wait()

    def all_sent():
        for i, (dr, dc, there) in enumerate(neighbours):
            every = got.at[:, pl.ds(0, 64 if dc == 0 else 32)]
            pl.when(there)(pltpu.make_async_copy(every, every, sent_sem.at[i]).wait)

    def halo(slot, k):
        right = got[slot, 128 + 64 * k : 160 + 64 * k].astype(F32)
        left = got[slot, 160 + 64 * k : 192 + 64 * k].astype(F32)
        top = jnp.where(low_lanes, right, pltpu.roll(left, 64, 1))
        bottom = jnp.where(low_lanes, pltpu.roll(right, 64, 1), left)
        return jnp.concatenate([top, bottom], 0)

    def patch(slot, middle):
        above, below = got[slot, 0:64].astype(F32), got[slot, 64:128].astype(F32)
        return [
            jnp.concatenate([tile, halo(slot, k)], 1) for k, tile in enumerate((above, middle, below))
        ]

    def columns_of(x):
        return dot(x, into_cols[...])

    def stacked(y, k):
        parts = []
        for b in (k, k + 1):
            rows = y[64 * b : 64 * b + 64]
            parts += [rows[:, :128], rows[:, 128:]]
        return jnp.concatenate(parts, 0)

    def adjoint(slot):
        tiles = (got[slot, 0:64], own[slot], got[slot, 64:128])
        x = jnp.concatenate(
            [jnp.concatenate([tile, halo(slot, k).astype(BF16)], 1) for k, tile in enumerate(tiles)], 0
        )
        y = columns_of(x)
        z = dot_parts_right(into_rows[...], jnp.concatenate([stacked(y, 0), stacked(y, 1)], 1))
        are, aim = z[:128, :128], z[128:, :128]
        bre, bim = z[:128, 128:], z[128:, 128:]
        reals, imags = [], []
        for m in range(MODES):
            h = [responses[1, m, i] for i in range(4)]
            reals.append(h[0] * are - h[1] * aim + (h[2] * bre - h[3] * bim))
            imags.append(h[0] * aim + h[1] * are + (h[2] * bim + h[3] * bre))
        spectrum = jnp.concatenate([jnp.concatenate(reals, 1), jnp.concatenate(imags, 1)], 0)
        v = dot_both_right(from_rows, spectrum)
        rows = [
            jnp.concatenate([v[:64, 128 * m : 128 * m + 128], v[64:, 128 * m : 128 * m + 128]], 1)
            for m in range(MODES)
        ]
        out = dot_both_left(jnp.concatenate(rows, 0), from_cols)
        return weights[0] * out[:64] + weights[1] * out[64:]

    def forward(values):
        x = jnp.concatenate(
            [
                (patch_weights[m, 64 * k : 64 * k + 64] * values[k]).astype(BF16)
                for m in range(MODES)
                for k in range(3)
            ],
            0,
        )
        y = columns_of(x)
        z = [
            dot_parts_right(
                into_rows[...], jnp.concatenate([stacked(y[:192], k), stacked(y[192:], k)], 1)
            )
            for k in range(2)
        ]
        real = jnp.zeros((FREQS, FREQS), F32)
        imag = real
        for m in range(MODES):
            h = [responses[0, m, i] for i in range(4)]
            lanes = slice(128 * m, 128 * m + 128)
            are, aim = z[0][:128, lanes], z[0][128:, lanes]
            bre, bim = z[1][:128, lanes], z[1][128:, lanes]
            real = real + (h[0] * are - h[1] * aim + (h[2] * bre - h[3] * bim))
            imag = imag + (h[0] * aim + h[1] * are + (h[2] * bim + h[3] * bre))
        v = dot_both_right(from_rows, jnp.concatenate([real, imag], 0))
        return dot_both_left(jnp.concatenate([v[:64], v[64:]], 1), from_cols)

    def build_responses(m, c):
        narrow = planes[m, :, 0:128].astype(BF16)
        even_lane = lax.broadcasted_iota(jnp.int32, (1, FREQS), 1) % 2 == 0
        sign_f = jnp.where(even_lane, 1.0, -1.0)
        even_row = lax.broadcasted_iota(jnp.int32, (FREQS, 1), 0) % 2 == 0
        sign_q = jnp.where(even_row, 1.0, -1.0)
        cols = dot(narrow, tap_cols[0]) + dot(narrow, tap_cols[1])
        re = cols[:, :128]
        im = cols[:, 128:] + planes[m, :, 128:129] * sign_f
        pairs = jnp.concatenate(
            [
                jnp.concatenate([re[0:64], re[64:128]], 1),
                jnp.concatenate([im[0:64], im[64:128]], 1),
            ],
            0,
        )
        high, low = halves(pairs)
        g = dot(tap_rows[0], high) + (dot(tap_rows[0], low) + dot(tap_rows[1], high))
        g0re, g0im, g1re, g1im = g[:128, :128], g[128:, :128], g[:128, 128:], g[128:, 128:]
        mid_re, mid_im, last_re, last_im = re[64:65], im[64:65], re[128:129], im[128:129]
        responses[0, m, 0] = g0re
        responses[0, m, 1] = g0im
        responses[0, m, 2] = g1re + sign_q * last_re
        responses[0, m, 3] = g1im + sign_q * last_im
        responses[1, m, 0] = sign_f * (sign_q * (g1im - mid_im) + last_im)
        responses[1, m, 1] = sign_f * (sign_q * (g1re - mid_re) + last_re)
        responses[1, m, 2] = sign_f * (sign_q * g0im + mid_im)
        responses[1, m, 3] = sign_f * (sign_q * g0re + mid_re)
        return c

    def note(n, i, part):
        parts[pl.ds(6 * n + i, 1)] = jnp.sum(part, axis=0, keepdims=True)

    def tell(semaphore, steps):
        for dr, dc in steps:
            row, col = my_row + dr, my_col + dc
            there = (row >= 0) & (row < row_count) & (col >= 0) & (col < col_count)

            @pl.when(there)
            def _(row=row, col=col):
                pl.semaphore_signal(semaphore, inc=1, device_id=(row, col), device_id_type=MESH)

    def both_ways(down, across):
        rows = 1 + (my_row >= down).astype(jnp.int32) + (my_row + down < row_count).astype(jnp.int32)
        cols = 1 + (my_col >= across).astype(jnp.int32) + (my_col + across < col_count).astype(jnp.int32)
        return rows * cols - 1

    def tell_4():
        tell(told_4, [(4 * i, 4 * j) for i in (-1, 0, 1) for j in (-1, 0, 1) if i or j])

    def tell_8():
        tell(told_8, [(0, -8), (0, 8)])

    z_count, y_count = row_count // 2, col_count // 4
    my_z, my_y = my_row // 2, lax.rem(my_col // 2, y_count)
    my_x, my_core = 2 * (my_col // (2 * y_count)) + lax.rem(my_row, 2), lax.rem(my_col, 2)
    chip_count = row_count * col_count // 2
    my_chip = my_row * (col_count // 2) + my_col // 2

    def start_sums():
        totals = jnp.sum(parts[...], axis=1, keepdims=True)
        here = lax.broadcasted_iota(jnp.int32, (16, TILE_COLS), 0) == lax.broadcasted_iota(
            jnp.int32, (16, TILE_COLS), 1
        )
        mine[0] = jnp.sum(jnp.where(here, totals, 0.0), axis=0, keepdims=True)
        pltpu.make_async_remote_copy(
            src_ref=mine.at[0],
            dst_ref=mine.at[1],
            send_sem=core_out,
            recv_sem=core_in,
            device_id=(my_row, my_col + 1 - 2 * my_core),
            device_id_type=MESH,
        ).start()

    def pass_sums_on():
        pltpu.make_async_copy(mine.at[1], mine.at[1], core_in).wait()
        mine[2] = mine[0] + mine[1]
        all_sums[my_chip] = mine[2]
        places = []
        for dx in (2, 1, 3, 0):
            x = lax.rem(my_x + dx, 4)
            places.append((lax.rem(x, 2), (x // 2) * 2 * y_count + my_core, dx == 0))

        def go(i, c):
            dz = lax.rem(z_count // 2 + (i // y_count) * (z_count - 1), z_count)
            dy = lax.rem(y_count // 2 + lax.rem(i, y_count) * (y_count - 1), y_count)
            row = 2 * lax.rem(my_z + dz, z_count)
            col = 2 * lax.rem(my_y + dy, y_count)
            for x_row, x_col, same in places:
                out = pltpu.make_async_remote_copy(
                    src_ref=mine.at[2],
                    dst_ref=all_sums.at[my_chip],
                    send_sem=sums_out,
                    recv_sem=sums_in,
                    device_id=(row + x_row, col + x_col),
                    device_id_type=MESH,
                )
                if same:
                    pl.when(dz + dy > 0)(out.start)
                else:
                    out.start()
            return c

        lax.fori_loop(0, z_count * y_count, go, 0)

    def summed():
        others = all_sums.at[pl.ds(0, chip_count - 1)]
        pltpu.make_async_copy(others, others, sums_in).wait()
        lanes = [all_sums[i] for i in range(8)]
        for i in range(8, chip_count):
            lanes[i % 8] = lanes[i % 8] + all_sums[i]
        while len(lanes) > 1:
            lanes = [a + b for a, b in zip(lanes[::2], lanes[1::2])]
        return lanes[0]

    def sums_sent():
        others = all_sums.at[pl.ds(0, chip_count - 1)]
        pltpu.make_async_copy(others, others, sums_out).wait()
        pltpu.make_async_copy(mine.at[0], mine.at[0], core_out).wait()

    zeros[...] = jnp.zeros_like(zeros)
    parts[...] = jnp.zeros_like(parts)
    for load in loads[:2]:
        load.wait()
    place(0, observed[...].astype(F32))
    place(1, (2 * probe[...] - 1).astype(F32))
    pl.semaphore_wait(barrier, partners)
    for slot in (0, 1):
        send(slot)
    loads[2].wait()
    for m in range(MODES):
        place(2 * WEIGHT_STAGE + m, weights[m])
        send(2 * WEIGHT_STAGE + m)
    lax.fori_loop(0, SLOTS, fill_edges, 0)
    for load in loads[3:]:
        load.wait()
    for m in range(MODES):
        planes[m] = taps[:, m, :].astype(F32)
    energy = jnp.sum(jnp.sum(planes[0] * planes[0] + planes[1] * planes[1], axis=0, keepdims=True), axis=1, keepdims=True)
    trial = 1.0 / (DAMPING + 0.85 * energy)
    lax.fori_loop(0, MODES, build_responses, 0)

    def right_side(n, c):
        arrived(n)
        r = adjoint(n)
        first[n] = r
        place(2 + n, r)
        send(2 + n)
        return c

    lax.fori_loop(0, 2, right_side, 0)

    def spread_weights(m, c):
        slot = 2 * WEIGHT_STAGE + m
        arrived(slot)
        for k, b in enumerate(patch(slot, weights[m])):
            patch_weights[m, 64 * k : 64 * k + 64] = b
        return c

    lax.fori_loop(0, MODES, spread_weights, 0)

    def blur_first(n, c):
        arrived(2 + n)
        r = first[n]
        place(4 + n, forward(patch(2 + n, r)))
        send(4 + n)
        u = own[4 + n].astype(F32)
        note(n, 0, r * r)
        note(n, 3, u * u)
        return c

    lax.fori_loop(0, 2, blur_first, 0)

    def back_first(n, c):
        arrived(4 + n)

        @pl.when(n == 0)
        def _():
            tell_4()

        r = first[n]
        w = adjoint(4 + n) + DAMPING * r
        v = r - trial * w
        place(6 + n, v)
        send(6 + n)
        image[n] = w
        second[n] = v
        note(n, 1, r * v)
        note(n, 2, v * v)
        return c

    lax.fori_loop(0, 2, back_first, 0)
    pl.semaphore_wait(told_4, both_ways(4, 4))
    tell_8()

    def blur_second(n, c):
        arrived(6 + n)
        place(8 + n, forward(patch(6 + n, second[n])))
        u, before = own[8 + n].astype(F32), own[4 + n].astype(F32)
        note(n, 4, u * before)
        note(n, 5, u * u)
        pl.when(n == 1)(start_sums)
        send(8 + n)
        return c

    lax.fori_loop(0, 2, blur_second, 0)
    pl.semaphore_wait(told_8, both_ways(row_count, 8))
    pass_sums_on()

    def back_second(n, c):
        arrived(8 + n)
        out[1, n] = adjoint(8 + n) + DAMPING * second[n]
        return c

    lax.fori_loop(0, 2, back_second, 0)
    all_sent()
    sums_sent()
    total = summed()
    for n in range(2):
        rr, rv, vv, uu, ut, tt = (total[:, i : i + 1] for i in range(6 * n, 6 * n + 6))
        curve0 = uu + DAMPING * rr
        step0 = rr / curve0
        turn = step0 / trial
        keep = 1.0 - turn
        norm1 = keep * keep * rr + 2.0 * keep * turn * rv + turn * turn * vv
        along = keep + norm1 / rr
        curve1 = along * along * curve0 + (
            2.0 * along * turn * (ut + DAMPING * rv) + turn * turn * (tt + DAMPING * vv)
        )
        step1 = norm1 / curve1
        r, v = first[n], second[n]
        out[0, n] = (step0 + step1 * along) * r + (step1 * turn) * v
        out[1, n] = (keep * r + turn * v) - step1 * (along * image[n] + turn * out[1, n])


def solution(mesh):
    row_count, col_count = mesh.shape["row"], mesh.shape["col"]
    constants = tables()

    def shards(observed, probe_signs, weights, kernels):
        pair = (2, TILE_ROWS, TILE_COLS)
        vmem = pl.BlockSpec(memory_space=pltpu.VMEM)
        operands = [observed, probe_signs, weights, jnp.transpose(kernels, (1, 0, 2)), *[jnp.asarray(c) for c in constants]]
        both = pl.pallas_call(
            functools.partial(kernel, row_count, col_count),
            out_shape=jax.ShapeDtypeStruct((2, *pair), F32),
            in_specs=[pl.BlockSpec(memory_space=pltpu.HBM)] * len(operands),
            out_specs=vmem,
            scratch_shapes=[
                *[pltpu.VMEM(x.shape, x.dtype) for x in operands],
                pltpu.VMEM((SLOTS, 320, TILE_COLS), BF16),
                pltpu.VMEM((SLOTS, TILE_ROWS, TILE_COLS), BF16),
                pltpu.VMEM((SLOTS, TILE_ROWS, TILE_COLS), BF16),
                pltpu.VMEM((TILE_ROWS, TILE_COLS), BF16),
                pltpu.VMEM((MODES, TAPS, TAPS), F32),
                pltpu.VMEM((MODES, 3 * TILE_ROWS, 2 * TILE_COLS), F32),
                pltpu.VMEM((2, MODES, 4, FREQS, FREQS), F32),
                pltpu.VMEM(pair, F32),
                pltpu.VMEM(pair, F32),
                pltpu.VMEM(pair, F32),
                pltpu.VMEM((16, TILE_COLS), F32),
                pltpu.VMEM((3, 1, TILE_COLS), F32),
                pltpu.VMEM((row_count * col_count // 2, 1, TILE_COLS), F32),
                pltpu.SemaphoreType.DMA((len(operands),)),
                pltpu.SemaphoreType.DMA((SLOTS,)),
                pltpu.SemaphoreType.DMA((8,)),
                *[pltpu.SemaphoreType.DMA] * 4,
                *[pltpu.SemaphoreType.REGULAR] * 2,
            ],
            compiler_params=pltpu.CompilerParams(
                collective_id=0, has_side_effects=True, vmem_limit_bytes=32 * 2**20
            ),
            name="deconvolve",
        )(*[pltpu.with_memory_space_constraint(x, pltpu.HBM) for x in operands])
        return both[0], both[1]

    return jax.shard_map(
        shards,
        mesh=mesh,
        in_specs=(P("row", "col"), P("row", "col"), P(None, "row", "col"), P()),
        out_specs=(P(None, "row", "col"), P(None, "row", "col")),
        check_vma=False,
    )
```

```python
import functools

import jax
import jax.numpy as jnp
import ml_dtypes
import numpy as np
from jax import lax
from jax.experimental import pallas as pl
from jax.experimental.pallas import tpu as pltpu
from jax.sharding import PartitionSpec as P

RADIUS = 64
MODES = 2
DAMPING = 1.0
TILE_ROWS = 64
TILE_COLS = 128
FREQS = 128
TAPS = 2 * RADIUS + 1
BF16 = jnp.bfloat16
F32 = jnp.float32
MESH = pl.DeviceIdType.MESH

WEIGHT_STAGE = 5
SLOTS = 12


def split(table):
    high = table.astype(ml_dtypes.bfloat16)
    low = (table - high.astype(np.float64)).astype(ml_dtypes.bfloat16)
    return np.stack([high, low])


def tables():
    theta = 2 * np.pi * (np.arange(FREQS) + 0.5) / 256
    phi = 2 * np.pi * np.arange(FREQS) / 128
    column = np.concatenate([64 + np.arange(128), 192 + np.arange(64), np.arange(64)])
    arg = np.outer(column, theta)
    into_cols = np.concatenate([np.cos(arg), -np.sin(arg)], 1)
    pieces = []
    for block in range(2):
        arg = np.outer(phi, 64 * block + np.arange(64))
        pieces.append(np.block([[np.cos(arg), np.sin(arg)], [-np.sin(arg), np.cos(arg)]]))
    into_rows = np.concatenate(pieces, 1)
    arg = np.outer(np.arange(64), phi)
    from_rows = np.block([[np.cos(arg), -np.sin(arg)], [np.sin(arg), np.cos(arg)]]) / 128
    arg = np.outer(theta, np.arange(128))
    from_cols = np.concatenate([np.cos(arg), -np.sin(arg)], 0) / 128
    arg = np.outer(np.arange(128), theta)
    tap_cols = np.concatenate([np.cos(arg), np.sin(arg)], 1)
    arg = np.outer(phi, np.arange(64))
    tap_rows = np.block([[np.cos(arg), -np.sin(arg)], [np.sin(arg), np.cos(arg)]])
    one_part = [t.astype(ml_dtypes.bfloat16) for t in (into_cols, into_rows)]
    return one_part + [split(t) for t in (from_rows, from_cols, tap_cols, tap_rows)]


def dot(a, b):
    return jnp.dot(a, b, preferred_element_type=F32)


def halves(x):
    high = x.astype(BF16)
    return high, (x - high.astype(F32)).astype(BF16)


def dot_parts_right(table, x):
    high, low = halves(x)
    return dot(table, high) + dot(table, low)


def dot_both_right(table, x):
    high, low = halves(x)
    rows = table.shape[1]
    both = dot(table[...].reshape(2 * rows, table.shape[2]), high)
    return both[:rows] + (both[rows:] + dot(table[0], low))


def dot_both_left(x, table):
    high, low = halves(x)
    rows = x.shape[0]
    both = dot(jnp.concatenate([high, low], 0), table[0])
    return both[:rows] + (both[rows:] + dot(high, table[1]))


def kernel(
    row_count,
    col_count,
    observed_hbm,
    probe_hbm,
    weights_hbm,
    taps_hbm,
    into_cols_hbm,
    into_rows_hbm,
    from_rows_hbm,
    from_cols_hbm,
    tap_cols_hbm,
    tap_rows_hbm,
    out,
    observed,
    probe,
    weights,
    taps,
    into_cols,
    into_rows,
    from_rows,
    from_cols,
    tap_cols,
    tap_rows,
    got,
    own,
    packed,
    zeros,
    planes,
    patch_weights,
    responses,
    first,
    image,
    second,
    parts,
    mine,
    all_sums,
    load_sem,
    got_sem,
    sent_sem,
    sums_in,
    sums_out,
    told_4,
    told_8,
):
    my_row = lax.axis_index("row")
    my_col = lax.axis_index("col")
    up_ok, down_ok = my_row > 0, my_row < row_count - 1
    left_ok, right_ok = my_col > 0, my_col < col_count - 1

    loads = [
        pltpu.make_async_copy(src, dst, load_sem.at[i])
        for i, (src, dst) in enumerate(
            (
                (observed_hbm, observed),
                (probe_hbm, probe),
                (weights_hbm, weights),
                (taps_hbm, taps),
                (tap_cols_hbm, tap_cols),
                (tap_rows_hbm, tap_rows),
                (into_cols_hbm, into_cols),
                (into_rows_hbm, into_rows),
                (from_rows_hbm, from_rows),
                (from_cols_hbm, from_cols),
            )
        )
    ]
    barrier = pltpu.get_barrier_semaphore()

    def greet(row, col):
        pl.semaphore_signal(barrier, inc=1, device_id=(row, col), device_id_type=MESH)

    row_there, col_there = {-1: up_ok, 1: down_ok}, {-1: left_ok, 1: right_ok}
    neighbours = [(dr, dc, row_there[dr] & col_there[dc]) for dr in (-1, 1) for dc in (-1, 1)]
    neighbours += [(dr, 0, row_there[dr]) for dr in (-1, 1)]
    neighbours += [(0, dc, col_there[dc]) for dc in (-1, 1)]
    for dr, dc, there in neighbours:
        pl.when(there)(functools.partial(greet, my_row + dr, my_col + dc))
    for load in loads[:2]:
        load.start()
    for load in loads[2:]:
        load.start()
    rows_here = 1 + up_ok.astype(jnp.int32) + down_ok.astype(jnp.int32)
    cols_here = 1 + left_ok.astype(jnp.int32) + right_ok.astype(jnp.int32)
    partners = rows_here * cols_here - 1

    lane = lax.broadcasted_iota(jnp.int32, (32, TILE_COLS), 1)
    low_lanes = lane < 64

    def place(slot, tile):
        own[slot] = tile.astype(BF16)
        turned = pltpu.roll(tile, 64, 1)
        packed[slot, 0:32] = jnp.where(low_lanes, tile[0:32], turned[32:64]).astype(BF16)
        packed[slot, 32:64] = jnp.where(low_lanes, turned[0:32], tile[32:64]).astype(BF16)

    def landing(slot, dr, dc):
        if dc == 0:
            return got.at[slot, pl.ds(0 if dr < 0 else 64, 64)]
        return got.at[slot, pl.ds(128 + 64 * (1 + dr) + (32 if dc < 0 else 0), 32)]

    def send(slot):
        for i, (dr, dc, there) in enumerate(neighbours):
            if dc == 0:
                piece = own.at[slot]
            else:
                piece = packed.at[slot, pl.ds(0 if dc < 0 else 32, 32)]
            out = pltpu.make_async_remote_copy(
                src_ref=piece,
                dst_ref=landing(slot, -dr, -dc),
                send_sem=sent_sem.at[i],
                recv_sem=got_sem.at[slot],
                device_id=(my_row + dr, my_col + dc),
                device_id_type=MESH,
            )
            pl.when(there)(out.start)

    def fill_edges(slot, c):
        for dr, dc, there in neighbours:
            edge = landing(slot, dr, dc)
            fill = pltpu.make_async_copy(zeros.at[pl.ds(0, edge.shape[0])], edge, got_sem.at[slot])
            pl.when(jnp.logical_not(there))(fill.start)
        return c

    def arrived(slot):
        pltpu.make_async_copy(got.at[slot], got.at[slot], got_sem.at[slot]).wait()

    def all_sent():
        for i, (dr, dc, there) in enumerate(neighbours):
            every = got.at[:, pl.ds(0, 64 if dc == 0 else 32)]
            pl.when(there)(pltpu.make_async_copy(every, every, sent_sem.at[i]).wait)

    def halo(slot, k):
        right = got[slot, 128 + 64 * k : 160 + 64 * k].astype(F32)
        left = got[slot, 160 + 64 * k : 192 + 64 * k].astype(F32)
        top = jnp.where(low_lanes, right, pltpu.roll(left, 64, 1))
        bottom = jnp.where(low_lanes, pltpu.roll(right, 64, 1), left)
        return jnp.concatenate([top, bottom], 0)

    def patch(slot, middle):
        above, below = got[slot, 0:64].astype(F32), got[slot, 64:128].astype(F32)
        return [
            jnp.concatenate([tile, halo(slot, k)], 1) for k, tile in enumerate((above, middle, below))
        ]

    def columns_of(x):
        return dot(x, into_cols[...])

    def stacked(y, k):
        parts = []
        for b in (k, k + 1):
            rows = y[64 * b : 64 * b + 64]
            parts += [rows[:, :128], rows[:, 128:]]
        return jnp.concatenate(parts, 0)

    def adjoint(slot):
        tiles = (got[slot, 0:64], own[slot], got[slot, 64:128])
        x = jnp.concatenate(
            [jnp.concatenate([tile, halo(slot, k).astype(BF16)], 1) for k, tile in enumerate(tiles)], 0
        )
        y = columns_of(x)
        z = dot_parts_right(into_rows[...], jnp.concatenate([stacked(y, 0), stacked(y, 1)], 1))
        are, aim = z[:128, :128], z[128:, :128]
        bre, bim = z[:128, 128:], z[128:, 128:]
        reals, imags = [], []
        for m in range(MODES):
            h = [responses[1, m, i] for i in range(4)]
            reals.append(h[0] * are - h[1] * aim + (h[2] * bre - h[3] * bim))
            imags.append(h[0] * aim + h[1] * are + (h[2] * bim + h[3] * bre))
        spectrum = jnp.concatenate([jnp.concatenate(reals, 1), jnp.concatenate(imags, 1)], 0)
        v = dot_both_right(from_rows, spectrum)
        rows = [
            jnp.concatenate([v[:64, 128 * m : 128 * m + 128], v[64:, 128 * m : 128 * m + 128]], 1)
            for m in range(MODES)
        ]
        out = dot_both_left(jnp.concatenate(rows, 0), from_cols)
        return weights[0] * out[:64] + weights[1] * out[64:]

    def forward(values):
        x = jnp.concatenate(
            [
                (patch_weights[m, 64 * k : 64 * k + 64] * values[k]).astype(BF16)
                for m in range(MODES)
                for k in range(3)
            ],
            0,
        )
        y = columns_of(x)
        z = [
            dot_parts_right(
                into_rows[...], jnp.concatenate([stacked(y[:192], k), stacked(y[192:], k)], 1)
            )
            for k in range(2)
        ]
        real = jnp.zeros((FREQS, FREQS), F32)
        imag = real
        for m in range(MODES):
            h = [responses[0, m, i] for i in range(4)]
            lanes = slice(128 * m, 128 * m + 128)
            are, aim = z[0][:128, lanes], z[0][128:, lanes]
            bre, bim = z[1][:128, lanes], z[1][128:, lanes]
            real = real + (h[0] * are - h[1] * aim + (h[2] * bre - h[3] * bim))
            imag = imag + (h[0] * aim + h[1] * are + (h[2] * bim + h[3] * bre))
        v = dot_both_right(from_rows, jnp.concatenate([real, imag], 0))
        return dot_both_left(jnp.concatenate([v[:64], v[64:]], 1), from_cols)

    def build_responses(m, c):
        narrow = planes[m, :, 0:128].astype(BF16)
        even_lane = lax.broadcasted_iota(jnp.int32, (1, FREQS), 1) % 2 == 0
        sign_f = jnp.where(even_lane, 1.0, -1.0)
        even_row = lax.broadcasted_iota(jnp.int32, (FREQS, 1), 0) % 2 == 0
        sign_q = jnp.where(even_row, 1.0, -1.0)
        cols = dot(narrow, tap_cols[0]) + dot(narrow, tap_cols[1])
        re = cols[:, :128]
        im = cols[:, 128:] + planes[m, :, 128:129] * sign_f
        pairs = jnp.concatenate(
            [
                jnp.concatenate([re[0:64], re[64:128]], 1),
                jnp.concatenate([im[0:64], im[64:128]], 1),
            ],
            0,
        )
        high, low = halves(pairs)
        g = dot(tap_rows[0], high) + (dot(tap_rows[0], low) + dot(tap_rows[1], high))
        g0re, g0im, g1re, g1im = g[:128, :128], g[128:, :128], g[:128, 128:], g[128:, 128:]
        mid_re, mid_im, last_re, last_im = re[64:65], im[64:65], re[128:129], im[128:129]
        responses[0, m, 0] = g0re
        responses[0, m, 1] = g0im
        responses[0, m, 2] = g1re + sign_q * last_re
        responses[0, m, 3] = g1im + sign_q * last_im
        responses[1, m, 0] = sign_f * (sign_q * (g1im - mid_im) + last_im)
        responses[1, m, 1] = sign_f * (sign_q * (g1re - mid_re) + last_re)
        responses[1, m, 2] = sign_f * (sign_q * g0im + mid_im)
        responses[1, m, 3] = sign_f * (sign_q * g0re + mid_re)
        return c

    def note(n, i, part):
        parts[pl.ds(6 * n + i, 1)] = jnp.sum(part, axis=0, keepdims=True)

    def tell(semaphore, steps):
        for dr, dc in steps:
            row, col = my_row + dr, my_col + dc
            there = (row >= 0) & (row < row_count) & (col >= 0) & (col < col_count)

            @pl.when(there)
            def _(row=row, col=col):
                pl.semaphore_signal(semaphore, inc=1, device_id=(row, col), device_id_type=MESH)

    def both_ways(down, across):
        rows = 1 + (my_row >= down).astype(jnp.int32) + (my_row + down < row_count).astype(jnp.int32)
        cols = 1 + (my_col >= across).astype(jnp.int32) + (my_col + across < col_count).astype(jnp.int32)
        return rows * cols - 1

    def tell_4():
        tell(told_4, [(4 * i, 4 * j) for i in (-1, 0, 1) for j in (-1, 0, 1) if i or j])

    def tell_8():
        tell(told_8, [(0, -8), (0, 8)])

    z_count, y_count = row_count // 2, col_count // 4
    my_z, my_y = my_row // 2, lax.rem(my_col // 2, y_count)
    my_x, my_core = 2 * (my_col // (2 * y_count)) + lax.rem(my_row, 2), lax.rem(my_col, 2)
    me = my_row * col_count + my_col
    others = row_count * col_count - 1

    def start_sums():
        totals = jnp.sum(parts[...], axis=1, keepdims=True)
        here = lax.broadcasted_iota(jnp.int32, (16, TILE_COLS), 0) == lax.broadcasted_iota(
            jnp.int32, (16, TILE_COLS), 1
        )
        mine[...] = jnp.sum(jnp.where(here, totals, 0.0), axis=0, keepdims=True)
        places = []
        for dx in (1, 2, 3, 0):
            x = lax.rem(my_x + dx, 4)
            for dcore in (1, 0):
                core = lax.rem(my_core + dcore, 2)
                places.append((lax.rem(x, 2), (x // 2) * 2 * y_count + core, dx == 0 and dcore == 0))

        def go(i, c):
            z, y = i // y_count, lax.rem(i, y_count)
            for x_row, x_col, same in places:
                out = pltpu.make_async_remote_copy(
                    src_ref=mine,
                    dst_ref=all_sums.at[me],
                    send_sem=sums_out,
                    recv_sem=sums_in,
                    device_id=(2 * z + x_row, 2 * y + x_col),
                    device_id_type=MESH,
                )
                if same:
                    pl.when((z != my_z) | (y != my_y))(out.start)
                else:
                    out.start()
            return c

        lax.fori_loop(0, z_count * y_count, go, 0)
        all_sums[me] = mine[...]

    def summed():
        rest = all_sums.at[pl.ds(0, others)]
        pltpu.make_async_copy(rest, rest, sums_in).wait()
        lanes = [all_sums[i] for i in range(8)]
        for i in range(8, others + 1):
            lanes[i % 8] = lanes[i % 8] + all_sums[i]
        while len(lanes) > 1:
            lanes = [a + b for a, b in zip(lanes[::2], lanes[1::2])]
        return lanes[0]

    def sums_sent():
        rest = all_sums.at[pl.ds(0, others)]
        pltpu.make_async_copy(rest, rest, sums_out).wait()

    zeros[...] = jnp.zeros_like(zeros)
    parts[...] = jnp.zeros_like(parts)
    for load in loads[:2]:
        load.wait()
    place(0, observed[...].astype(F32))
    place(1, (2 * probe[...] - 1).astype(F32))
    pl.semaphore_wait(barrier, partners)
    for slot in (0, 1):
        send(slot)
    loads[2].wait()
    for m in range(MODES):
        place(2 * WEIGHT_STAGE + m, weights[m])
        send(2 * WEIGHT_STAGE + m)
    lax.fori_loop(0, SLOTS, fill_edges, 0)
    for load in loads[3:]:
        load.wait()
    for m in range(MODES):
        planes[m] = taps[:, m, :].astype(F32)
    energy = jnp.sum(jnp.sum(planes[0] * planes[0] + planes[1] * planes[1], axis=0, keepdims=True), axis=1, keepdims=True)
    trial = 1.0 / (DAMPING + 0.85 * energy)
    lax.fori_loop(0, MODES, build_responses, 0)

    def right_side(n, c):
        arrived(n)
        r = adjoint(n)
        first[n] = r
        place(2 + n, r)
        send(2 + n)
        return c

    lax.fori_loop(0, 2, right_side, 0)

    def spread_weights(m, c):
        slot = 2 * WEIGHT_STAGE + m
        arrived(slot)
        for k, b in enumerate(patch(slot, weights[m])):
            patch_weights[m, 64 * k : 64 * k + 64] = b
        return c

    lax.fori_loop(0, MODES, spread_weights, 0)

    def blur_first(n, c):
        arrived(2 + n)
        r = first[n]
        place(4 + n, forward(patch(2 + n, r)))
        send(4 + n)
        u = own[4 + n].astype(F32)
        note(n, 0, r * r)
        note(n, 3, u * u)
        return c

    lax.fori_loop(0, 2, blur_first, 0)

    def back_first(n, c):
        arrived(4 + n)

        @pl.when(n == 0)
        def _():
            tell_4()

        r = first[n]
        w = adjoint(4 + n) + DAMPING * r
        v = r - trial * w
        place(6 + n, v)
        send(6 + n)
        image[n] = w
        second[n] = v
        note(n, 1, r * v)
        note(n, 2, v * v)
        return c

    lax.fori_loop(0, 2, back_first, 0)
    pl.semaphore_wait(told_4, both_ways(4, 4))
    tell_8()

    def blur_second(n, c):
        arrived(6 + n)
        place(8 + n, forward(patch(6 + n, second[n])))
        u, before = own[8 + n].astype(F32), own[4 + n].astype(F32)
        note(n, 4, u * before)
        note(n, 5, u * u)

        @pl.when(n == 1)
        def _():
            pl.semaphore_wait(told_8, both_ways(row_count, 8))
            start_sums()

        send(8 + n)
        return c

    lax.fori_loop(0, 2, blur_second, 0)

    def back_second(n, c):
        arrived(8 + n)
        out[1, n] = adjoint(8 + n) + DAMPING * second[n]
        return c

    lax.fori_loop(0, 2, back_second, 0)
    all_sent()
    sums_sent()
    total = summed()
    for n in range(2):
        rr, rv, vv, uu, ut, tt = (total[:, i : i + 1] for i in range(6 * n, 6 * n + 6))
        curve0 = uu + DAMPING * rr
        step0 = rr / curve0
        turn = step0 / trial
        keep = 1.0 - turn
        norm1 = keep * keep * rr + 2.0 * keep * turn * rv + turn * turn * vv
        along = keep + norm1 / rr
        curve1 = along * along * curve0 + (
            2.0 * along * turn * (ut + DAMPING * rv) + turn * turn * (tt + DAMPING * vv)
        )
        step1 = norm1 / curve1
        r, v = first[n], second[n]
        out[0, n] = (step0 + step1 * along) * r + (step1 * turn) * v
        out[1, n] = (keep * r + turn * v) - step1 * (along * image[n] + turn * out[1, n])


def solution(mesh):
    row_count, col_count = mesh.shape["row"], mesh.shape["col"]
    constants = tables()

    def shards(observed, probe_signs, weights, kernels):
        pair = (2, TILE_ROWS, TILE_COLS)
        vmem = pl.BlockSpec(memory_space=pltpu.VMEM)
        operands = [observed, probe_signs, weights, jnp.transpose(kernels, (1, 0, 2)), *[jnp.asarray(c) for c in constants]]
        both = pl.pallas_call(
            functools.partial(kernel, row_count, col_count),
            out_shape=jax.ShapeDtypeStruct((2, *pair), F32),
            in_specs=[pl.BlockSpec(memory_space=pltpu.HBM)] * len(operands),
            out_specs=vmem,
            scratch_shapes=[
                *[pltpu.VMEM(x.shape, x.dtype) for x in operands],
                pltpu.VMEM((SLOTS, 320, TILE_COLS), BF16),
                pltpu.VMEM((SLOTS, TILE_ROWS, TILE_COLS), BF16),
                pltpu.VMEM((SLOTS, TILE_ROWS, TILE_COLS), BF16),
                pltpu.VMEM((TILE_ROWS, TILE_COLS), BF16),
                pltpu.VMEM((MODES, TAPS, TAPS), F32),
                pltpu.VMEM((MODES, 3 * TILE_ROWS, 2 * TILE_COLS), F32),
                pltpu.VMEM((2, MODES, 4, FREQS, FREQS), F32),
                pltpu.VMEM(pair, F32),
                pltpu.VMEM(pair, F32),
                pltpu.VMEM(pair, F32),
                pltpu.VMEM((16, TILE_COLS), F32),
                pltpu.VMEM((1, TILE_COLS), F32),
                pltpu.VMEM((row_count * col_count, 1, TILE_COLS), F32),
                pltpu.SemaphoreType.DMA((len(operands),)),
                pltpu.SemaphoreType.DMA((SLOTS,)),
                pltpu.SemaphoreType.DMA((8,)),
                *[pltpu.SemaphoreType.DMA] * 2,
                *[pltpu.SemaphoreType.REGULAR] * 2,
            ],
            compiler_params=pltpu.CompilerParams(
                collective_id=0, has_side_effects=True, vmem_limit_bytes=32 * 2**20
            ),
            name="deconvolve",
        )(*[pltpu.with_memory_space_constraint(x, pltpu.HBM) for x in operands])
        return both[0], both[1]

    return jax.shard_map(
        shards,
        mesh=mesh,
        in_specs=(P("row", "col"), P("row", "col"), P(None, "row", "col"), P()),
        out_specs=(P(None, "row", "col"), P(None, "row", "col")),
        check_vma=False,
    )
```

```python
import functools

import jax
import jax.numpy as jnp
import ml_dtypes
import numpy as np
from jax import lax
from jax.experimental import pallas as pl
from jax.experimental.pallas import tpu as pltpu
from jax.sharding import PartitionSpec as P

RADIUS = 64
MODES = 2
DAMPING = 1.0
TILE_ROWS = 64
TILE_COLS = 128
FREQS = 128
TAPS = 2 * RADIUS + 1
BF16 = jnp.bfloat16
F32 = jnp.float32
MESH = pl.DeviceIdType.MESH

WEIGHT_STAGE = 5
SLOTS = 12


def split(table):
    high = table.astype(ml_dtypes.bfloat16)
    low = (table - high.astype(np.float64)).astype(ml_dtypes.bfloat16)
    return np.stack([high, low])


def tables():
    theta = 2 * np.pi * (np.arange(FREQS) + 0.5) / 256
    phi = 2 * np.pi * np.arange(FREQS) / 128
    column = np.concatenate([64 + np.arange(128), 192 + np.arange(64), np.arange(64)])
    arg = np.outer(column, theta)
    into_cols = np.concatenate([np.cos(arg), -np.sin(arg)], 1)
    pieces = []
    for block in range(2):
        arg = np.outer(phi, 64 * block + np.arange(64))
        pieces.append(np.block([[np.cos(arg), np.sin(arg)], [-np.sin(arg), np.cos(arg)]]))
    into_rows = np.concatenate(pieces, 1)
    arg = np.outer(np.arange(64), phi)
    from_rows = np.block([[np.cos(arg), -np.sin(arg)], [np.sin(arg), np.cos(arg)]]) / 128
    arg = np.outer(theta, np.arange(128))
    from_cols = np.concatenate([np.cos(arg), -np.sin(arg)], 0) / 128
    arg = np.outer(np.arange(128), theta)
    tap_cols = np.concatenate([np.cos(arg), np.sin(arg)], 1)
    arg = np.outer(phi, np.arange(64))
    tap_rows = np.block([[np.cos(arg), -np.sin(arg)], [np.sin(arg), np.cos(arg)]])
    one_part = [t.astype(ml_dtypes.bfloat16) for t in (into_cols, into_rows)]
    return one_part + [split(t) for t in (from_rows, from_cols, tap_cols, tap_rows)]


def dot(a, b):
    return jnp.dot(a, b, preferred_element_type=F32)


def halves(x):
    high = x.astype(BF16)
    return high, (x - high.astype(F32)).astype(BF16)


def dot_parts_right(table, x):
    high, low = halves(x)
    return dot(table, high) + dot(table, low)


def dot_both_right(table, x):
    high, low = halves(x)
    rows = table.shape[1]
    both = dot(table[...].reshape(2 * rows, table.shape[2]), high)
    return both[:rows] + (both[rows:] + dot(table[0], low))


def dot_both_left(x, table):
    high, low = halves(x)
    rows = x.shape[0]
    both = dot(jnp.concatenate([high, low], 0), table[0])
    return both[:rows] + (both[rows:] + dot(high, table[1]))


def kernel(
    row_count,
    col_count,
    observed_hbm,
    probe_hbm,
    weights_hbm,
    taps_hbm,
    into_cols_hbm,
    into_rows_hbm,
    from_rows_hbm,
    from_cols_hbm,
    tap_cols_hbm,
    tap_rows_hbm,
    out,
    observed,
    probe,
    weights,
    taps,
    into_cols,
    into_rows,
    from_rows,
    from_cols,
    tap_cols,
    tap_rows,
    got,
    own,
    packed,
    zeros,
    planes,
    patch_weights,
    responses,
    first,
    image,
    second,
    parts,
    mine,
    all_sums,
    load_sem,
    got_sem,
    sent_sem,
    sums_in,
    sums_out,
    told_4,
    told_8,
):
    my_row = lax.axis_index("row")
    my_col = lax.axis_index("col")
    up_ok, down_ok = my_row > 0, my_row < row_count - 1
    left_ok, right_ok = my_col > 0, my_col < col_count - 1

    loads = [
        pltpu.make_async_copy(src, dst, load_sem.at[i])
        for i, (src, dst) in enumerate(
            (
                (observed_hbm, observed),
                (probe_hbm, probe),
                (weights_hbm, weights),
                (taps_hbm, taps),
                (tap_cols_hbm, tap_cols),
                (tap_rows_hbm, tap_rows),
                (into_cols_hbm, into_cols),
                (into_rows_hbm, into_rows),
                (from_rows_hbm, from_rows),
                (from_cols_hbm, from_cols),
            )
        )
    ]
    barrier = pltpu.get_barrier_semaphore()

    def greet(row, col):
        pl.semaphore_signal(barrier, inc=1, device_id=(row, col), device_id_type=MESH)

    row_there, col_there = {-1: up_ok, 1: down_ok}, {-1: left_ok, 1: right_ok}
    neighbours = [(dr, dc, row_there[dr] & col_there[dc]) for dr in (-1, 1) for dc in (-1, 1)]
    neighbours += [(dr, 0, row_there[dr]) for dr in (-1, 1)]
    neighbours += [(0, dc, col_there[dc]) for dc in (-1, 1)]
    for dr, dc, there in neighbours:
        pl.when(there)(functools.partial(greet, my_row + dr, my_col + dc))
    for load in loads[:2]:
        load.start()
    for load in loads[2:]:
        load.start()
    rows_here = 1 + up_ok.astype(jnp.int32) + down_ok.astype(jnp.int32)
    cols_here = 1 + left_ok.astype(jnp.int32) + right_ok.astype(jnp.int32)
    partners = rows_here * cols_here - 1

    lane = lax.broadcasted_iota(jnp.int32, (32, TILE_COLS), 1)
    low_lanes = lane < 64

    def place(slot, tile):
        own[slot] = tile.astype(BF16)
        turned = pltpu.roll(tile, 64, 1)
        packed[slot, 0:32] = jnp.where(low_lanes, tile[0:32], turned[32:64]).astype(BF16)
        packed[slot, 32:64] = jnp.where(low_lanes, turned[0:32], tile[32:64]).astype(BF16)

    def landing(slot, dr, dc):
        if dc == 0:
            return got.at[slot, pl.ds(0 if dr < 0 else 64, 64)]
        return got.at[slot, pl.ds(128 + 64 * (1 + dr) + (32 if dc < 0 else 0), 32)]

    def send(slot):
        for i, (dr, dc, there) in enumerate(neighbours):
            if dc == 0:
                piece = own.at[slot]
            else:
                piece = packed.at[slot, pl.ds(0 if dc < 0 else 32, 32)]
            out = pltpu.make_async_remote_copy(
                src_ref=piece,
                dst_ref=landing(slot, -dr, -dc),
                send_sem=sent_sem.at[i],
                recv_sem=got_sem.at[slot],
                device_id=(my_row + dr, my_col + dc),
                device_id_type=MESH,
            )
            pl.when(there)(out.start)

    def fill_edges(slot, c):
        for dr, dc, there in neighbours:
            edge = landing(slot, dr, dc)
            fill = pltpu.make_async_copy(zeros.at[pl.ds(0, edge.shape[0])], edge, got_sem.at[slot])
            pl.when(jnp.logical_not(there))(fill.start)
        return c

    def arrived(slot):
        pltpu.make_async_copy(got.at[slot], got.at[slot], got_sem.at[slot]).wait()

    def all_sent():
        for i, (dr, dc, there) in enumerate(neighbours):
            every = got.at[:, pl.ds(0, 64 if dc == 0 else 32)]
            pl.when(there)(pltpu.make_async_copy(every, every, sent_sem.at[i]).wait)

    def halo(slot, k):
        right = got[slot, 128 + 64 * k : 160 + 64 * k].astype(F32)
        left = got[slot, 160 + 64 * k : 192 + 64 * k].astype(F32)
        top = jnp.where(low_lanes, right, pltpu.roll(left, 64, 1))
        bottom = jnp.where(low_lanes, pltpu.roll(right, 64, 1), left)
        return jnp.concatenate([top, bottom], 0)

    def patch(slot, middle):
        above, below = got[slot, 0:64].astype(F32), got[slot, 64:128].astype(F32)
        return [
            jnp.concatenate([tile, halo(slot, k)], 1) for k, tile in enumerate((above, middle, below))
        ]

    def columns_of(x):
        return dot(x, into_cols[...])

    def stacked(y, k):
        parts = []
        for b in (k, k + 1):
            rows = y[64 * b : 64 * b + 64]
            parts += [rows[:, :128], rows[:, 128:]]
        return jnp.concatenate(parts, 0)

    def adjoint(slot):
        tiles = (got[slot, 0:64], own[slot], got[slot, 64:128])
        x = jnp.concatenate(
            [jnp.concatenate([tile, halo(slot, k).astype(BF16)], 1) for k, tile in enumerate(tiles)], 0
        )
        y = columns_of(x)
        z = dot_parts_right(into_rows[...], jnp.concatenate([stacked(y, 0), stacked(y, 1)], 1))
        are, aim = z[:128, :128], z[128:, :128]
        bre, bim = z[:128, 128:], z[128:, 128:]
        reals, imags = [], []
        for m in range(MODES):
            h = [responses[1, m, i] for i in range(4)]
            reals.append(h[0] * are - h[1] * aim + (h[2] * bre - h[3] * bim))
            imags.append(h[0] * aim + h[1] * are + (h[2] * bim + h[3] * bre))
        spectrum = jnp.concatenate([jnp.concatenate(reals, 1), jnp.concatenate(imags, 1)], 0)
        v = dot_both_right(from_rows, spectrum)
        rows = [
            jnp.concatenate([v[:64, 128 * m : 128 * m + 128], v[64:, 128 * m : 128 * m + 128]], 1)
            for m in range(MODES)
        ]
        out = dot_both_left(jnp.concatenate(rows, 0), from_cols)
        return weights[0] * out[:64] + weights[1] * out[64:]

    def forward(values):
        x = jnp.concatenate(
            [
                (patch_weights[m, 64 * k : 64 * k + 64] * values[k]).astype(BF16)
                for m in range(MODES)
                for k in range(3)
            ],
            0,
        )
        y = columns_of(x)
        z = [
            dot_parts_right(
                into_rows[...], jnp.concatenate([stacked(y[:192], k), stacked(y[192:], k)], 1)
            )
            for k in range(2)
        ]
        real = jnp.zeros((FREQS, FREQS), F32)
        imag = real
        for m in range(MODES):
            h = [responses[0, m, i] for i in range(4)]
            lanes = slice(128 * m, 128 * m + 128)
            are, aim = z[0][:128, lanes], z[0][128:, lanes]
            bre, bim = z[1][:128, lanes], z[1][128:, lanes]
            real = real + (h[0] * are - h[1] * aim + (h[2] * bre - h[3] * bim))
            imag = imag + (h[0] * aim + h[1] * are + (h[2] * bim + h[3] * bre))
        v = dot_both_right(from_rows, jnp.concatenate([real, imag], 0))
        return dot_both_left(jnp.concatenate([v[:64], v[64:]], 1), from_cols)

    def build_responses(m, c):
        narrow = planes[m, :, 0:128].astype(BF16)
        even_lane = lax.broadcasted_iota(jnp.int32, (1, FREQS), 1) % 2 == 0
        sign_f = jnp.where(even_lane, 1.0, -1.0)
        even_row = lax.broadcasted_iota(jnp.int32, (FREQS, 1), 0) % 2 == 0
        sign_q = jnp.where(even_row, 1.0, -1.0)
        cols = dot(narrow, tap_cols[0]) + dot(narrow, tap_cols[1])
        re = cols[:, :128]
        im = cols[:, 128:] + planes[m, :, 128:129] * sign_f
        pairs = jnp.concatenate(
            [
                jnp.concatenate([re[0:64], re[64:128]], 1),
                jnp.concatenate([im[0:64], im[64:128]], 1),
            ],
            0,
        )
        high, low = halves(pairs)
        g = dot(tap_rows[0], high) + (dot(tap_rows[0], low) + dot(tap_rows[1], high))
        g0re, g0im, g1re, g1im = g[:128, :128], g[128:, :128], g[:128, 128:], g[128:, 128:]
        mid_re, mid_im, last_re, last_im = re[64:65], im[64:65], re[128:129], im[128:129]
        responses[0, m, 0] = g0re
        responses[0, m, 1] = g0im
        responses[0, m, 2] = g1re + sign_q * last_re
        responses[0, m, 3] = g1im + sign_q * last_im
        responses[1, m, 0] = sign_f * (sign_q * (g1im - mid_im) + last_im)
        responses[1, m, 1] = sign_f * (sign_q * (g1re - mid_re) + last_re)
        responses[1, m, 2] = sign_f * (sign_q * g0im + mid_im)
        responses[1, m, 3] = sign_f * (sign_q * g0re + mid_re)
        return c

    def note(n, i, part):
        parts[pl.ds(6 * n + i, 1)] = jnp.sum(part, axis=0, keepdims=True)

    def tell(semaphore, steps):
        for dr, dc in steps:
            row, col = my_row + dr, my_col + dc
            there = (row >= 0) & (row < row_count) & (col >= 0) & (col < col_count)

            @pl.when(there)
            def _(row=row, col=col):
                pl.semaphore_signal(semaphore, inc=1, device_id=(row, col), device_id_type=MESH)

    def both_ways(down, across):
        rows = 1 + (my_row >= down).astype(jnp.int32) + (my_row + down < row_count).astype(jnp.int32)
        cols = 1 + (my_col >= across).astype(jnp.int32) + (my_col + across < col_count).astype(jnp.int32)
        return rows * cols - 1

    def tell_4():
        tell(told_4, [(4 * i, 4 * j) for i in (-1, 0, 1) for j in (-1, 0, 1) if i or j])

    def tell_8():
        tell(told_8, [(0, -8), (0, 8)])

    z_count, y_count = row_count // 2, col_count // 4
    my_z, my_y = my_row // 2, lax.rem(my_col // 2, y_count)
    my_x, my_core = 2 * (my_col // (2 * y_count)) + lax.rem(my_row, 2), lax.rem(my_col, 2)
    me = my_row * col_count + my_col
    others = row_count * col_count - 1

    def start_sums():
        totals = jnp.sum(parts[...], axis=1, keepdims=True)
        here = lax.broadcasted_iota(jnp.int32, (16, TILE_COLS), 0) == lax.broadcasted_iota(
            jnp.int32, (16, TILE_COLS), 1
        )
        mine[...] = jnp.sum(jnp.where(here, totals, 0.0), axis=0, keepdims=True)
        places = []
        for dx in (1, 2, 3, 0):
            x = lax.rem(my_x + dx, 4)
            for dcore in (1, 0):
                core = lax.rem(my_core + dcore, 2)
                places.append((lax.rem(x, 2), (x // 2) * 2 * y_count + core, dx == 0 and dcore == 0))

        def go(i, c):
            z, y = i // y_count, lax.rem(i, y_count)
            for x_row, x_col, same in places:
                out = pltpu.make_async_remote_copy(
                    src_ref=mine,
                    dst_ref=all_sums.at[me],
                    send_sem=sums_out,
                    recv_sem=sums_in,
                    device_id=(2 * z + x_row, 2 * y + x_col),
                    device_id_type=MESH,
                )
                if same:
                    pl.when((z != my_z) | (y != my_y))(out.start)
                else:
                    out.start()
            return c

        lax.fori_loop(0, z_count * y_count, go, 0)
        all_sums[me] = mine[...]

    def summed():
        rest = all_sums.at[pl.ds(0, others)]
        pltpu.make_async_copy(rest, rest, sums_in).wait()
        lanes = [all_sums[i] for i in range(8)]
        for i in range(8, others + 1):
            lanes[i % 8] = lanes[i % 8] + all_sums[i]
        while len(lanes) > 1:
            lanes = [a + b for a, b in zip(lanes[::2], lanes[1::2])]
        return lanes[0]

    def sums_sent():
        rest = all_sums.at[pl.ds(0, others)]
        pltpu.make_async_copy(rest, rest, sums_out).wait()

    zeros[...] = jnp.zeros_like(zeros)
    parts[...] = jnp.zeros_like(parts)
    for load in loads[:2]:
        load.wait()
    place(0, observed[...].astype(F32))
    place(1, (2 * probe[...] - 1).astype(F32))
    pl.semaphore_wait(barrier, partners)
    for slot in (0, 1):
        send(slot)
    loads[2].wait()
    for m in range(MODES):
        place(2 * WEIGHT_STAGE + m, weights[m])
        send(2 * WEIGHT_STAGE + m)
    at_border = jnp.logical_not(up_ok & down_ok & left_ok & right_ok)

    @pl.when(at_border)
    def _():
        lax.fori_loop(0, SLOTS, fill_edges, 0)

    for load in loads[3:]:
        load.wait()
    for m in range(MODES):
        planes[m] = taps[:, m, :].astype(F32)
    energy = jnp.sum(jnp.sum(planes[0] * planes[0] + planes[1] * planes[1], axis=0, keepdims=True), axis=1, keepdims=True)
    trial = 1.0 / (DAMPING + 0.85 * energy)
    lax.fori_loop(0, MODES, build_responses, 0)

    def right_side(n, c):
        arrived(n)
        r = adjoint(n)
        first[n] = r
        place(2 + n, r)
        send(2 + n)
        return c

    lax.fori_loop(0, 2, right_side, 0)

    def spread_weights(m, c):
        slot = 2 * WEIGHT_STAGE + m
        arrived(slot)
        for k, b in enumerate(patch(slot, weights[m])):
            patch_weights[m, 64 * k : 64 * k + 64] = b
        return c

    lax.fori_loop(0, MODES, spread_weights, 0)

    def blur_first(n, c):
        arrived(2 + n)
        r = first[n]
        place(4 + n, forward(patch(2 + n, r)))
        send(4 + n)
        u = own[4 + n].astype(F32)
        note(n, 0, r * r)
        note(n, 3, u * u)
        return c

    lax.fori_loop(0, 2, blur_first, 0)

    def back_first(n, c):
        arrived(4 + n)

        @pl.when(n == 0)
        def _():
            tell_4()

        r = first[n]
        w = adjoint(4 + n) + DAMPING * r
        v = r - trial * w
        place(6 + n, v)
        send(6 + n)
        image[n] = w
        second[n] = v
        note(n, 1, r * v)
        note(n, 2, v * v)
        return c

    lax.fori_loop(0, 2, back_first, 0)
    pl.semaphore_wait(told_4, both_ways(4, 4))
    tell_8()

    def blur_second(n, c):
        arrived(6 + n)
        place(8 + n, forward(patch(6 + n, second[n])))
        u, before = own[8 + n].astype(F32), own[4 + n].astype(F32)
        note(n, 4, u * before)
        note(n, 5, u * u)

        @pl.when(n == 1)
        def _():
            pl.semaphore_wait(told_8, both_ways(row_count, 8))
            start_sums()
            send(8)
            send(9)

        return c

    lax.fori_loop(0, 2, blur_second, 0)

    def back_second(n, c):
        arrived(8 + n)
        out[1, n] = adjoint(8 + n) + DAMPING * second[n]
        return c

    lax.fori_loop(0, 2, back_second, 0)
    all_sent()
    sums_sent()
    total = summed()
    for n in range(2):
        rr, rv, vv, uu, ut, tt = (total[:, i : i + 1] for i in range(6 * n, 6 * n + 6))
        curve0 = uu + DAMPING * rr
        step0 = rr / curve0
        turn = step0 / trial
        keep = 1.0 - turn
        norm1 = keep * keep * rr + 2.0 * keep * turn * rv + turn * turn * vv
        along = keep + norm1 / rr
        curve1 = along * along * curve0 + (
            2.0 * along * turn * (ut + DAMPING * rv) + turn * turn * (tt + DAMPING * vv)
        )
        step1 = norm1 / curve1
        r, v = first[n], second[n]
        out[0, n] = (step0 + step1 * along) * r + (step1 * turn) * v
        out[1, n] = (keep * r + turn * v) - step1 * (along * image[n] + turn * out[1, n])


def solution(mesh):
    row_count, col_count = mesh.shape["row"], mesh.shape["col"]
    constants = tables()

    def shards(observed, probe_signs, weights, kernels):
        pair = (2, TILE_ROWS, TILE_COLS)
        vmem = pl.BlockSpec(memory_space=pltpu.VMEM)
        operands = [observed, probe_signs, weights, jnp.transpose(kernels, (1, 0, 2)), *[jnp.asarray(c) for c in constants]]
        both = pl.pallas_call(
            functools.partial(kernel, row_count, col_count),
            out_shape=jax.ShapeDtypeStruct((2, *pair), F32),
            in_specs=[pl.BlockSpec(memory_space=pltpu.HBM)] * len(operands),
            out_specs=vmem,
            scratch_shapes=[
                *[pltpu.VMEM(x.shape, x.dtype) for x in operands],
                pltpu.VMEM((SLOTS, 320, TILE_COLS), BF16),
                pltpu.VMEM((SLOTS, TILE_ROWS, TILE_COLS), BF16),
                pltpu.VMEM((SLOTS, TILE_ROWS, TILE_COLS), BF16),
                pltpu.VMEM((TILE_ROWS, TILE_COLS), BF16),
                pltpu.VMEM((MODES, TAPS, TAPS), F32),
                pltpu.VMEM((MODES, 3 * TILE_ROWS, 2 * TILE_COLS), F32),
                pltpu.VMEM((2, MODES, 4, FREQS, FREQS), F32),
                pltpu.VMEM(pair, F32),
                pltpu.VMEM(pair, F32),
                pltpu.VMEM(pair, F32),
                pltpu.VMEM((16, TILE_COLS), F32),
                pltpu.VMEM((1, TILE_COLS), F32),
                pltpu.VMEM((row_count * col_count, 1, TILE_COLS), F32),
                pltpu.SemaphoreType.DMA((len(operands),)),
                pltpu.SemaphoreType.DMA((SLOTS,)),
                pltpu.SemaphoreType.DMA((8,)),
                *[pltpu.SemaphoreType.DMA] * 2,
                *[pltpu.SemaphoreType.REGULAR] * 2,
            ],
            compiler_params=pltpu.CompilerParams(
                collective_id=0, has_side_effects=True, vmem_limit_bytes=32 * 2**20
            ),
            name="deconvolve",
        )(*[pltpu.with_memory_space_constraint(x, pltpu.HBM) for x in operands])
        return both[0], both[1]

    return jax.shard_map(
        shards,
        mesh=mesh,
        in_specs=(P("row", "col"), P("row", "col"), P(None, "row", "col"), P()),
        out_specs=(P(None, "row", "col"), P(None, "row", "col")),
        check_vma=False,
    )
```

```python
import functools

import jax
import jax.numpy as jnp
import ml_dtypes
import numpy as np
from jax import lax
from jax.experimental import pallas as pl
from jax.experimental.pallas import tpu as pltpu
from jax.sharding import PartitionSpec as P

RADIUS = 64
MODES = 2
DAMPING = 1.0
TILE_ROWS = 64
TILE_COLS = 128
FREQS = 128
TAPS = 2 * RADIUS + 1
BF16 = jnp.bfloat16
F32 = jnp.float32
MESH = pl.DeviceIdType.MESH

WEIGHT_STAGE = 5
SLOTS = 12


def split(table):
    high = table.astype(ml_dtypes.bfloat16)
    low = (table - high.astype(np.float64)).astype(ml_dtypes.bfloat16)
    return np.stack([high, low])


def tables():
    theta = 2 * np.pi * (np.arange(FREQS) + 0.5) / 256
    phi = 2 * np.pi * np.arange(FREQS) / 128
    column = np.concatenate([64 + np.arange(128), 192 + np.arange(64), np.arange(64)])
    arg = np.outer(column, theta)
    into_cols = np.concatenate([np.cos(arg), -np.sin(arg)], 1)
    pieces = []
    for block in range(2):
        arg = np.outer(phi, 64 * block + np.arange(64))
        pieces.append(np.block([[np.cos(arg), np.sin(arg)], [-np.sin(arg), np.cos(arg)]]))
    into_rows = np.concatenate(pieces, 1)
    arg = np.outer(np.arange(64), phi)
    from_rows = np.block([[np.cos(arg), -np.sin(arg)], [np.sin(arg), np.cos(arg)]]) / 128
    arg = np.outer(theta, np.arange(128))
    from_cols = np.concatenate([np.cos(arg), -np.sin(arg)], 0) / 128
    from_cols = np.concatenate([from_cols, np.roll(from_cols, 64, axis=1)], 1)
    arg = np.outer(np.arange(128), theta)
    tap_cols = np.concatenate([np.cos(arg), np.sin(arg)], 1)
    arg = np.outer(phi, np.arange(64))
    tap_rows = np.block([[np.cos(arg), -np.sin(arg)], [np.sin(arg), np.cos(arg)]])
    one_part = [t.astype(ml_dtypes.bfloat16) for t in (into_cols, into_rows)]
    return one_part + [split(t) for t in (from_rows, from_cols, tap_cols, tap_rows)]


def dot(a, b):
    return jnp.dot(a, b, preferred_element_type=F32)


def halves(x):
    high = x.astype(BF16)
    return high, (x - high.astype(F32)).astype(BF16)


def dot_parts_right(table, x):
    high, low = halves(x)
    return dot(table, high) + dot(table, low)


def dot_both_right(table, x):
    high, low = halves(x)
    rows = table.shape[1]
    both = dot(table[...].reshape(2 * rows, table.shape[2]), high)
    return both[:rows] + (both[rows:] + dot(table[0], low))


def dot_both_left(x, table, columns):
    high, low = halves(x)
    rows = x.shape[0]
    both = dot(jnp.concatenate([high, low], 0), table[0, :, 0:columns])
    return both[:rows] + (both[rows:] + dot(high, table[1, :, 0:columns]))


def kernel(
    row_count,
    col_count,
    observed_hbm,
    probe_hbm,
    weights_hbm,
    taps_hbm,
    into_cols_hbm,
    into_rows_hbm,
    from_rows_hbm,
    from_cols_hbm,
    tap_cols_hbm,
    tap_rows_hbm,
    out,
    observed,
    probe,
    weights,
    taps,
    into_cols,
    into_rows,
    from_rows,
    from_cols,
    tap_cols,
    tap_rows,
    got,
    own,
    packed,
    zeros,
    planes,
    patch_weights,
    responses,
    first,
    image,
    second,
    parts,
    mine,
    all_sums,
    load_sem,
    got_sem,
    sent_sem,
    sums_in,
    sums_out,
    told_4,
    told_8,
):
    my_row = lax.axis_index("row")
    my_col = lax.axis_index("col")
    up_ok, down_ok = my_row > 0, my_row < row_count - 1
    left_ok, right_ok = my_col > 0, my_col < col_count - 1

    loads = [
        pltpu.make_async_copy(src, dst, load_sem.at[i])
        for i, (src, dst) in enumerate(
            (
                (observed_hbm, observed),
                (probe_hbm, probe),
                (weights_hbm, weights),
                (taps_hbm, taps),
                (tap_cols_hbm, tap_cols),
                (tap_rows_hbm, tap_rows),
                (into_cols_hbm, into_cols),
                (into_rows_hbm, into_rows),
                (from_rows_hbm, from_rows),
                (from_cols_hbm, from_cols),
            )
        )
    ]
    barrier = pltpu.get_barrier_semaphore()

    def greet(row, col):
        pl.semaphore_signal(barrier, inc=1, device_id=(row, col), device_id_type=MESH)

    row_there, col_there = {-1: up_ok, 1: down_ok}, {-1: left_ok, 1: right_ok}
    neighbours = [(dr, dc, row_there[dr] & col_there[dc]) for dr in (-1, 1) for dc in (-1, 1)]
    neighbours += [(dr, 0, row_there[dr]) for dr in (-1, 1)]
    neighbours += [(0, dc, col_there[dc]) for dc in (-1, 1)]
    for dr, dc, there in neighbours:
        pl.when(there)(functools.partial(greet, my_row + dr, my_col + dc))
    for load in loads[:2]:
        load.start()
    for load in loads[2:]:
        load.start()
    rows_here = 1 + up_ok.astype(jnp.int32) + down_ok.astype(jnp.int32)
    cols_here = 1 + left_ok.astype(jnp.int32) + right_ok.astype(jnp.int32)
    partners = rows_here * cols_here - 1

    lane = lax.broadcasted_iota(jnp.int32, (32, TILE_COLS), 1)
    low_lanes = lane < 64

    def place(slot, tile, turned=None):
        own[slot] = tile.astype(BF16)
        if turned is None:
            turned = pltpu.roll(tile, 64, 1)
        packed[slot, 0:32] = jnp.where(low_lanes, tile[0:32], turned[32:64]).astype(BF16)
        packed[slot, 32:64] = jnp.where(low_lanes, turned[0:32], tile[32:64]).astype(BF16)

    def landing(slot, dr, dc):
        if dc == 0:
            return got.at[slot, pl.ds(0 if dr < 0 else 64, 64)]
        return got.at[slot, pl.ds(128 + 64 * (1 + dr) + (32 if dc < 0 else 0), 32)]

    def send(slot):
        for i, (dr, dc, there) in enumerate(neighbours):
            if dc == 0:
                piece = own.at[slot]
            else:
                piece = packed.at[slot, pl.ds(0 if dc < 0 else 32, 32)]
            out = pltpu.make_async_remote_copy(
                src_ref=piece,
                dst_ref=landing(slot, -dr, -dc),
                send_sem=sent_sem.at[i],
                recv_sem=got_sem.at[slot],
                device_id=(my_row + dr, my_col + dc),
                device_id_type=MESH,
            )
            pl.when(there)(out.start)

    def fill_edges(slot, c):
        for dr, dc, there in neighbours:
            edge = landing(slot, dr, dc)
            fill = pltpu.make_async_copy(zeros.at[pl.ds(0, edge.shape[0])], edge, got_sem.at[slot])
            pl.when(jnp.logical_not(there))(fill.start)
        return c

    def arrived(slot):
        pltpu.make_async_copy(got.at[slot], got.at[slot], got_sem.at[slot]).wait()

    def all_sent():
        for i, (dr, dc, there) in enumerate(neighbours):
            every = got.at[:, pl.ds(0, 64 if dc == 0 else 32)]
            pl.when(there)(pltpu.make_async_copy(every, every, sent_sem.at[i]).wait)

    def halo(slot, k):
        right = got[slot, 128 + 64 * k : 160 + 64 * k].astype(F32)
        left = got[slot, 160 + 64 * k : 192 + 64 * k].astype(F32)
        top = jnp.where(low_lanes, right, pltpu.roll(left, 64, 1))
        bottom = jnp.where(low_lanes, pltpu.roll(right, 64, 1), left)
        return jnp.concatenate([top, bottom], 0)

    def patch(slot, middle):
        above, below = got[slot, 0:64].astype(F32), got[slot, 64:128].astype(F32)
        return [
            jnp.concatenate([tile, halo(slot, k)], 1) for k, tile in enumerate((above, middle, below))
        ]

    def columns_of(x):
        return dot(x, into_cols[...])

    def stacked(y, k):
        parts = []
        for b in (k, k + 1):
            rows = y[64 * b : 64 * b + 64]
            parts += [rows[:, :128], rows[:, 128:]]
        return jnp.concatenate(parts, 0)

    def adjoint(slot):
        tiles = (got[slot, 0:64], own[slot], got[slot, 64:128])
        x = jnp.concatenate(
            [jnp.concatenate([tile, halo(slot, k).astype(BF16)], 1) for k, tile in enumerate(tiles)], 0
        )
        y = columns_of(x)
        z = dot_parts_right(into_rows[...], jnp.concatenate([stacked(y, 0), stacked(y, 1)], 1))
        are, aim = z[:128, :128], z[128:, :128]
        bre, bim = z[:128, 128:], z[128:, 128:]
        reals, imags = [], []
        for m in range(MODES):
            h = [responses[1, m, i] for i in range(4)]
            reals.append(h[0] * are - h[1] * aim + (h[2] * bre - h[3] * bim))
            imags.append(h[0] * aim + h[1] * are + (h[2] * bim + h[3] * bre))
        spectrum = jnp.concatenate([jnp.concatenate(reals, 1), jnp.concatenate(imags, 1)], 0)
        v = dot_both_right(from_rows, spectrum)
        rows = [
            jnp.concatenate([v[:64, 128 * m : 128 * m + 128], v[64:, 128 * m : 128 * m + 128]], 1)
            for m in range(MODES)
        ]
        out = dot_both_left(jnp.concatenate(rows, 0), from_cols, TILE_COLS)
        return weights[0] * out[:64] + weights[1] * out[64:]

    def forward(values):
        x = jnp.concatenate(
            [
                (patch_weights[m, 64 * k : 64 * k + 64] * values[k]).astype(BF16)
                for m in range(MODES)
                for k in range(3)
            ],
            0,
        )
        y = columns_of(x)
        z = [
            dot_parts_right(
                into_rows[...], jnp.concatenate([stacked(y[:192], k), stacked(y[192:], k)], 1)
            )
            for k in range(2)
        ]
        real = jnp.zeros((FREQS, FREQS), F32)
        imag = real
        for m in range(MODES):
            h = [responses[0, m, i] for i in range(4)]
            lanes = slice(128 * m, 128 * m + 128)
            are, aim = z[0][:128, lanes], z[0][128:, lanes]
            bre, bim = z[1][:128, lanes], z[1][128:, lanes]
            real = real + (h[0] * are - h[1] * aim + (h[2] * bre - h[3] * bim))
            imag = imag + (h[0] * aim + h[1] * are + (h[2] * bim + h[3] * bre))
        v = dot_both_right(from_rows, jnp.concatenate([real, imag], 0))
        return dot_both_left(jnp.concatenate([v[:64], v[64:]], 1), from_cols, 2 * TILE_COLS)

    def build_responses(m, c):
        narrow = planes[m, :, 0:128].astype(BF16)
        even_lane = lax.broadcasted_iota(jnp.int32, (1, FREQS), 1) % 2 == 0
        sign_f = jnp.where(even_lane, 1.0, -1.0)
        even_row = lax.broadcasted_iota(jnp.int32, (FREQS, 1), 0) % 2 == 0
        sign_q = jnp.where(even_row, 1.0, -1.0)
        cols = dot(narrow, tap_cols[0]) + dot(narrow, tap_cols[1])
        re = cols[:, :128]
        im = cols[:, 128:] + planes[m, :, 128:129] * sign_f
        pairs = jnp.concatenate(
            [
                jnp.concatenate([re[0:64], re[64:128]], 1),
                jnp.concatenate([im[0:64], im[64:128]], 1),
            ],
            0,
        )
        high, low = halves(pairs)
        g = dot(tap_rows[0], high) + (dot(tap_rows[0], low) + dot(tap_rows[1], high))
        g0re, g0im, g1re, g1im = g[:128, :128], g[128:, :128], g[:128, 128:], g[128:, 128:]
        mid_re, mid_im, last_re, last_im = re[64:65], im[64:65], re[128:129], im[128:129]
        responses[0, m, 0] = g0re
        responses[0, m, 1] = g0im
        responses[0, m, 2] = g1re + sign_q * last_re
        responses[0, m, 3] = g1im + sign_q * last_im
        responses[1, m, 0] = sign_f * (sign_q * (g1im - mid_im) + last_im)
        responses[1, m, 1] = sign_f * (sign_q * (g1re - mid_re) + last_re)
        responses[1, m, 2] = sign_f * (sign_q * g0im + mid_im)
        responses[1, m, 3] = sign_f * (sign_q * g0re + mid_re)
        return c

    def note(n, i, part):
        parts[pl.ds(6 * n + i, 1)] = jnp.sum(part, axis=0, keepdims=True)

    def tell(semaphore, steps):
        for dr, dc in steps:
            row, col = my_row + dr, my_col + dc
            there = (row >= 0) & (row < row_count) & (col >= 0) & (col < col_count)

            @pl.when(there)
            def _(row=row, col=col):
                pl.semaphore_signal(semaphore, inc=1, device_id=(row, col), device_id_type=MESH)

    def both_ways(down, across):
        rows = 1 + (my_row >= down).astype(jnp.int32) + (my_row + down < row_count).astype(jnp.int32)
        cols = 1 + (my_col >= across).astype(jnp.int32) + (my_col + across < col_count).astype(jnp.int32)
        return rows * cols - 1

    def tell_4():
        tell(told_4, [(4 * i, 4 * j) for i in (-1, 0, 1) for j in (-1, 0, 1) if i or j])

    def tell_8():
        tell(told_8, [(0, -8), (0, 8)])

    z_count, y_count = row_count // 2, col_count // 4
    my_z, my_y = my_row // 2, lax.rem(my_col // 2, y_count)
    my_x, my_core = 2 * (my_col // (2 * y_count)) + lax.rem(my_row, 2), lax.rem(my_col, 2)
    me = my_row * col_count + my_col
    others = row_count * col_count - 1

    def start_sums():
        totals = jnp.sum(parts[...], axis=1, keepdims=True)
        here = lax.broadcasted_iota(jnp.int32, (16, TILE_COLS), 0) == lax.broadcasted_iota(
            jnp.int32, (16, TILE_COLS), 1
        )
        mine[...] = jnp.sum(jnp.where(here, totals, 0.0), axis=0, keepdims=True)
        places = []
        for dx in (1, 2, 3, 0):
            x = lax.rem(my_x + dx, 4)
            for dcore in (1, 0):
                core = lax.rem(my_core + dcore, 2)
                places.append((lax.rem(x, 2), (x // 2) * 2 * y_count + core, dx == 0 and dcore == 0))

        def go(i, c):
            z, y = i // y_count, lax.rem(i, y_count)
            for x_row, x_col, same in places:
                out = pltpu.make_async_remote_copy(
                    src_ref=mine,
                    dst_ref=all_sums.at[me],
                    send_sem=sums_out,
                    recv_sem=sums_in,
                    device_id=(2 * z + x_row, 2 * y + x_col),
                    device_id_type=MESH,
                )
                if same:
                    pl.when((z != my_z) | (y != my_y))(out.start)
                else:
                    out.start()
            return c

        lax.fori_loop(0, z_count * y_count, go, 0)
        all_sums[me] = mine[...]

    def summed():
        rest = all_sums.at[pl.ds(0, others)]
        pltpu.make_async_copy(rest, rest, sums_in).wait()
        lanes = [all_sums[i] for i in range(8)]
        for i in range(8, others + 1):
            lanes[i % 8] = lanes[i % 8] + all_sums[i]
        while len(lanes) > 1:
            lanes = [a + b for a, b in zip(lanes[::2], lanes[1::2])]
        return lanes[0]

    def sums_sent():
        rest = all_sums.at[pl.ds(0, others)]
        pltpu.make_async_copy(rest, rest, sums_out).wait()

    zeros[...] = jnp.zeros_like(zeros)
    parts[...] = jnp.zeros_like(parts)
    for load in loads[:2]:
        load.wait()
    place(0, observed[...].astype(F32))
    place(1, (2 * probe[...] - 1).astype(F32))
    pl.semaphore_wait(barrier, partners)
    for slot in (0, 1):
        send(slot)
    loads[2].wait()
    for m in range(MODES):
        place(2 * WEIGHT_STAGE + m, weights[m])
        send(2 * WEIGHT_STAGE + m)
    at_border = jnp.logical_not(up_ok & down_ok & left_ok & right_ok)

    @pl.when(at_border)
    def _():
        lax.fori_loop(0, SLOTS, fill_edges, 0)

    for load in loads[3:]:
        load.wait()
    for m in range(MODES):
        planes[m] = taps[:, m, :].astype(F32)
    energy = jnp.sum(jnp.sum(planes[0] * planes[0] + planes[1] * planes[1], axis=0, keepdims=True), axis=1, keepdims=True)
    trial = 1.0 / (DAMPING + 0.85 * energy)
    lax.fori_loop(0, MODES, build_responses, 0)

    def right_side(n, c):
        arrived(n)
        r = adjoint(n)
        first[n] = r
        place(2 + n, r)
        send(2 + n)
        return c

    lax.fori_loop(0, 2, right_side, 0)

    def spread_weights(m, c):
        slot = 2 * WEIGHT_STAGE + m
        arrived(slot)
        for k, b in enumerate(patch(slot, weights[m])):
            patch_weights[m, 64 * k : 64 * k + 64] = b
        return c

    lax.fori_loop(0, MODES, spread_weights, 0)

    def blur_first(n, c):
        arrived(2 + n)
        r = first[n]
        u = forward(patch(2 + n, r))
        place(4 + n, u[:, :TILE_COLS], u[:, TILE_COLS:])
        send(4 + n)
        u = own[4 + n].astype(F32)
        note(n, 0, r * r)
        note(n, 3, u * u)
        return c

    lax.fori_loop(0, 2, blur_first, 0)

    def back_first(n, c):
        arrived(4 + n)

        @pl.when(n == 0)
        def _():
            tell_4()

        r = first[n]
        w = adjoint(4 + n) + DAMPING * r
        v = r - trial * w
        place(6 + n, v)
        send(6 + n)
        image[n] = w
        second[n] = v
        note(n, 1, r * v)
        note(n, 2, v * v)
        return c

    lax.fori_loop(0, 2, back_first, 0)
    pl.semaphore_wait(told_4, both_ways(4, 4))
    tell_8()

    def blur_second(n, c):
        arrived(6 + n)
        u = forward(patch(6 + n, second[n]))
        place(8 + n, u[:, :TILE_COLS], u[:, TILE_COLS:])
        u, before = own[8 + n].astype(F32), own[4 + n].astype(F32)
        note(n, 4, u * before)
        note(n, 5, u * u)

        @pl.when(n == 1)
        def _():
            pl.semaphore_wait(told_8, both_ways(row_count, 8))
            start_sums()
            send(8)
            send(9)

        return c

    lax.fori_loop(0, 2, blur_second, 0)

    def back_second(n, c):
        arrived(8 + n)
        out[1, n] = adjoint(8 + n) + DAMPING * second[n]
        return c

    lax.fori_loop(0, 2, back_second, 0)
    all_sent()
    sums_sent()
    total = summed()
    for n in range(2):
        rr, rv, vv, uu, ut, tt = (total[:, i : i + 1] for i in range(6 * n, 6 * n + 6))
        curve0 = uu + DAMPING * rr
        step0 = rr / curve0
        turn = step0 / trial
        keep = 1.0 - turn
        norm1 = keep * keep * rr + 2.0 * keep * turn * rv + turn * turn * vv
        along = keep + norm1 / rr
        curve1 = along * along * curve0 + (
            2.0 * along * turn * (ut + DAMPING * rv) + turn * turn * (tt + DAMPING * vv)
        )
        step1 = norm1 / curve1
        r, v = first[n], second[n]
        out[0, n] = (step0 + step1 * along) * r + (step1 * turn) * v
        out[1, n] = (keep * r + turn * v) - step1 * (along * image[n] + turn * out[1, n])


def solution(mesh):
    row_count, col_count = mesh.shape["row"], mesh.shape["col"]
    constants = tables()

    def shards(observed, probe_signs, weights, kernels):
        pair = (2, TILE_ROWS, TILE_COLS)
        vmem = pl.BlockSpec(memory_space=pltpu.VMEM)
        operands = [observed, probe_signs, weights, jnp.transpose(kernels, (1, 0, 2)), *[jnp.asarray(c) for c in constants]]
        both = pl.pallas_call(
            functools.partial(kernel, row_count, col_count),
            out_shape=jax.ShapeDtypeStruct((2, *pair), F32),
            in_specs=[pl.BlockSpec(memory_space=pltpu.HBM)] * len(operands),
            out_specs=vmem,
            scratch_shapes=[
                *[pltpu.VMEM(x.shape, x.dtype) for x in operands],
                pltpu.VMEM((SLOTS, 320, TILE_COLS), BF16),
                pltpu.VMEM((SLOTS, TILE_ROWS, TILE_COLS), BF16),
                pltpu.VMEM((SLOTS, TILE_ROWS, TILE_COLS), BF16),
                pltpu.VMEM((TILE_ROWS, TILE_COLS), BF16),
                pltpu.VMEM((MODES, TAPS, TAPS), F32),
                pltpu.VMEM((MODES, 3 * TILE_ROWS, 2 * TILE_COLS), F32),
                pltpu.VMEM((2, MODES, 4, FREQS, FREQS), F32),
                pltpu.VMEM(pair, F32),
                pltpu.VMEM(pair, F32),
                pltpu.VMEM(pair, F32),
                pltpu.VMEM((16, TILE_COLS), F32),
                pltpu.VMEM((1, TILE_COLS), F32),
                pltpu.VMEM((row_count * col_count, 1, TILE_COLS), F32),
                pltpu.SemaphoreType.DMA((len(operands),)),
                pltpu.SemaphoreType.DMA((SLOTS,)),
                pltpu.SemaphoreType.DMA((8,)),
                *[pltpu.SemaphoreType.DMA] * 2,
                *[pltpu.SemaphoreType.REGULAR] * 2,
            ],
            compiler_params=pltpu.CompilerParams(
                collective_id=0, has_side_effects=True, vmem_limit_bytes=32 * 2**20
            ),
            name="deconvolve",
        )(*[pltpu.with_memory_space_constraint(x, pltpu.HBM) for x in operands])
        return both[0], both[1]

    return jax.shard_map(
        shards,
        mesh=mesh,
        in_specs=(P("row", "col"), P("row", "col"), P(None, "row", "col"), P()),
        out_specs=(P(None, "row", "col"), P(None, "row", "col")),
        check_vma=False,
    )
```

```python
import functools

import jax
import jax.numpy as jnp
import ml_dtypes
import numpy as np
from jax import lax
from jax.experimental import pallas as pl
from jax.experimental.pallas import tpu as pltpu
from jax.sharding import PartitionSpec as P

RADIUS = 64
MODES = 2
DAMPING = 1.0
TILE_ROWS = 64
TILE_COLS = 128
FREQS = 128
TAPS = 2 * RADIUS + 1
BF16 = jnp.bfloat16
F32 = jnp.float32
MESH = pl.DeviceIdType.MESH

WEIGHT_STAGE = 5
SLOTS = 12


def split(table):
    high = table.astype(ml_dtypes.bfloat16)
    low = (table - high.astype(np.float64)).astype(ml_dtypes.bfloat16)
    return np.stack([high, low])


def tables():
    theta = 2 * np.pi * (np.arange(FREQS) + 0.5) / 256
    phi = 2 * np.pi * np.arange(FREQS) / 128
    column = np.concatenate([64 + np.arange(128), 192 + np.arange(64), np.arange(64)])
    arg = np.outer(column, theta)
    into_cols = np.concatenate([np.cos(arg), -np.sin(arg)], 1)
    pieces = []
    for block in range(2):
        arg = np.outer(phi, 64 * block + np.arange(64))
        pieces.append(np.block([[np.cos(arg), np.sin(arg)], [-np.sin(arg), np.cos(arg)]]))
    into_rows = np.concatenate(pieces, 1)
    arg = np.outer(np.arange(64), phi)
    from_rows = np.block([[np.cos(arg), -np.sin(arg)], [np.sin(arg), np.cos(arg)]]) / 128
    arg = np.outer(theta, np.arange(128))
    from_cols = np.concatenate([np.cos(arg), -np.sin(arg)], 0) / 128
    from_cols = np.concatenate([from_cols, np.roll(from_cols, 64, axis=1)], 1)
    arg = np.outer(np.arange(128), theta)
    tap_cols = np.concatenate([np.cos(arg), np.sin(arg)], 1)
    arg = np.outer(phi, np.arange(64))
    tap_rows = np.block([[np.cos(arg), -np.sin(arg)], [np.sin(arg), np.cos(arg)]])
    one_part = [t.astype(ml_dtypes.bfloat16) for t in (into_cols, into_rows)]
    return one_part + [split(t) for t in (from_rows, from_cols, tap_cols, tap_rows)]


def dot(a, b):
    return jnp.dot(a, b, preferred_element_type=F32)


def halves(x):
    high = x.astype(BF16)
    return high, (x - high.astype(F32)).astype(BF16)


def dot_parts_right(table, x):
    high, low = halves(x)
    return dot(table, high) + dot(table, low)


def dot_both_right(table, x):
    high, low = halves(x)
    rows = table.shape[1]
    both = dot(table[...].reshape(2 * rows, table.shape[2]), high)
    return both[:rows] + (both[rows:] + dot(table[0], low))


def dot_both_left(x, table, columns):
    high, low = halves(x)
    rows = x.shape[0]
    both = dot(jnp.concatenate([high, low], 0), table[0, :, 0:columns])
    return both[:rows] + (both[rows:] + dot(high, table[1, :, 0:columns]))


def kernel(
    row_count,
    col_count,
    observed_hbm,
    probe_hbm,
    weights_hbm,
    taps_hbm,
    into_cols_hbm,
    into_rows_hbm,
    from_rows_hbm,
    from_cols_hbm,
    tap_cols_hbm,
    tap_rows_hbm,
    out,
    observed,
    probe,
    weights,
    taps,
    into_cols,
    into_rows,
    from_rows,
    from_cols,
    tap_cols,
    tap_rows,
    got,
    own,
    packed,
    zeros,
    planes,
    patch_weights,
    responses,
    first,
    image,
    second,
    parts,
    mine,
    all_sums,
    load_sem,
    got_sem,
    sent_sem,
    sums_in,
    sums_out,
    told_4,
    told_8,
):
    my_row = lax.axis_index("row")
    my_col = lax.axis_index("col")
    up_ok, down_ok = my_row > 0, my_row < row_count - 1
    left_ok, right_ok = my_col > 0, my_col < col_count - 1

    loads = [
        pltpu.make_async_copy(src, dst, load_sem.at[i])
        for i, (src, dst) in enumerate(
            (
                (observed_hbm, observed),
                (probe_hbm, probe),
                (weights_hbm, weights),
                (taps_hbm, taps),
                (tap_cols_hbm, tap_cols),
                (tap_rows_hbm, tap_rows),
                (into_cols_hbm, into_cols),
                (into_rows_hbm, into_rows),
                (from_rows_hbm, from_rows),
                (from_cols_hbm, from_cols),
            )
        )
    ]
    barrier = pltpu.get_barrier_semaphore()

    def greet(row, col):
        pl.semaphore_signal(barrier, inc=1, device_id=(row, col), device_id_type=MESH)

    row_there, col_there = {-1: up_ok, 1: down_ok}, {-1: left_ok, 1: right_ok}
    neighbours = [(dr, dc, row_there[dr] & col_there[dc]) for dr in (-1, 1) for dc in (-1, 1)]
    neighbours += [(dr, 0, row_there[dr]) for dr in (-1, 1)]
    neighbours += [(0, dc, col_there[dc]) for dc in (-1, 1)]
    for dr, dc, there in neighbours:
        pl.when(there)(functools.partial(greet, my_row + dr, my_col + dc))
    for load in loads[:2]:
        load.start()
    for load in loads[2:]:
        load.start()
    rows_here = 1 + up_ok.astype(jnp.int32) + down_ok.astype(jnp.int32)
    cols_here = 1 + left_ok.astype(jnp.int32) + right_ok.astype(jnp.int32)
    partners = rows_here * cols_here - 1

    lane = lax.broadcasted_iota(jnp.int32, (32, TILE_COLS), 1)
    low_lanes = lane < 64

    def place(slot, tile, turned=None):
        own[slot] = tile.astype(BF16)
        if turned is None:
            turned = pltpu.roll(tile, 64, 1)
        packed[slot, 0:32] = jnp.where(low_lanes, tile[0:32], turned[32:64]).astype(BF16)
        packed[slot, 32:64] = jnp.where(low_lanes, turned[0:32], tile[32:64]).astype(BF16)

    def landing(slot, dr, dc):
        if dc == 0:
            return got.at[slot, pl.ds(0 if dr < 0 else 64, 64)]
        return got.at[slot, pl.ds(128 + 64 * (1 + dr) + (32 if dc < 0 else 0), 32)]

    def send(slot):
        for i, (dr, dc, there) in enumerate(neighbours):
            if dc == 0:
                piece = own.at[slot]
            else:
                piece = packed.at[slot, pl.ds(0 if dc < 0 else 32, 32)]
            out = pltpu.make_async_remote_copy(
                src_ref=piece,
                dst_ref=landing(slot, -dr, -dc),
                send_sem=sent_sem.at[i],
                recv_sem=got_sem.at[slot],
                device_id=(my_row + dr, my_col + dc),
                device_id_type=MESH,
            )
            pl.when(there)(out.start)

    def fill_edges(slot, c):
        for dr, dc, there in neighbours:
            edge = landing(slot, dr, dc)
            fill = pltpu.make_async_copy(zeros.at[pl.ds(0, edge.shape[0])], edge, got_sem.at[slot])
            pl.when(jnp.logical_not(there))(fill.start)
        return c

    def arrived(slot):
        pltpu.make_async_copy(got.at[slot], got.at[slot], got_sem.at[slot]).wait()

    def all_sent():
        for i, (dr, dc, there) in enumerate(neighbours):
            every = got.at[:, pl.ds(0, 64 if dc == 0 else 32)]
            pl.when(there)(pltpu.make_async_copy(every, every, sent_sem.at[i]).wait)

    def halo(slot, k):
        right = got[slot, 128 + 64 * k : 160 + 64 * k].astype(F32)
        left = got[slot, 160 + 64 * k : 192 + 64 * k].astype(F32)
        top = jnp.where(low_lanes, right, pltpu.roll(left, 64, 1))
        bottom = jnp.where(low_lanes, pltpu.roll(right, 64, 1), left)
        return jnp.concatenate([top, bottom], 0)

    def patch(slot, middle):
        above, below = got[slot, 0:64].astype(F32), got[slot, 64:128].astype(F32)
        return [
            jnp.concatenate([tile, halo(slot, k)], 1) for k, tile in enumerate((above, middle, below))
        ]

    def columns_of(x):
        return dot(x, into_cols[...])

    def stacked(y, k):
        parts = []
        for b in (k, k + 1):
            rows = y[64 * b : 64 * b + 64]
            parts += [rows[:, :128], rows[:, 128:]]
        return jnp.concatenate(parts, 0)

    def beside(x):
        return jnp.concatenate([x, pltpu.roll(x, 64, 1)], 1)

    def adjoint(slot):
        tiles = (got[slot, 0:64], own[slot], got[slot, 64:128])
        x = jnp.concatenate(
            [jnp.concatenate([tile, halo(slot, k).astype(BF16)], 1) for k, tile in enumerate(tiles)], 0
        )
        y = columns_of(x)
        z = dot_parts_right(into_rows[...], jnp.concatenate([stacked(y, 0), stacked(y, 1)], 1))
        are, aim = z[:128, :128], z[128:, :128]
        bre, bim = z[:128, 128:], z[128:, 128:]
        reals, imags = [], []
        for m in range(MODES):
            h = [responses[1, m, i] for i in range(4)]
            reals.append(h[0] * are - h[1] * aim + (h[2] * bre - h[3] * bim))
            imags.append(h[0] * aim + h[1] * are + (h[2] * bim + h[3] * bre))
        spectrum = jnp.concatenate([jnp.concatenate(reals, 1), jnp.concatenate(imags, 1)], 0)
        v = dot_both_right(from_rows, spectrum)
        rows = [
            jnp.concatenate([v[:64, 128 * m : 128 * m + 128], v[64:, 128 * m : 128 * m + 128]], 1)
            for m in range(MODES)
        ]
        out = dot_both_left(jnp.concatenate(rows, 0), from_cols, 2 * TILE_COLS)
        return beside(weights[0]) * out[:64] + beside(weights[1]) * out[64:]

    def forward(values):
        x = jnp.concatenate(
            [
                (patch_weights[m, 64 * k : 64 * k + 64] * values[k]).astype(BF16)
                for m in range(MODES)
                for k in range(3)
            ],
            0,
        )
        y = columns_of(x)
        z = [
            dot_parts_right(
                into_rows[...], jnp.concatenate([stacked(y[:192], k), stacked(y[192:], k)], 1)
            )
            for k in range(2)
        ]
        real = jnp.zeros((FREQS, FREQS), F32)
        imag = real
        for m in range(MODES):
            h = [responses[0, m, i] for i in range(4)]
            lanes = slice(128 * m, 128 * m + 128)
            are, aim = z[0][:128, lanes], z[0][128:, lanes]
            bre, bim = z[1][:128, lanes], z[1][128:, lanes]
            real = real + (h[0] * are - h[1] * aim + (h[2] * bre - h[3] * bim))
            imag = imag + (h[0] * aim + h[1] * are + (h[2] * bim + h[3] * bre))
        v = dot_both_right(from_rows, jnp.concatenate([real, imag], 0))
        return dot_both_left(jnp.concatenate([v[:64], v[64:]], 1), from_cols, 2 * TILE_COLS)

    def build_responses(m, c):
        narrow = planes[m, :, 0:128].astype(BF16)
        even_lane = lax.broadcasted_iota(jnp.int32, (1, FREQS), 1) % 2 == 0
        sign_f = jnp.where(even_lane, 1.0, -1.0)
        even_row = lax.broadcasted_iota(jnp.int32, (FREQS, 1), 0) % 2 == 0
        sign_q = jnp.where(even_row, 1.0, -1.0)
        cols = dot(narrow, tap_cols[0]) + dot(narrow, tap_cols[1])
        re = cols[:, :128]
        im = cols[:, 128:] + planes[m, :, 128:129] * sign_f
        pairs = jnp.concatenate(
            [
                jnp.concatenate([re[0:64], re[64:128]], 1),
                jnp.concatenate([im[0:64], im[64:128]], 1),
            ],
            0,
        )
        high, low = halves(pairs)
        g = dot(tap_rows[0], high) + (dot(tap_rows[0], low) + dot(tap_rows[1], high))
        g0re, g0im, g1re, g1im = g[:128, :128], g[128:, :128], g[:128, 128:], g[128:, 128:]
        mid_re, mid_im, last_re, last_im = re[64:65], im[64:65], re[128:129], im[128:129]
        responses[0, m, 0] = g0re
        responses[0, m, 1] = g0im
        responses[0, m, 2] = g1re + sign_q * last_re
        responses[0, m, 3] = g1im + sign_q * last_im
        responses[1, m, 0] = sign_f * (sign_q * (g1im - mid_im) + last_im)
        responses[1, m, 1] = sign_f * (sign_q * (g1re - mid_re) + last_re)
        responses[1, m, 2] = sign_f * (sign_q * g0im + mid_im)
        responses[1, m, 3] = sign_f * (sign_q * g0re + mid_re)
        return c

    def note(n, i, part):
        parts[pl.ds(6 * n + i, 1)] = jnp.sum(part, axis=0, keepdims=True)

    def tell(semaphore, steps):
        for dr, dc in steps:
            row, col = my_row + dr, my_col + dc
            there = (row >= 0) & (row < row_count) & (col >= 0) & (col < col_count)

            @pl.when(there)
            def _(row=row, col=col):
                pl.semaphore_signal(semaphore, inc=1, device_id=(row, col), device_id_type=MESH)

    def both_ways(down, across):
        rows = 1 + (my_row >= down).astype(jnp.int32) + (my_row + down < row_count).astype(jnp.int32)
        cols = 1 + (my_col >= across).astype(jnp.int32) + (my_col + across < col_count).astype(jnp.int32)
        return rows * cols - 1

    def tell_4():
        tell(told_4, [(4 * i, 4 * j) for i in (-1, 0, 1) for j in (-1, 0, 1) if i or j])

    def tell_8():
        tell(told_8, [(0, -8), (0, 8)])

    z_count, y_count = row_count // 2, col_count // 4
    my_z, my_y = my_row // 2, lax.rem(my_col // 2, y_count)
    my_x, my_core = 2 * (my_col // (2 * y_count)) + lax.rem(my_row, 2), lax.rem(my_col, 2)
    me = my_row * col_count + my_col
    others = row_count * col_count - 1

    def start_sums():
        totals = jnp.sum(parts[...], axis=1, keepdims=True)
        here = lax.broadcasted_iota(jnp.int32, (16, TILE_COLS), 0) == lax.broadcasted_iota(
            jnp.int32, (16, TILE_COLS), 1
        )
        mine[...] = jnp.sum(jnp.where(here, totals, 0.0), axis=0, keepdims=True)
        places = []
        for dx in (1, 2, 3, 0):
            x = lax.rem(my_x + dx, 4)
            for dcore in (1, 0):
                core = lax.rem(my_core + dcore, 2)
                places.append((lax.rem(x, 2), (x // 2) * 2 * y_count + core, dx == 0 and dcore == 0))

        def go(i, c):
            z, y = i // y_count, lax.rem(i, y_count)
            for x_row, x_col, same in places:
                out = pltpu.make_async_remote_copy(
                    src_ref=mine,
                    dst_ref=all_sums.at[me],
                    send_sem=sums_out,
                    recv_sem=sums_in,
                    device_id=(2 * z + x_row, 2 * y + x_col),
                    device_id_type=MESH,
                )
                if same:
                    pl.when((z != my_z) | (y != my_y))(out.start)
                else:
                    out.start()
            return c

        lax.fori_loop(0, z_count * y_count, go, 0)
        all_sums[me] = mine[...]

    def summed():
        rest = all_sums.at[pl.ds(0, others)]
        pltpu.make_async_copy(rest, rest, sums_in).wait()
        lanes = [all_sums[i] for i in range(8)]
        for i in range(8, others + 1):
            lanes[i % 8] = lanes[i % 8] + all_sums[i]
        while len(lanes) > 1:
            lanes = [a + b for a, b in zip(lanes[::2], lanes[1::2])]
        return lanes[0]

    def sums_sent():
        rest = all_sums.at[pl.ds(0, others)]
        pltpu.make_async_copy(rest, rest, sums_out).wait()

    zeros[...] = jnp.zeros_like(zeros)
    parts[...] = jnp.zeros_like(parts)
    for load in loads[:2]:
        load.wait()
    place(0, observed[...].astype(F32))
    place(1, (2 * probe[...] - 1).astype(F32))
    pl.semaphore_wait(barrier, partners)
    for slot in (0, 1):
        send(slot)
    loads[2].wait()
    for m in range(MODES):
        place(2 * WEIGHT_STAGE + m, weights[m])
        send(2 * WEIGHT_STAGE + m)
    at_border = jnp.logical_not(up_ok & down_ok & left_ok & right_ok)

    @pl.when(at_border)
    def _():
        lax.fori_loop(0, SLOTS, fill_edges, 0)

    for load in loads[3:]:
        load.wait()
    for m in range(MODES):
        planes[m] = taps[:, m, :].astype(F32)
    energy = jnp.sum(jnp.sum(planes[0] * planes[0] + planes[1] * planes[1], axis=0, keepdims=True), axis=1, keepdims=True)
    trial = 1.0 / (DAMPING + 0.85 * energy)
    lax.fori_loop(0, MODES, build_responses, 0)

    def right_side(n, c):
        arrived(n)
        r = adjoint(n)
        first[n] = r[:, :TILE_COLS]
        place(2 + n, r[:, :TILE_COLS], r[:, TILE_COLS:])
        send(2 + n)
        return c

    lax.fori_loop(0, 2, right_side, 0)

    def spread_weights(m, c):
        slot = 2 * WEIGHT_STAGE + m
        arrived(slot)
        for k, b in enumerate(patch(slot, weights[m])):
            patch_weights[m, 64 * k : 64 * k + 64] = b
        return c

    lax.fori_loop(0, MODES, spread_weights, 0)

    def blur_first(n, c):
        arrived(2 + n)
        r = first[n]
        u = forward(patch(2 + n, r))
        place(4 + n, u[:, :TILE_COLS], u[:, TILE_COLS:])
        send(4 + n)
        u = own[4 + n].astype(F32)
        note(n, 0, r * r)
        note(n, 3, u * u)
        return c

    lax.fori_loop(0, 2, blur_first, 0)

    def back_first(n, c):
        arrived(4 + n)

        @pl.when(n == 0)
        def _():
            tell_4()

        r = first[n]
        wide = beside(r)
        w = adjoint(4 + n) + DAMPING * wide
        v = wide - trial * w
        place(6 + n, v[:, :TILE_COLS], v[:, TILE_COLS:])
        w, v = w[:, :TILE_COLS], v[:, :TILE_COLS]
        send(6 + n)
        image[n] = w
        second[n] = v
        note(n, 1, r * v)
        note(n, 2, v * v)
        return c

    lax.fori_loop(0, 2, back_first, 0)
    pl.semaphore_wait(told_4, both_ways(4, 4))
    tell_8()

    def blur_second(n, c):
        arrived(6 + n)
        u = forward(patch(6 + n, second[n]))
        place(8 + n, u[:, :TILE_COLS], u[:, TILE_COLS:])
        u, before = own[8 + n].astype(F32), own[4 + n].astype(F32)
        note(n, 4, u * before)
        note(n, 5, u * u)

        @pl.when(n == 1)
        def _():
            pl.semaphore_wait(told_8, both_ways(row_count, 8))
            start_sums()
            send(8)
            send(9)

        return c

    lax.fori_loop(0, 2, blur_second, 0)

    def back_second(n, c):
        arrived(8 + n)
        out[1, n] = adjoint(8 + n)[:, :TILE_COLS] + DAMPING * second[n]
        return c

    lax.fori_loop(0, 2, back_second, 0)
    all_sent()
    sums_sent()
    total = summed()
    for n in range(2):
        rr, rv, vv, uu, ut, tt = (total[:, i : i + 1] for i in range(6 * n, 6 * n + 6))
        curve0 = uu + DAMPING * rr
        step0 = rr / curve0
        turn = step0 / trial
        keep = 1.0 - turn
        norm1 = keep * keep * rr + 2.0 * keep * turn * rv + turn * turn * vv
        along = keep + norm1 / rr
        curve1 = along * along * curve0 + (
            2.0 * along * turn * (ut + DAMPING * rv) + turn * turn * (tt + DAMPING * vv)
        )
        step1 = norm1 / curve1
        r, v = first[n], second[n]
        out[0, n] = (step0 + step1 * along) * r + (step1 * turn) * v
        out[1, n] = (keep * r + turn * v) - step1 * (along * image[n] + turn * out[1, n])


def solution(mesh):
    row_count, col_count = mesh.shape["row"], mesh.shape["col"]
    constants = tables()

    def shards(observed, probe_signs, weights, kernels):
        pair = (2, TILE_ROWS, TILE_COLS)
        vmem = pl.BlockSpec(memory_space=pltpu.VMEM)
        operands = [observed, probe_signs, weights, jnp.transpose(kernels, (1, 0, 2)), *[jnp.asarray(c) for c in constants]]
        both = pl.pallas_call(
            functools.partial(kernel, row_count, col_count),
            out_shape=jax.ShapeDtypeStruct((2, *pair), F32),
            in_specs=[pl.BlockSpec(memory_space=pltpu.HBM)] * len(operands),
            out_specs=vmem,
            scratch_shapes=[
                *[pltpu.VMEM(x.shape, x.dtype) for x in operands],
                pltpu.VMEM((SLOTS, 320, TILE_COLS), BF16),
                pltpu.VMEM((SLOTS, TILE_ROWS, TILE_COLS), BF16),
                pltpu.VMEM((SLOTS, TILE_ROWS, TILE_COLS), BF16),
                pltpu.VMEM((TILE_ROWS, TILE_COLS), BF16),
                pltpu.VMEM((MODES, TAPS, TAPS), F32),
                pltpu.VMEM((MODES, 3 * TILE_ROWS, 2 * TILE_COLS), F32),
                pltpu.VMEM((2, MODES, 4, FREQS, FREQS), F32),
                pltpu.VMEM(pair, F32),
                pltpu.VMEM(pair, F32),
                pltpu.VMEM(pair, F32),
                pltpu.VMEM((16, TILE_COLS), F32),
                pltpu.VMEM((1, TILE_COLS), F32),
                pltpu.VMEM((row_count * col_count, 1, TILE_COLS), F32),
                pltpu.SemaphoreType.DMA((len(operands),)),
                pltpu.SemaphoreType.DMA((SLOTS,)),
                pltpu.SemaphoreType.DMA((8,)),
                *[pltpu.SemaphoreType.DMA] * 2,
                *[pltpu.SemaphoreType.REGULAR] * 2,
            ],
            compiler_params=pltpu.CompilerParams(
                collective_id=0, has_side_effects=True, vmem_limit_bytes=32 * 2**20
            ),
            name="deconvolve",
        )(*[pltpu.with_memory_space_constraint(x, pltpu.HBM) for x in operands])
        return both[0], both[1]

    return jax.shard_map(
        shards,
        mesh=mesh,
        in_specs=(P("row", "col"), P("row", "col"), P(None, "row", "col"), P()),
        out_specs=(P(None, "row", "col"), P(None, "row", "col")),
        check_vma=False,
    )
```
